32 devices in a mesh: groups: 2 (over x), tile: 16 (over z, y, core).
Axes of the slice: x: 2, y: 2, z: 4, core: 2. Of those that a mesh axis runs over, the one named last changes fastest.
Arguments:
- reference_feat: float32 [8, 1024, 256], P('groups', 'tile'), parts along dimension 0, may hold values from -32 to 32
- secondary_feat: float32 [4, 4, 1024, 256], P('groups', None, 'tile'), parts along dimension 0, may hold values from -32 to 32
- pair_offsets: int32 [4, 16], P('groups', 'tile'), parts along dimension 0, may hold values from 0 to 63, as said below
- w_query_key: float32 [256, 64], replicated, may hold values from -0.375 to 0.375
- w_value: float32 [256, 64], replicated, may hold values from -0.375 to 0.375
- conv_first: float32 [8, 8, 3, 3, 3], replicated, may hold values from -0.8 to 0.8
- conv_second: float32 [8, 8, 3, 3, 3], replicated, may hold values from -0.4 to 0.4
Outputs:
- disparity: float32 [8, 1024], P('groups', 'tile'), parts along dimension 0
The draws below stay inside these ranges and needn't reach their ends.
There are 2 independent parts, one for each index of `groups`. The reference program is written for one: setup_inputs(seed, part) draws one part's arguments, and reference() takes and returns one part's arrays. A program takes and returns all parts, laid end to end along the dimension named above; an argument that names none is the same for every part. Nothing has to cross between parts.
Inputs may be any that keep to these rules, and one draw needn't show every extreme that they name: `pair_offsets`: in each pair's row some tile holds 63 and the next tile, cyclically, holds 0.
All inputs are finite; a program needn't handle non-finite values.
Results may differ from the reference program's by a relative error of at most 0.0003.
Values sent between devices are 32-bit elements; how exact they have to be, the bound alone decides.
A program may use at most 192 MiB of HBM per device.

```python
from functools import reduce
import jax
import jax.numpy as jnp
from jax import lax

F = 256
CH = 64
CORR_GROUPS = 8
CONV_CH = 8
DISP = 128
RAD = 3
TW = 64
ROWS = 4
PAIRS = 2
NTILES = 16
NX = 1024


def spiked_draw(key, shape):
    base_key = jax.random.fold_in(key, 0)
    values = jax.random.normal(base_key, shape, jnp.float32)
    return jnp.clip(values, -6.0, 6.0)


def draw_reference_feat(key, part):
    return spiked_draw(jax.random.fold_in(key, 11), (ROWS, NX, F))


def draw_secondary_feat(key, part):
    return spiked_draw(jax.random.fold_in(key, 23), (PAIRS, ROWS, NX, F))


def draw_pair_offsets(key, part):
    base_key, peak_key = jax.random.split(jax.random.fold_in(key, 37))
    offset_table = jax.random.randint(base_key, (PAIRS, NTILES), 0, TW)
    peak_at = jax.random.randint(peak_key, (PAIRS, 1), 0, NTILES)
    positions = jnp.arange(NTILES)[None, :]
    offset_table = jnp.where(positions == peak_at, TW - 1, offset_table)
    offset_table = jnp.where(positions == (peak_at + 1) % NTILES, 0, offset_table)
    return offset_table.astype(jnp.int32)


def centred(own_key, extent, scale, bound, kind=jnp.bfloat16):
    result = scale * jax.random.normal(own_key, extent, jnp.float32)
    return jnp.clip(result, min=-bound, max=bound).astype(kind)


def setup_inputs(seed: int = 0, part: int = 0) -> dict:
    arg_keys = jax.random.split(jax.random.key(seed), 8)
    own_keys = jax.random.split(jax.random.fold_in(arg_keys[7], part), 8)
    reference_feat = draw_reference_feat(jax.random.fold_in(jax.random.fold_in(arg_keys[7], part), 71), part)
    secondary_feat = draw_secondary_feat(jax.random.fold_in(jax.random.fold_in(arg_keys[7], part), 71), part)
    pair_offsets = draw_pair_offsets(jax.random.fold_in(jax.random.fold_in(arg_keys[7], part), 71), part)
    w_query_key = centred(arg_keys[3], (F, CH), F ** -0.5, 0.375, jnp.float32)
    w_value = centred(arg_keys[4], (F, CH), F ** -0.5, 0.375, jnp.float32)
    conv_first = centred(arg_keys[5], (CONV_CH, CORR_GROUPS, 3, 3, 3), 0.2, 0.8, jnp.float32)
    conv_second = centred(arg_keys[6], (CONV_CH, CONV_CH, 3, 3, 3), 0.1, 0.4, jnp.float32)
    return dict(reference_feat=reference_feat, secondary_feat=secondary_feat, pair_offsets=pair_offsets, w_query_key=w_query_key, w_value=w_value, conv_first=conv_first, conv_second=conv_second)


precise = lax.Precision.HIGHEST


def window_attention(query_key, value_proj, widened, row_valid, col_valid, channels):
    row_count = query_key.shape[1]
    col_count = query_key.shape[2]
    scores = []
    for row_step in range(3):
        for col_step in range(2 * RAD + 1):
            keys_here = widened[:, row_step:row_step + row_count, col_step:col_step + col_count, :channels]
            allowed = row_valid[row_step:row_step + row_count][:, None] & col_valid[col_step:col_step + col_count][None, :]
            raw_score = jnp.sum(query_key * keys_here, axis=-1) / channels
            scores.append(jnp.where(allowed[None], raw_score, -1e30))
    row_peak = reduce(jnp.maximum, scores)
    weights = [jnp.exp(score_one - row_peak) for score_one in scores]
    exp_sum = reduce(jnp.add, weights)
    mixed = jnp.zeros(value_proj.shape, jnp.float32)
    position = 0
    for row_step in range(3):
        for col_step in range(2 * RAD + 1):
            vals_here = widened[:, row_step:row_step + row_count, col_step:col_step + col_count, channels:]
            mixed = mixed + weights[position][..., None] * vals_here
            position = position + 1
    return value_proj + mixed / exp_sum[..., None]


def attend(images, w_query_key, w_value):
    query_key = jnp.einsum('vrxf,fc->vrxc', images, w_query_key, precision=precise)
    value_proj = jnp.einsum('vrxf,fc->vrxc', images, w_value, precision=precise)
    channels = query_key.shape[-1]
    row_count = images.shape[1]
    col_count = images.shape[2]
    joined = jnp.concatenate([query_key, value_proj], axis=-1)
    widened = jnp.pad(joined, ((0, 0), (1, 1), (RAD, RAD), (0, 0)))
    row_ids = jnp.arange(row_count + 2)
    col_ids = jnp.arange(col_count + 2 * RAD)
    row_valid = (row_ids >= 1) & (row_ids <= row_count)
    col_valid = (col_ids >= RAD) & (col_ids < col_count + RAD)
    return window_attention(query_key, value_proj, widened, row_valid, col_valid, channels)


def correlate(left_feat, right_feat, shifts):
    row_count = left_feat.shape[0]
    channels = left_feat.shape[2]
    group_size = channels // CORR_GROUPS
    padded = jnp.pad(right_feat, ((0, 0), (0, TW + DISP), (0, 0)))
    grouped_left = left_feat.reshape(row_count, NTILES, TW, CORR_GROUPS, group_size)
    spread = jnp.arange(TW)[:, None] + jnp.arange(DISP)[None, :]

    def one_tile(tile_pos):
        start = (tile_pos * TW + shifts[tile_pos]).astype(jnp.int32)
        window = lax.dynamic_slice_in_dim(padded, start, TW + DISP - 1, 1)
        taken_cols = window[:, spread, :].reshape(row_count, TW, DISP, CORR_GROUPS, group_size)
        left_tile = lax.dynamic_index_in_dim(grouped_left, tile_pos, 1, keepdims=False)
        return jnp.sum(left_tile[:, :, None] * taken_cols, axis=-1) / group_size

    volume = lax.map(one_tile, jnp.arange(NTILES, dtype=jnp.int32))
    volume = jnp.transpose(volume, (4, 1, 0, 2, 3))
    return volume.reshape(CORR_GROUPS, row_count, NTILES * TW, DISP)


def filter_costs(volume, conv_first, conv_second):
    conv_layout = ('NCHWD', 'OIHWD', 'NCHWD')
    first_out = jax.nn.relu(lax.conv_general_dilated(volume[None], conv_first, (1, 1, 1), ((1, 1), (1, 1), (1, 1)), dimension_numbers=conv_layout, precision=precise))
    second_out = jax.nn.relu(lax.conv_general_dilated(first_out, conv_second, (1, 1, 1), ((1, 1), (1, 1), (1, 1)), dimension_numbers=conv_layout, precision=precise))
    return jnp.sum(second_out[0], axis=0)


def reference(reference_feat, secondary_feat, pair_offsets, w_query_key, w_value, conv_first, conv_second):
    images = jnp.concatenate([reference_feat[None], secondary_feat], axis=0)
    features = attend(images, w_query_key, w_value)
    score_sum = jnp.zeros((reference_feat.shape[0], reference_feat.shape[1], DISP), jnp.float32)
    for pair_pos in range(PAIRS):
        volume = correlate(features[0], features[pair_pos + 1], pair_offsets[pair_pos])
        score_sum = score_sum + filter_costs(volume, conv_first, conv_second)
    row_peak = jnp.max(score_sum, axis=-1, keepdims=True)
    disp_prob = jnp.exp(score_sum - row_peak)
    disp_prob = disp_prob / jnp.sum(disp_prob, axis=-1, keepdims=True)
    levels = jnp.arange(DISP, dtype=jnp.float32)
    return jnp.sum(disp_prob * levels, axis=-1) / DISP
```

```python
import functools
from functools import reduce

import jax
import jax.numpy as jnp
from jax import lax
from jax.experimental import pallas as pl
from jax.experimental.pallas import tpu as pltpu
from jax.sharding import PartitionSpec as P

GROUPS = 8
DISP = 128
RAD = 3
ROWS = 4
CH = 64
LANES = ROWS * CH
HALO = 8
COLS = 6
F32 = jnp.float32
BF16 = jnp.bfloat16


def dot(a, b):
    return jnp.dot(a, b, preferred_element_type=F32)


def split2(x):
    hi = x.astype(BF16)
    return hi, (x - hi.astype(F32)).astype(BF16)


def split3(x):
    hi = x.astype(BF16)
    rest = x - hi.astype(F32)
    mid = rest.astype(BF16)
    return hi, mid, (rest - mid.astype(F32)).astype(BF16)


def attend_kernel(images, width, count, offsets, ref, sec, wq, wv,
                  out_ref, out_sec, out_halo, next0, next1, next2, before, after,
                  left, right, stacked, edges, weights, query, value, scores, send, recv):
    wide = width + 2 * HALO
    tile = lax.axis_index("tile")
    nexts = (next0, next1, next2)

    def present(step):
        return (tile + step >= 0) & (tile + step < count)

    def remote(source, target, place, step):
        return pltpu.make_async_remote_copy(
            src_ref=source, dst_ref=target, send_sem=send.at[place], recv_sem=recv.at[place],
            device_id={"tile": tile + step}, device_id_type=pl.DeviceIdType.MESH)

    barrier = pltpu.get_barrier_semaphore()
    partners = 0
    for step in (1, -1, 3, -3):
        @pl.when(present(step))
        def _(step=step):
            pl.semaphore_signal(barrier, inc=1, device_id={"tile": tile + step}, device_id_type=pl.DeviceIdType.MESH)

        partners = partners + jnp.where(present(step), 1, 0)
    pl.semaphore_wait(barrier, partners)

    tail = pl.ds(width - HALO, HALO)
    head = pl.ds(0, HALO)
    upward = [
        remote(ref.at[:, tail, :], left.at[0], 0, 1),
        remote(sec.at[:, :, tail, :], left.at[pl.ds(1, images - 1)], 1, 1),
        remote(offsets, before, 2, 1),
    ]
    downward = [
        remote(ref.at[:, head, :], right.at[0], 3, -1),
        remote(sec.at[:, :, head, :], right.at[pl.ds(1, images - 1)], 4, -1),
        remote(offsets, after, 5, -1),
    ]
    for step, copies in ((1, upward), (-1, downward)):
        @pl.when(present(step))
        def _(copies=copies):
            for copy in copies:
                copy.start()
    for step, halo, entry in ((-1, left, before), (1, right, after)):
        @pl.when(jnp.logical_not(present(step)))
        def _(halo=halo, entry=entry):
            halo[...] = jnp.zeros_like(halo)
            entry[...] = jnp.zeros_like(entry)
    for step, buffer in ((1, next0), (2, next1), (3, next2)):
        @pl.when(jnp.logical_not(present(step)))
        def _(buffer=buffer):
            buffer[...] = jnp.zeros_like(buffer)

    weights[:, :CH] = wq[...]
    weights[:, CH:] = wv[...]
    zeros = jnp.zeros((HALO, LANES), F32)
    for image in range(images):
        for row in range(ROWS):
            stacked[row * width:(row + 1) * width, :] = ref[row] if image == 0 else sec[image - 1, row]
        both = jnp.dot(stacked[...], weights[...], precision=lax.Precision.HIGHEST, preferred_element_type=F32)
        for row in range(ROWS):
            part = both[row * width:(row + 1) * width, :]
            query[image, 2 * HALO:2 * HALO + width, row * CH:(row + 1) * CH] = part[:, :CH]
            value[image, 2 * HALO:2 * HALO + width, row * CH:(row + 1) * CH] = part[:, CH:]
        for buffer in (query, value):
            buffer[image, 0:HALO, :] = zeros
            buffer[image, HALO + wide:, :] = zeros
    for step, copies in ((1, upward), (-1, downward)):
        @pl.when(present(step))
        def _(copies=copies):
            for copy in copies:
                copy.wait_send()

        @pl.when(present(-step))
        def _(copies=copies):
            for copy in copies:
                copy.wait_recv()
    for image in range(images):
        for row in range(ROWS):
            base = (image * ROWS + row) * 2 * HALO
            edges[base:base + HALO, :] = left[image, row]
            edges[base + HALO:base + 2 * HALO, :] = right[image, row]
    both = jnp.dot(edges[...], weights[...], precision=lax.Precision.HIGHEST, preferred_element_type=F32)
    for image in range(images):
        for row in range(ROWS):
            base = (image * ROWS + row) * 2 * HALO
            lanes = slice(row * CH, (row + 1) * CH)
            query[image, HALO:2 * HALO, lanes] = both[base:base + HALO, :CH]
            value[image, HALO:2 * HALO, lanes] = both[base:base + HALO, CH:]
            query[image, HALO + wide - HALO:HALO + wide, lanes] = both[base + HALO:base + 2 * HALO, :CH]
            value[image, HALO + wide - HALO:HALO + wide, lanes] = both[base + HALO:base + 2 * HALO, CH:]
    ones = jnp.where(
        lax.broadcasted_iota(jnp.int32, (LANES, LANES), 0) // CH
        == lax.broadcasted_iota(jnp.int32, (LANES, LANES), 1) // CH,
        1.0 / CH, 0.0).astype(BF16)

    def attention(image, length):
        lane_row = lax.broadcasted_iota(jnp.int32, (length, LANES), 1) // CH
        column = lax.broadcasted_iota(jnp.int32, (length, LANES), 0) + (tile * width - HALO)
        own = query[image, HALO:HALO + length, :]
        peak = jnp.full((length, LANES), -1e30, F32)
        place = 0
        for shift in range(-RAD, RAD + 1):
            keys = query[image, HALO + shift:HALO + shift + length, :]
            col_ok = (column + shift >= 0) & (column + shift < count * width)
            for step in (-1, 0, 1):
                moved = pltpu.roll(keys, (-step * CH) % LANES, 1) if step else keys
                hi, mid, low = split3(own * moved)
                score = dot(hi, ones) + dot(mid, ones) + dot(low, ones)
                row_ok = (lane_row + step >= 0) & (lane_row + step < ROWS)
                score = jnp.where(col_ok & row_ok, score, -1e30)
                scores[place, :length] = score
                peak = jnp.maximum(peak, score)
                place += 1
        total = jnp.zeros((length, LANES), F32)
        mixed = jnp.zeros((length, LANES), F32)
        place = 0
        for shift in range(-RAD, RAD + 1):
            vals = value[image, HALO + shift:HALO + shift + length, :]
            for step in (-1, 0, 1):
                moved = pltpu.roll(vals, (-step * CH) % LANES, 1) if step else vals
                weight = jnp.exp(scores[place, :length] - peak)
                total = total + weight
                mixed = mixed + weight * moved
                place += 1
        return column, value[image, HALO:HALO + length, :] + mixed / total

    sends = []
    for pair in range(images - 1):
        _, feature = attention(pair + 1, HALO + width)
        out_halo[pair] = feature[:HALO]
        out_sec[pair] = feature[HALO:]
        for step in (1, 3):
            copy = remote(out_sec.at[pair], nexts[step - 1].at[pair], 6 + 3 * pair + step - 1, -step)
            sends.append((step, copy))

            @pl.when(present(-step))
            def _(copy=copy):
                copy.start()

    column, feature = attention(0, wide)
    out_ref[...] = jnp.where((column >= 0) & (column < count * width), feature, 0.0)
    odd = tile % 2 == 1
    forwards = []
    for step, copy in sends:
        @pl.when(present(step))
        def _(copy=copy):
            copy.wait_recv()

        pair = len(forwards) // 2
        source, offset, chosen = (next0, -1, odd) if step == 1 else (next2, 1, jnp.logical_not(odd))
        forward = remote(source.at[pair], next1.at[pair], 7 + 3 * pair, offset)
        going = chosen & present(step)
        forwards.append((going, forward))

        @pl.when(going)
        def _(forward=forward):
            forward.start()

    for step, copy in sends:
        @pl.when(present(-step))
        def _(copy=copy):
            copy.wait_send()

    for going, forward in forwards:
        @pl.when(going)
        def _(forward=forward):
            forward.wait_send()

    for _, forward in forwards[::2]:
        @pl.when(present(2))
        def _(forward=forward):
            forward.wait_recv()


def dot_nt(a, b):
    return lax.dot_general(a, b, (((1,), (1,)), ((), ())), preferred_element_type=F32)


def cost_kernel(pairs, width, info, first, second, feat, halo, sec0, sec1, sec2, sec3, out,
                spread, edge, main, volume_hi, volume_lo, first_hi, first_lo, w_hi, w_lo, sums):
    group = ROWS * GROUPS
    span = COLS * group
    half = LANES // 2
    pad = HALO - 2
    lane = lax.broadcasted_iota(jnp.int32, (8, 128), 1)
    secs = (sec0, sec1, sec2, sec3)

    def doubled(value, row):
        low = lax.broadcasted_iota(jnp.int32, value.shape, 1) < CH
        other = pltpu.roll(value, CH, 1)
        return jnp.where(low, value, other) if row % 2 == 0 else jnp.where(low, other, value)

    def joined(hi, lo, row):
        low = lax.broadcasted_iota(jnp.int32, hi.shape, 1) < CH
        if row % 2 == 0:
            return jnp.where(low, hi, pltpu.roll(lo, CH, 1))
        return jnp.where(low, pltpu.roll(hi, CH, 1), lo)

    def rounded(value):
        hi = value.astype(BF16).astype(F32)
        return hi, value - hi

    for conv, taps in enumerate((first, second)):
        for tap in range(3):
            for row in range(ROWS):
                pieces = []
                for col in range(3):
                    for source in range(ROWS):
                        step = source - row + 1
                        pieces.append(taps[step, col, tap] if 0 <= step < 3 else jnp.zeros((GROUPS, GROUPS), F32))
                pieces.append(jnp.zeros((GROUPS, 128 - 3 * group), F32))
                spread[(conv * 3 + tap) * ROWS + row] = jnp.concatenate(pieces, axis=1)
    zero = jnp.zeros((8, 128), F32)
    for conv in range(2):
        for tap in range(3):
            for col in range(COLS):
                shift = col * group
                lanes = [[], []]
                for row in range(ROWS):
                    base = spread[(conv * 3 + tap) * ROWS + row]
                    turned = pltpu.roll(base, shift % 128, 1) if shift % 128 else base
                    if shift + 3 * group <= 128:
                        parts = (turned, zero)
                    elif shift >= 128:
                        parts = (zero, turned)
                    else:
                        parts = (jnp.where(lane >= shift, turned, 0.0), jnp.where(lane < shift, turned, 0.0))
                    for place in range(2):
                        lanes[place].append(parts[place])
                for place in range(2):
                    hi, lo = split2(jnp.concatenate(lanes[place], axis=0))
                    rows = slice(tap * span + shift, tap * span + shift + group)
                    w_hi[conv, rows, place * 128:(place + 1) * 128] = hi
                    w_lo[conv, rows, place * 128:(place + 1) * 128] = lo

    own_group = (lane % CH) // (CH // GROUPS) == lax.broadcasted_iota(jnp.int32, (8, 128), 0)
    for tile in range(2):
        values = rounded(feat[:, tile * half:(tile + 1) * half] * (1.0 / (CH // GROUPS)))
        for row in (2 * tile, 2 * tile + 1):
            for place, value in enumerate(values):
                edge[row, place] = doubled(value, row)
    count = width + 4
    for row in range(ROWS):
        for place in range(2):
            for col in range(0, count, 2):
                pair_rows = [
                    jnp.where(own_group, jnp.broadcast_to(edge[row, place, pad + at:pad + at + 1, :], (8, 128)), 0.0)
                    for at in (col, col + 1)
                ]
                main[row, col * 8:col * 8 + 16, place * 128:(place + 1) * 128] = (
                    jnp.concatenate(pair_rows, axis=0).astype(BF16))

    for pair in range(pairs):
        for tile in range(2):
            lanes = slice(tile * half, (tile + 1) * half)
            seen = [rounded(sec[pair, :, lanes]) for sec in secs]
            near = rounded(halo[pair, :, lanes])
            products = []
            for row in (2 * tile, 2 * tile + 1):
                parts = [joined(hi, lo, row).astype(BF16) for hi, lo in seen]
                right = jnp.concatenate(parts, axis=0)
                turn = jnp.concatenate(
                    [jnp.zeros((width - HALO, half), F32), joined(*near, row)], axis=0).astype(BF16)
                wrap = jnp.concatenate([parts[2], turn], axis=0)
                whole = dot_nt(main[row], jnp.concatenate([right, right], axis=1))
                ends = dot_nt(main[row, 0:16, :], jnp.concatenate([wrap, wrap], axis=1))
                products.append((whole, ends))
            for col in range(count):
                x = col - 2
                offset = info[3 * pair + (1 if x < 0 else 2 if x >= width else 0)]
                begin = offset + x
                turn = lax.rem(256 - begin, 128)
                own = (lane + begin >= 0) & (lane + begin < 128)
                values = []
                for whole, ends in products:
                    rows = slice(col * 8, (col + 1) * 8)
                    a = whole[rows, 0:128]
                    b = ends[rows] if x < 0 else whole[rows, 128:256]
                    values.append(jnp.where(own, pltpu.roll(a, turn, 1), pltpu.roll(b, turn, 1)))
                hi, lo = split2(jnp.concatenate(values, axis=0))
                rows = slice(col * group + tile * 16, col * group + tile * 16 + 16)
                volume_hi[rows, pair * 128:(pair + 1) * 128] = hi
                volume_lo[rows, pair * 128:(pair + 1) * 128] = lo

    def convolved(conv, hi_ref, lo_ref, start, cols):
        rows = slice(start * group, (start + cols + 2) * group)
        hi, lo = hi_ref[rows, :], lo_ref[rows, :]
        if cols == COLS:
            wh, wl = w_hi[conv], w_lo[conv]
        else:
            picked = [
                jnp.concatenate([w[conv, tap * span:tap * span + cols * group, 0:(cols + 2) * group]
                                 for tap in range(3)], axis=0)
                for w in (w_hi, w_lo)
            ]
            wh, wl = picked
        both = dot(wh, hi) + dot(wl, hi) + dot(wh, lo)
        size = cols * group
        level = lax.broadcasted_iota(jnp.int32, (size, 128), 1)
        result = []
        for pair in range(pairs):
            lanes = slice(pair * 128, (pair + 1) * 128)
            before = jnp.where(level >= 1, pltpu.roll(both[0:size, lanes], 1, 1), 0.0)
            after = jnp.where(level < DISP - 1, pltpu.roll(both[2 * size:, lanes], 127, 1), 0.0)
            result.append(jnp.maximum(both[size:2 * size, lanes] + before + after, 0.0))
        return result

    is_first, is_last = info[3 * pairs], info[3 * pairs + 1]
    for start in range(0, width + 2, COLS):
        cols = min(COLS, width + 2 - start)
        results = convolved(0, volume_hi, volume_lo, start, cols)
        at = lax.broadcasted_iota(jnp.int32, (cols * group, 128), 0)
        for pair in range(pairs):
            value = results[pair]
            if start == 0:
                value = jnp.where((at < group) & (is_first == 1), 0.0, value)
            if start + cols == width + 2:
                value = jnp.where((at >= (cols - 1) * group) & (is_last == 1), 0.0, value)
            hi, lo = split2(value)
            rows = slice(start * group, (start + cols) * group)
            first_hi[rows, pair * 128:(pair + 1) * 128] = hi
            first_lo[rows, pair * 128:(pair + 1) * 128] = lo
    for start in range(0, width, COLS):
        cols = min(COLS, width - start)
        total = reduce(jnp.add, convolved(1, first_hi, first_lo, start, cols))
        score = jnp.sum(total.reshape(cols * ROWS, GROUPS, 128), axis=1)
        sums[start * ROWS:(start + cols) * ROWS, :] = score
    score = sums[...]
    weight = jnp.exp(score - jnp.max(score, axis=1, keepdims=True))
    level = lax.broadcasted_iota(jnp.int32, score.shape, 1).astype(F32)
    mean = jnp.sum(weight * level, axis=1, keepdims=True) / (jnp.sum(weight, axis=1, keepdims=True) * DISP)
    pixel = lax.broadcasted_iota(jnp.int32, score.shape, 0)
    placed = jnp.where(pixel // ROWS == lax.broadcasted_iota(jnp.int32, score.shape, 1), mean, 0.0)
    pick = jnp.where(
        lax.broadcasted_iota(jnp.int32, (16, width * ROWS), 1) % ROWS
        == lax.broadcasted_iota(jnp.int32, (16, width * ROWS), 0), 1.0, 0.0).astype(BF16)
    final = reduce(jnp.add, [dot(pick, part) for part in split3(placed)])
    out[...] = final[:ROWS, :width]


def exchange(pairs, width, count, features):
    images = pairs + 1
    wide = width + 2 * HALO
    vmem = pl.BlockSpec(memory_space=pltpu.VMEM)
    shifted = jax.ShapeDtypeStruct((pairs, width, LANES), F32)
    entry = jax.ShapeDtypeStruct((pairs, 128), jnp.int32)
    copies = 6 + 3 * pairs

    def ordered(*args):
        feat, own, halo, next0, next1, next2, before, after = call(*args)
        return feat, halo, own, next0, next1, next2, before, after

    call = pl.pallas_call(
        functools.partial(attend_kernel, images, width, count),
        out_shape=(
            jax.ShapeDtypeStruct((wide, LANES), F32),
            shifted,
            jax.ShapeDtypeStruct((pairs, HALO, LANES), F32),
            shifted, shifted, shifted, entry, entry,
        ),
        in_specs=[vmem] * 5,
        out_specs=(vmem,) * 8,
        scratch_shapes=[
            pltpu.VMEM((images, ROWS, HALO, features), F32),
            pltpu.VMEM((images, ROWS, HALO, features), F32),
            pltpu.VMEM((ROWS * width, features), F32),
            pltpu.VMEM((images * ROWS * 2 * HALO, features), F32),
            pltpu.VMEM((features, 2 * CH), F32),
            pltpu.VMEM((images, wide + 2 * HALO, LANES), F32),
            pltpu.VMEM((images, wide + 2 * HALO, LANES), F32),
            pltpu.VMEM((3 * (2 * RAD + 1), wide, LANES), F32),
            pltpu.SemaphoreType.DMA((copies,)),
            pltpu.SemaphoreType.DMA((copies,)),
        ],
        compiler_params=pltpu.CompilerParams(
            vmem_limit_bytes=24 << 20, collective_id=0, has_side_effects=True),
    )
    return ordered


def on_device(reference_feat, secondary_feat, pair_offsets, w_query_key, w_value, conv_first, conv_second):
    pairs = secondary_feat.shape[0]
    width = reference_feat.shape[1]
    tile_id = lax.axis_index("tile")
    count = lax.axis_size("tile")
    group = ROWS * GROUPS
    vmem = pl.BlockSpec(memory_space=pltpu.VMEM)
    smem = pl.BlockSpec(memory_space=pltpu.SMEM)
    features = reference_feat.shape[2]
    entries = jnp.broadcast_to(pair_offsets, (pairs, 128))
    first, second = (jnp.transpose(conv, (2, 3, 4, 0, 1)) for conv in (conv_first, conv_second))
    feat, halo, own, next0, next1, next2, before, after = exchange(
        pairs, width, lax.axis_size("tile"), features)(entries, reference_feat, secondary_feat, w_query_key, w_value)
    info = jnp.concatenate([
        jnp.concatenate([pair_offsets, before[:, :1], after[:, :1]], axis=1).reshape(-1),
        jnp.stack([tile_id == 0, tile_id == count - 1]).astype(jnp.int32),
    ])
    lanes = pairs * DISP
    return pl.pallas_call(
        functools.partial(cost_kernel, pairs, width),
        out_shape=jax.ShapeDtypeStruct((ROWS, width), F32),
        in_specs=[smem] + [vmem] * 8,
        out_specs=vmem,
        scratch_shapes=[
            pltpu.VMEM((6 * ROWS, GROUPS, 128), F32),
            pltpu.VMEM((ROWS, 2, width + 2 * HALO, 128), F32),
            pltpu.VMEM((ROWS, (width + 4) * GROUPS, 256), BF16),
            pltpu.VMEM(((width + 4) * group, lanes), BF16),
            pltpu.VMEM(((width + 4) * group, lanes), BF16),
            pltpu.VMEM(((width + 2) * group, lanes), BF16),
            pltpu.VMEM(((width + 2) * group, lanes), BF16),
            pltpu.VMEM((2, 3 * COLS * group, (COLS + 2) * group), BF16),
            pltpu.VMEM((2, 3 * COLS * group, (COLS + 2) * group), BF16),
            pltpu.VMEM((width * ROWS, 128), F32),
        ],
        compiler_params=pltpu.CompilerParams(vmem_limit_bytes=48 << 20),
    )(info, first, second, feat, halo, own, next0, next1, next2)


def solution(mesh):
    return jax.shard_map(
        on_device,
        mesh=mesh,
        in_specs=(
            P("groups", "tile", None),
            P("groups", None, "tile", None),
            P("groups", "tile"),
            P(),
            P(),
            P(),
            P(),
        ),
        out_specs=P("groups", "tile"),
        check_vma=False,
    )
```

```python
import functools
from functools import reduce

import jax
import jax.numpy as jnp
from jax import lax
from jax.experimental import pallas as pl
from jax.experimental.pallas import tpu as pltpu
from jax.sharding import PartitionSpec as P

GROUPS = 8
DISP = 128
RAD = 3
ROWS = 4
CH = 64
LANES = ROWS * CH
HALO = 8
COLS = 6
F32 = jnp.float32
BF16 = jnp.bfloat16


def dot(a, b):
    return jnp.dot(a, b, preferred_element_type=F32)


def split2(x):
    hi = x.astype(BF16)
    return hi, (x - hi.astype(F32)).astype(BF16)


def split3(x):
    hi = x.astype(BF16)
    rest = x - hi.astype(F32)
    mid = rest.astype(BF16)
    return hi, mid, (rest - mid.astype(F32)).astype(BF16)


def dot_nt(a, b):
    return lax.dot_general(a, b, (((1,), (1,)), ((), ())), preferred_element_type=F32)


def rounded(value):
    hi = value.astype(BF16).astype(F32)
    return hi, value - hi


def lower_half(value):
    return lax.broadcasted_iota(jnp.int32, value.shape, 1) < CH


def band_weights(taps, spread, w_hi, w_lo):
    group = ROWS * GROUPS
    span = COLS * group
    lane = lax.broadcasted_iota(jnp.int32, (8, 128), 1)
    for conv in range(2):
        for tap in range(3):
            for row in range(ROWS):
                pieces = []
                for col in range(3):
                    for source in range(ROWS):
                        step = source - row + 1
                        pieces.append(taps[conv, step, col, tap] if 0 <= step < 3 else jnp.zeros((GROUPS, GROUPS), F32))
                pieces.append(jnp.zeros((GROUPS, 128 - 3 * group), F32))
                spread[(conv * 3 + tap) * ROWS + row] = jnp.concatenate(pieces, axis=1)
    zero = jnp.zeros((8, 128), F32)
    for conv in range(2):
        for tap in range(3):
            for col in range(COLS):
                shift = col * group
                lanes = [[], []]
                for row in range(ROWS):
                    base = spread[(conv * 3 + tap) * ROWS + row]
                    turned = pltpu.roll(base, shift % 128, 1) if shift % 128 else base
                    if shift + 3 * group <= 128:
                        parts = (turned, zero)
                    elif shift >= 128:
                        parts = (zero, turned)
                    else:
                        parts = (jnp.where(lane >= shift, turned, 0.0), jnp.where(lane < shift, turned, 0.0))
                    for place in range(2):
                        lanes[place].append(parts[place])
                for place in range(2):
                    hi, lo = split2(jnp.concatenate(lanes[place], axis=0))
                    rows = slice(tap * span + shift, tap * span + shift + group)
                    w_hi[conv, rows, place * 128:(place + 1) * 128] = hi
                    w_lo[conv, rows, place * 128:(place + 1) * 128] = lo


def attend_kernel(images, width, count, offsets, ref, sec, wq, wv, first, second,
                  main, w_hi, w_lo, out_sec, out_halo, next0, next1, next2, before, after,
                  left, right, own, weights, taps, spread, projected, bias, keys, values, edge, local, send, recv):
    wide = width + 2 * HALO
    reach = 256
    tile = lax.axis_index("tile")
    nexts = (next0, next1, next2)

    def present(step):
        return (tile + step >= 0) & (tile + step < count)

    def remote(source, target, place, step):
        return pltpu.make_async_remote_copy(
            src_ref=source, dst_ref=target, send_sem=send.at[place], recv_sem=recv.at[place],
            device_id={"tile": tile + step}, device_id_type=pl.DeviceIdType.MESH)

    barrier = pltpu.get_barrier_semaphore()
    partners = 0
    for step in (1, -1, 3, -3):
        @pl.when(present(step))
        def _(step=step):
            pl.semaphore_signal(barrier, inc=1, device_id={"tile": tile + step}, device_id_type=pl.DeviceIdType.MESH)

        partners = partners + jnp.where(present(step), 1, 0)
    loads = [
        pltpu.make_async_copy(source, target, local.at[place])
        for place, (source, target) in enumerate((
            (wq, weights.at[pl.ds(0, CH)]),
            (wv, weights.at[pl.ds(CH, CH)]),
            (sec, own.at[pl.ds(1, images - 1)]),
            (ref, own.at[0]),
            (first, taps.at[0]),
            (second, taps.at[1]),
        ))
    ]
    for load in loads:
        load.start()
    pl.semaphore_wait(barrier, partners)

    tail = pl.ds(width - HALO, HALO)
    head = pl.ds(0, HALO)
    upward = [
        remote(sec.at[:, :, tail, :], left.at[pl.ds(1, images - 1)], 1, 1),
        remote(ref.at[:, tail, :], left.at[0], 0, 1),
        remote(offsets, before, 2, 1),
    ]
    downward = [
        remote(sec.at[:, :, head, :], right.at[pl.ds(1, images - 1)], 4, -1),
        remote(ref.at[:, head, :], right.at[0], 3, -1),
        remote(offsets, after, 5, -1),
    ]
    for step, copies in ((1, upward), (-1, downward)):
        @pl.when(present(step))
        def _(copies=copies):
            for copy in copies:
                copy.start()
    for step, halo, entry in ((-1, left, before), (1, right, after)):
        @pl.when(jnp.logical_not(present(step)))
        def _(halo=halo, entry=entry):
            halo[...] = jnp.zeros_like(halo)
            entry[...] = jnp.zeros_like(entry)
    for step, buffer in ((1, next0), (2, next1), (3, next2)):
        @pl.when(jnp.logical_not(present(step)))
        def _(buffer=buffer):
            buffer[...] = jnp.zeros_like(buffer)

    lane = lax.broadcasted_iota(jnp.int32, (wide, reach), 1)
    query = lax.broadcasted_iota(jnp.int32, (wide, reach), 0)
    key = lane - jnp.where(lane >= 2 * wide, 2 * wide, jnp.where(lane >= wide, wide, 0))
    column = key + (tile * width - HALO)
    near = (key - query <= RAD) & (query - key <= RAD) & (column >= 0) & (column < count * width) & (lane < 3 * wide)
    for row in range(ROWS):
        allowed = near
        if row == 0:
            allowed = allowed & (lane >= wide)
        if row == ROWS - 1:
            allowed = allowed & (lane < 2 * wide)
        bias[row] = jnp.where(allowed, 0.0, -1e30)
    for image in range(images):
        for at, size in ((0, wide), ((ROWS + 1) * wide, reach - 2 * wide)):
            keys[image, at:at + size, :] = jnp.zeros((size, 128), BF16)
            values[image, at:at + size, :] = jnp.zeros((size, 128), BF16)
    loads[0].wait()
    loads[1].wait()
    packed = jnp.concatenate(split2(weights[...]), axis=0)

    def project(value):
        hi, lo = split2(value)
        both = dot_nt(hi, packed) + dot_nt(lo, packed)
        return both[:, :128] + both[:, 128:]

    loads[2].wait()
    loads[3].wait()
    for image in (*range(1, images), 0):
        both = project(own[image].reshape(ROWS * width, own.shape[3]))
        for row in range(ROWS):
            projected[image, row, HALO:HALO + width, :] = both[row * width:(row + 1) * width]
    loads[4].wait()
    loads[5].wait()
    band_weights(taps, spread, w_hi, w_lo)
    for step, copies in ((1, upward), (-1, downward)):
        @pl.when(present(step))
        def _(copies=copies):
            for copy in copies:
                copy.wait_send()

        @pl.when(present(-step))
        def _(copies=copies):
            for copy in copies:
                copy.wait_recv()
    span = images * ROWS * HALO
    both = project(jnp.concatenate(
        [left[...].reshape(span, own.shape[3]), right[...].reshape(span, own.shape[3])], axis=0))
    for image in range(images):
        for row in range(ROWS):
            base = (image * ROWS + row) * HALO
            projected[image, row, 0:HALO, :] = both[base:base + HALO]
            projected[image, row, HALO + width:wide, :] = both[span + base:span + base + HALO]
    ones = jnp.ones((reach, 128), BF16)

    def attention(image):
        queries = []
        for row in range(ROWS):
            value = projected[image, row]
            low = lower_half(value)
            hi, rest = rounded(value)
            turned_hi, turned_rest = pltpu.roll(hi, CH, 1), pltpu.roll(rest, CH, 1)
            queries.append(jnp.concatenate(
                [jnp.where(low, hi, turned_hi) * (1.0 / CH), jnp.where(low, rest, turned_rest) * (1.0 / CH)],
                axis=1).astype(BF16))
            rows = slice((row + 1) * wide, (row + 2) * wide)
            keys[image, rows, :] = jnp.where(low, hi, turned_rest).astype(BF16)
            values[image, rows, :] = jnp.where(low, turned_hi, rest).astype(BF16)
        result = []
        for row in range(ROWS):
            rows = slice(row * wide, row * wide + reach)
            seen = keys[image, rows, :]
            score = dot_nt(queries[row], jnp.concatenate([seen, seen], axis=1)) + bias[row]
            weight = jnp.exp(score - jnp.max(score, axis=1, keepdims=True))
            hi, lo = split2(weight)
            mixed = jnp.concatenate([values[image, rows, :], ones], axis=1)
            total = dot(hi, mixed) + dot(lo, mixed)
            shared = total[:, :128] + pltpu.roll(total[:, :128], CH, 1)
            value = projected[image, row]
            value = jnp.where(lower_half(value), pltpu.roll(value, CH, 1), value)
            result.append(value + shared / total[:, 128:])
        return result

    sends = []
    for pair in range(images - 1):
        parts = attention(pair + 1)
        for place in range(2):
            feature = jnp.where(lower_half(parts[0]), parts[2 * place], parts[2 * place + 1])
            out_halo[pair, :, place * 128:(place + 1) * 128] = feature[:HALO]
            out_sec[pair, :, place * 128:(place + 1) * 128] = feature[HALO:HALO + width]
        for step in (1, 3):
            copy = remote(out_sec.at[pair], nexts[step - 1].at[pair], 6 + 3 * pair + step - 1, -step)
            sends.append((step, copy))

            @pl.when(present(-step))
            def _(copy=copy):
                copy.start()

    column = lax.broadcasted_iota(jnp.int32, (wide, 128), 0) + (tile * width - HALO)
    inside = (column >= 0) & (column < count * width)
    for row, feature in enumerate(attention(0)):
        for place, part in enumerate(rounded(jnp.where(inside, feature, 0.0) * (1.0 / (CH // GROUPS)))):
            edge[row, place] = part
    small = lax.broadcasted_iota(jnp.int32, (8, 128), 1)
    own_group = (small % CH) // (CH // GROUPS) == lax.broadcasted_iota(jnp.int32, (8, 128), 0)
    pad = HALO - 2
    for row in range(ROWS):
        for place in range(2):
            for col in range(0, width + 4, 2):
                pair_rows = [
                    jnp.where(own_group, jnp.broadcast_to(edge[row, place, pad + at:pad + at + 1, :], (8, 128)), 0.0)
                    for at in (col, col + 1)
                ]
                main[row, col * 8:col * 8 + 16, place * 128:(place + 1) * 128] = (
                    jnp.concatenate(pair_rows, axis=0).astype(BF16))
    odd = tile % 2 == 1
    forwards = []
    for step, copy in sends:
        @pl.when(present(step))
        def _(copy=copy):
            copy.wait_recv()

        pair = len(forwards) // 2
        source, offset, chosen = (next0, -1, odd) if step == 1 else (next2, 1, jnp.logical_not(odd))
        forward = remote(source.at[pair], next1.at[pair], 7 + 3 * pair, offset)
        going = chosen & present(step)
        forwards.append((going, forward))

        @pl.when(going)
        def _(forward=forward):
            forward.start()

    for step, copy in sends:
        @pl.when(present(-step))
        def _(copy=copy):
            copy.wait_send()

    for going, forward in forwards:
        @pl.when(going)
        def _(forward=forward):
            forward.wait_send()

    for _, forward in forwards[::2]:
        @pl.when(present(2))
        def _(forward=forward):
            forward.wait_recv()


def cost_kernel(pairs, width, tiles, offsets, before, after, main, w_hi, w_lo, halo, sec0, sec1, sec2, sec3, out,
                volume_hi, volume_lo, first_hi, first_lo, sums):
    tile_at = lax.axis_index("tile")
    count = width + 4
    group = ROWS * GROUPS
    span = COLS * group
    half = LANES // 2
    lane = lax.broadcasted_iota(jnp.int32, (8, 128), 1)
    secs = (sec0, sec1, sec2, sec3)

    def joined(hi, lo, row):
        low = lax.broadcasted_iota(jnp.int32, hi.shape, 1) < CH
        if row % 2 == 0:
            return jnp.where(low, hi, pltpu.roll(lo, CH, 1))
        return jnp.where(low, pltpu.roll(hi, CH, 1), lo)

    for pair in range(pairs):
        for tile in range(2):
            lanes = slice(tile * half, (tile + 1) * half)
            seen = [rounded(sec[pair, :, lanes]) for sec in secs]
            near = rounded(halo[pair, :, lanes])
            products = []
            for row in (2 * tile, 2 * tile + 1):
                parts = [joined(hi, lo, row).astype(BF16) for hi, lo in seen]
                right = jnp.concatenate(parts, axis=0)
                turn = jnp.concatenate(
                    [jnp.zeros((width - HALO, half), F32), joined(*near, row)], axis=0).astype(BF16)
                wrap = jnp.concatenate([parts[2], turn], axis=0)
                whole = dot_nt(main[row], jnp.concatenate([right, right], axis=1))
                ends = dot_nt(main[row, 0:16, :], jnp.concatenate([wrap, wrap], axis=1))
                products.append((whole, ends))
            for col in range(count):
                x = col - 2
                offset = (before if x < 0 else after if x >= width else offsets)[0, pair]
                begin = offset + x
                turn = lax.rem(256 - begin, 128)
                own = (lane + begin >= 0) & (lane + begin < 128)
                values = []
                for whole, ends in products:
                    rows = slice(col * 8, (col + 1) * 8)
                    a = whole[rows, 0:128]
                    b = ends[rows] if x < 0 else whole[rows, 128:256]
                    values.append(jnp.where(own, pltpu.roll(a, turn, 1), pltpu.roll(b, turn, 1)))
                hi, lo = split2(jnp.concatenate(values, axis=0))
                rows = slice(col * group + tile * 16, col * group + tile * 16 + 16)
                volume_hi[rows, pair * 128:(pair + 1) * 128] = hi
                volume_lo[rows, pair * 128:(pair + 1) * 128] = lo

    def convolved(conv, hi_ref, lo_ref, start, cols):
        rows = slice(start * group, (start + cols + 2) * group)
        hi, lo = hi_ref[rows, :], lo_ref[rows, :]
        if cols == COLS:
            wh, wl = w_hi[conv], w_lo[conv]
        else:
            picked = [
                jnp.concatenate([w[conv, tap * span:tap * span + cols * group, 0:(cols + 2) * group]
                                 for tap in range(3)], axis=0)
                for w in (w_hi, w_lo)
            ]
            wh, wl = picked
        both = dot(wh, hi) + dot(wl, hi) + dot(wh, lo)
        size = cols * group
        level = lax.broadcasted_iota(jnp.int32, (size, 128), 1)
        result = []
        for pair in range(pairs):
            lanes = slice(pair * 128, (pair + 1) * 128)
            before = jnp.where(level >= 1, pltpu.roll(both[0:size, lanes], 1, 1), 0.0)
            after = jnp.where(level < DISP - 1, pltpu.roll(both[2 * size:, lanes], 127, 1), 0.0)
            result.append(jnp.maximum(both[size:2 * size, lanes] + before + after, 0.0))
        return result

    for start in range(0, width + 2, COLS):
        cols = min(COLS, width + 2 - start)
        results = convolved(0, volume_hi, volume_lo, start, cols)
        at = lax.broadcasted_iota(jnp.int32, (cols * group, 128), 0)
        for pair in range(pairs):
            value = results[pair]
            if start == 0:
                value = jnp.where((at < group) & (tile_at == 0), 0.0, value)
            if start + cols == width + 2:
                value = jnp.where((at >= (cols - 1) * group) & (tile_at == tiles - 1), 0.0, value)
            hi, lo = split2(value)
            rows = slice(start * group, (start + cols) * group)
            first_hi[rows, pair * 128:(pair + 1) * 128] = hi
            first_lo[rows, pair * 128:(pair + 1) * 128] = lo
    for start in range(0, width, COLS):
        cols = min(COLS, width - start)
        total = reduce(jnp.add, convolved(1, first_hi, first_lo, start, cols))
        score = jnp.sum(total.reshape(cols * ROWS, GROUPS, 128), axis=1)
        sums[start * ROWS:(start + cols) * ROWS, :] = score
    score = sums[...]
    weight = jnp.exp(score - jnp.max(score, axis=1, keepdims=True))
    level = lax.broadcasted_iota(jnp.int32, score.shape, 1).astype(F32)
    mean = jnp.sum(weight * level, axis=1, keepdims=True) / (jnp.sum(weight, axis=1, keepdims=True) * DISP)
    pixel = lax.broadcasted_iota(jnp.int32, score.shape, 0)
    placed = jnp.where(pixel // ROWS == lax.broadcasted_iota(jnp.int32, score.shape, 1), mean, 0.0)
    pick = jnp.where(
        lax.broadcasted_iota(jnp.int32, (16, width * ROWS), 1) % ROWS
        == lax.broadcasted_iota(jnp.int32, (16, width * ROWS), 0), 1.0, 0.0).astype(BF16)
    final = reduce(jnp.add, [dot(pick, part) for part in split3(placed)])
    out[...] = final[:ROWS, :width]


def exchange(pairs, width, count, features):
    images = pairs + 1
    wide = width + 2 * HALO
    vmem = pl.BlockSpec(memory_space=pltpu.VMEM)
    hbm = pl.BlockSpec(memory_space=pltpu.HBM)
    shifted = jax.ShapeDtypeStruct((pairs, width, LANES), F32)
    entry = jax.ShapeDtypeStruct((1, pairs), jnp.int32)
    banded = jax.ShapeDtypeStruct((2, 3 * COLS * ROWS * GROUPS, (COLS + 2) * ROWS * GROUPS), BF16)
    copies = 6 + 3 * pairs
    held = (ROWS + 2) * wide + 2 * 128 - 3 * wide
    return pl.pallas_call(
        functools.partial(attend_kernel, images, width, count),
        out_shape=(
            jax.ShapeDtypeStruct((ROWS, (width + 4) * GROUPS, 256), BF16),
            banded, banded,
            shifted,
            jax.ShapeDtypeStruct((pairs, HALO, LANES), F32),
            shifted, shifted, shifted, entry, entry,
        ),
        in_specs=[hbm] * 7,
        out_specs=(vmem,) * 10,
        scratch_shapes=[
            pltpu.VMEM((images, ROWS, HALO, features), F32),
            pltpu.VMEM((images, ROWS, HALO, features), F32),
            pltpu.VMEM((images, ROWS, width, features), F32),
            pltpu.VMEM((2 * CH, features), F32),
            pltpu.VMEM((2, 3, 3, 3, GROUPS, GROUPS), F32),
            pltpu.VMEM((6 * ROWS, GROUPS, 128), F32),
            pltpu.VMEM((images, ROWS, wide, 2 * CH), F32),
            pltpu.VMEM((ROWS, wide, 256), F32),
            pltpu.VMEM((images, held, 128), BF16),
            pltpu.VMEM((images, held, 128), BF16),
            pltpu.VMEM((ROWS, 2, wide, 128), F32),
            pltpu.SemaphoreType.DMA((6,)),
            pltpu.SemaphoreType.DMA((copies,)),
            pltpu.SemaphoreType.DMA((copies,)),
        ],
        compiler_params=pltpu.CompilerParams(
            vmem_limit_bytes=24 << 20, collective_id=0, has_side_effects=True),
    )


def on_device(reference_feat, secondary_feat, pair_offsets, w_query_key, w_value, conv_first, conv_second):
    pairs = secondary_feat.shape[0]
    width = reference_feat.shape[1]
    count = lax.axis_size("tile")
    group = ROWS * GROUPS
    vmem = pl.BlockSpec(memory_space=pltpu.VMEM)
    smem = pl.BlockSpec(memory_space=pltpu.SMEM)
    offsets = pair_offsets.T
    first, second = (jnp.transpose(conv, (2, 3, 4, 0, 1)) for conv in (conv_first, conv_second))
    main, w_hi, w_lo, own, halo, next0, next1, next2, before, after = exchange(
        pairs, width, count, reference_feat.shape[2])(
            offsets, reference_feat, secondary_feat, w_query_key.T, w_value.T, first, second)
    lanes = pairs * DISP
    return pl.pallas_call(
        functools.partial(cost_kernel, pairs, width, count),
        out_shape=jax.ShapeDtypeStruct((ROWS, width), F32),
        in_specs=[smem] * 3 + [vmem] * 8,
        out_specs=vmem,
        scratch_shapes=[
            pltpu.VMEM(((width + 4) * group, lanes), BF16),
            pltpu.VMEM(((width + 4) * group, lanes), BF16),
            pltpu.VMEM(((width + 2) * group, lanes), BF16),
            pltpu.VMEM(((width + 2) * group, lanes), BF16),
            pltpu.VMEM((width * ROWS, 128), F32),
        ],
        compiler_params=pltpu.CompilerParams(vmem_limit_bytes=40 << 20),
    )(offsets, before, after, main, w_hi, w_lo, halo, own, next0, next1, next2)


def solution(mesh):
    return jax.shard_map(
        on_device,
        mesh=mesh,
        in_specs=(
            P("groups", "tile", None),
            P("groups", None, "tile", None),
            P("groups", "tile"),
            P(),
            P(),
            P(),
            P(),
        ),
        out_specs=P("groups", "tile"),
        check_vma=False,
    )
```

```python
import functools
from functools import reduce

import jax
import jax.numpy as jnp
from jax import lax
from jax.experimental import pallas as pl
from jax.experimental.pallas import tpu as pltpu
from jax.sharding import PartitionSpec as P

GROUPS = 8
DISP = 128
RAD = 3
ROWS = 4
CH = 64
LANES = ROWS * CH
HALO = 8
COLS = 6
F32 = jnp.float32
BF16 = jnp.bfloat16


def dot(a, b):
    return jnp.dot(a, b, preferred_element_type=F32)


def split2(x):
    hi = x.astype(BF16)
    return hi, (x - hi.astype(F32)).astype(BF16)


def split3(x):
    hi = x.astype(BF16)
    rest = x - hi.astype(F32)
    mid = rest.astype(BF16)
    return hi, mid, (rest - mid.astype(F32)).astype(BF16)


def dot_nt(a, b):
    return lax.dot_general(a, b, (((1,), (1,)), ((), ())), preferred_element_type=F32)


def rounded(value):
    hi = value.astype(BF16).astype(F32)
    return hi, value - hi


def lower_half(value):
    return lax.broadcasted_iota(jnp.int32, value.shape, 1) < CH


def band_weights(taps, spread, w_hi, w_lo):
    group = ROWS * GROUPS
    span = COLS * group
    lane = lax.broadcasted_iota(jnp.int32, (8, 128), 1)
    for conv in range(2):
        for tap in range(3):
            for row in range(ROWS):
                pieces = []
                for col in range(3):
                    for source in range(ROWS):
                        step = source - row + 1
                        pieces.append(taps[conv, step, col, tap] if 0 <= step < 3 else jnp.zeros((GROUPS, GROUPS), F32))
                pieces.append(jnp.zeros((GROUPS, 128 - 3 * group), F32))
                spread[(conv * 3 + tap) * ROWS + row] = jnp.concatenate(pieces, axis=1)
    zero = jnp.zeros((8, 128), F32)
    for conv in range(2):
        for tap in range(3):
            for col in range(COLS):
                shift = col * group
                lanes = [[], []]
                for row in range(ROWS):
                    base = spread[(conv * 3 + tap) * ROWS + row]
                    turned = pltpu.roll(base, shift % 128, 1) if shift % 128 else base
                    if shift + 3 * group <= 128:
                        parts = (turned, zero)
                    elif shift >= 128:
                        parts = (zero, turned)
                    else:
                        parts = (jnp.where(lane >= shift, turned, 0.0), jnp.where(lane < shift, turned, 0.0))
                    for place in range(2):
                        lanes[place].append(parts[place])
                for place in range(2):
                    hi, lo = split2(jnp.concatenate(lanes[place], axis=0))
                    rows = slice(tap * span + shift, tap * span + shift + group)
                    w_hi[conv, rows, place * 128:(place + 1) * 128] = hi
                    w_lo[conv, rows, place * 128:(place + 1) * 128] = lo


def stereo_kernel(images, width, count, offsets, ref, sec, wq, wv, first, second, out,
                  left, right, own, weights, taps, spread, projected, bias, queries, keys, values, edge, main,
                  w_hi, w_lo, middle, rim, behind, before, after, shifts,
                  volume_hi, volume_lo, first_hi, first_lo, sums, local, send, recv):
    pairs = images - 1
    wide = width + 2 * HALO
    reach = 256
    group = ROWS * GROUPS
    span = COLS * group
    tile = lax.axis_index("tile")
    lane = lax.broadcasted_iota(jnp.int32, (8, 128), 1)

    def present(step):
        return (tile + step >= 0) & (tile + step < count)

    def remote(source, target, place, step):
        return pltpu.make_async_remote_copy(
            src_ref=source, dst_ref=target, send_sem=send.at[place], recv_sem=recv.at[place],
            device_id={"tile": tile + step}, device_id_type=pl.DeviceIdType.MESH)

    barrier = pltpu.get_barrier_semaphore()
    partners = 0
    for step in (1, -1, 2, -2, 3, -3):
        @pl.when(present(step))
        def _(step=step):
            pl.semaphore_signal(barrier, inc=1, device_id={"tile": tile + step}, device_id_type=pl.DeviceIdType.MESH)

        partners = partners + jnp.where(present(step), 1, 0)
    loads = [
        pltpu.make_async_copy(source, target, local.at[place])
        for place, (source, target) in enumerate((
            (wq, weights.at[pl.ds(0, CH)]),
            (wv, weights.at[pl.ds(CH, CH)]),
            (sec, own.at[pl.ds(1, pairs)]),
            (ref, own.at[0]),
            (first, taps.at[0]),
            (second, taps.at[1]),
            (offsets, shifts.at[0]),
        ))
    ]
    for load in loads:
        load.start()
    pl.semaphore_wait(barrier, partners)

    tail = pl.ds(width - HALO, HALO)
    head = pl.ds(0, HALO)
    upward = [
        remote(sec.at[:, :, tail, :], left.at[pl.ds(1, pairs)], 0, 1),
        remote(ref.at[:, tail, :], left.at[0], 1, 1),
        remote(offsets, before, 2, 1),
    ]
    downward = [
        remote(sec.at[:, :, head, :], right.at[pl.ds(1, pairs)], 3, -1),
        remote(ref.at[:, head, :], right.at[0], 4, -1),
        remote(offsets, after, 5, -1),
    ]
    for step, copies in ((1, upward), (-1, downward)):
        @pl.when(present(step))
        def _(copies=copies):
            for copy in copies:
                copy.start()
    for step, halo, entry in ((-1, left, before), (1, right, after)):
        @pl.when(jnp.logical_not(present(step)))
        def _(halo=halo, entry=entry):
            halo[...] = jnp.zeros_like(halo)
            entry[...] = jnp.zeros_like(entry)
    for step in (1, 2, 3):
        @pl.when(jnp.logical_not(present(step)))
        def _(step=step):
            middle[step] = jnp.zeros(middle.shape[1:], F32)
            rim[step] = jnp.zeros(rim.shape[1:], F32)

    spot = lax.broadcasted_iota(jnp.int32, (wide, reach), 1)
    query = lax.broadcasted_iota(jnp.int32, (wide, reach), 0)
    key = spot - jnp.where(spot >= 2 * wide, 2 * wide, jnp.where(spot >= wide, wide, 0))
    column = key + (tile * width - HALO)
    near = (key - query <= RAD) & (query - key <= RAD) & (column >= 0) & (column < count * width) & (spot < 3 * wide)
    for row in range(ROWS):
        allowed = near
        if row == 0:
            allowed = allowed & (spot >= wide)
        if row == ROWS - 1:
            allowed = allowed & (spot < 2 * wide)
        bias[row] = jnp.where(allowed, 0.0, -1e30)
    for image in range(images):
        for at, size in ((0, wide), ((ROWS + 1) * wide, reach - 2 * wide)):
            keys[image, at:at + size, :] = jnp.zeros((size, 128), BF16)
            values[image, at:at + size, :] = jnp.zeros((size, 128), BF16)
        for row in range(ROWS):
            for at in (0, HALO + width):
                projected[image, row, at:at + HALO, :] = jnp.zeros((HALO, 128), F32)
    loads[0].wait()
    loads[1].wait()
    packed = jnp.concatenate(split2(weights[...]), axis=0)

    def project(value):
        hi, lo = split2(value)
        both = dot_nt(hi, packed) + dot_nt(lo, packed)
        return both[:, :128] + both[:, 128:]

    def project_own(image):
        both = project(own[image].reshape(ROWS * width, own.shape[3]))
        for row in range(ROWS):
            projected[image, row, HALO:HALO + width, :] = both[row * width:(row + 1) * width]

    ones = jnp.ones((reach, 128), BF16)

    def prepare(image, parts):
        for row in range(ROWS):
            for at, size in parts:
                value = projected[image, row, at:at + size, :]
                low = lower_half(value)
                hi, rest = rounded(value)
                turned_hi, turned_rest = pltpu.roll(hi, CH, 1), pltpu.roll(rest, CH, 1)
                queries[image, row, at:at + size, :] = jnp.concatenate(
                    [jnp.where(low, hi, turned_hi) * (1.0 / CH), jnp.where(low, rest, turned_rest) * (1.0 / CH)],
                    axis=1).astype(BF16)
                rows = slice((row + 1) * wide + at, (row + 1) * wide + at + size)
                keys[image, rows, :] = jnp.where(low, hi, turned_rest).astype(BF16)
                values[image, rows, :] = jnp.where(low, turned_hi, rest).astype(BF16)

    def attention(image, parts):
        def taken(array):
            pieces = [array[at:at + size] for at, size in parts]
            return pieces[0] if len(pieces) == 1 else jnp.concatenate(pieces, axis=0)

        result = []
        for row in range(ROWS):
            rows = slice(row * wide, row * wide + reach)
            seen = keys[image, rows, :]
            score = dot_nt(taken(queries.at[image, row]), jnp.concatenate([seen, seen], axis=1)) + taken(bias.at[row])
            weight = jnp.exp(score - jnp.max(score, axis=1, keepdims=True))
            hi, lo = split2(weight)
            mixed = jnp.concatenate([values[image, rows, :], ones], axis=1)
            total = dot(hi, mixed) + dot(lo, mixed)
            shared = total[:, :128] + pltpu.roll(total[:, :128], CH, 1)
            value = taken(projected.at[image, row])
            value = jnp.where(lower_half(value), pltpu.roll(value, CH, 1), value)
            result.append(value + shared / total[:, 128:])
        return result

    def paired(parts, place):
        return jnp.where(lower_half(parts[0]), parts[2 * place], parts[2 * place + 1])

    def keep_reference(parts, start):
        size = parts[0].shape[0]
        column = lax.broadcasted_iota(jnp.int32, (size, 128), 0) + (tile * width - HALO + start)
        inside = (column >= 0) & (column < count * width)
        for row in range(ROWS):
            scaled = jnp.where(inside, parts[row], 0.0) * (1.0 / (CH // GROUPS))
            for place, part in enumerate(rounded(scaled)):
                edge[row, place, start:start + size, :] = part

    inner = ((2 * HALO, width - 2 * HALO),)
    outer = ((0, 2 * HALO), (width, 2 * HALO))
    loads[2].wait()
    sends = []
    for pair in range(pairs):
        project_own(pair + 1)
        prepare(pair + 1, ((0, wide),))
        parts = attention(pair + 1, inner)
        for place in range(2):
            middle[0, pair, :, place * 128:(place + 1) * 128] = paired(parts, place)
        for step in (1, 3):
            copy = remote(middle.at[0, pair], middle.at[step, pair], 6 + 3 * pair + step - 1, -step)
            sends.append((step, copy))

            @pl.when(present(-step))
            def _(copy=copy):
                copy.start()

    loads[3].wait()
    project_own(0)
    prepare(0, ((0, wide),))
    keep_reference(attention(0, inner), 2 * HALO)
    loads[4].wait()
    loads[5].wait()
    loads[6].wait()
    band_weights(taps, spread, w_hi, w_lo)
    for step, copies in ((1, upward), (-1, downward)):
        @pl.when(present(-step))
        def _(copies=copies):
            for copy in copies:
                copy.wait_recv()

    entries = [
        pltpu.make_async_copy(source, shifts.at[place], local.at[6 + place])
        for place, source in ((1, before), (2, after))
    ]
    for entry in entries:
        entry.start()
    size = images * ROWS * HALO
    both = project(jnp.concatenate(
        [left[...].reshape(size, own.shape[3]), right[...].reshape(size, own.shape[3])], axis=0))
    for image in range(images):
        for row in range(ROWS):
            base = (image * ROWS + row) * HALO
            projected[image, row, 0:HALO, :] = both[base:base + HALO]
            projected[image, row, HALO + width:wide, :] = both[size + base:size + base + HALO]
    for pair in range(pairs):
        prepare(pair + 1, outer)
        parts = attention(pair + 1, outer)
        for place in range(2):
            feature = paired(parts, place)
            behind[pair, :, place * 128:(place + 1) * 128] = feature[:HALO]
            rim[0, pair, :, place * 128:(place + 1) * 128] = feature[HALO:3 * HALO]
    rims = []
    for step in (1, 2, 3):
        copy = remote(rim.at[0], rim.at[step], 6 + 3 * pairs + step - 1, -step)
        rims.append((step, copy))

        @pl.when(present(-step))
        def _(copy=copy):
            copy.start()

    odd = tile % 2 == 1
    forwards = []
    for step, copy in sends:
        @pl.when(present(step))
        def _(copy=copy):
            copy.wait_recv()

        pair = len(forwards) // 2
        offset, chosen = (-1, odd) if step == 1 else (1, jnp.logical_not(odd))
        forward = remote(middle.at[step, pair], middle.at[2, pair], 7 + 3 * pair, offset)
        going = chosen & present(step)
        forwards.append((going, forward))

        @pl.when(going)
        def _(forward=forward):
            forward.start()

    prepare(0, outer)
    parts = attention(0, outer)
    keep_reference([part[:2 * HALO] for part in parts], 0)
    keep_reference([part[2 * HALO:] for part in parts], width)
    own_group = (lane % CH) // (CH // GROUPS) == lax.broadcasted_iota(jnp.int32, (8, 128), 0)
    pad = HALO - 2
    for row in range(ROWS):
        for place in range(2):
            for col in range(0, width + 4, 2):
                pair_rows = [
                    jnp.where(own_group, jnp.broadcast_to(edge[row, place, pad + at:pad + at + 1, :], (8, 128)), 0.0)
                    for at in (col, col + 1)
                ]
                main[row, col * 8:col * 8 + 16, place * 128:(place + 1) * 128] = (
                    jnp.concatenate(pair_rows, axis=0).astype(BF16))
    for entry in entries:
        entry.wait()

    def joined(hi, lo, row):
        low = lower_half(hi)
        if row % 2 == 0:
            return jnp.where(low, hi, pltpu.roll(lo, CH, 1))
        return jnp.where(low, pltpu.roll(hi, CH, 1), lo)

    for step, copy in rims:
        @pl.when(present(step))
        def _(copy=copy):
            copy.wait_recv()

    for pair in range(pairs):
        @pl.when(present(2))
        def _(forward=forwards[2 * pair][1]):
            forward.wait_recv()

        for side in range(2):
            lanes = slice(side * 128, (side + 1) * 128)
            seen = [
                rounded(jnp.concatenate(
                    [rim[step, pair, :HALO, lanes], middle[step, pair, :, lanes], rim[step, pair, HALO:, lanes]], axis=0))
                for step in range(4)
            ]
            near = rounded(behind[pair, :, lanes])
            products = []
            for row in (2 * side, 2 * side + 1):
                parts = [joined(hi, lo, row).astype(BF16) for hi, lo in seen]
                whole = jnp.concatenate(parts, axis=0)
                turn = jnp.concatenate(
                    [jnp.zeros((width - HALO, 128), F32), joined(*near, row)], axis=0).astype(BF16)
                wrap = jnp.concatenate([parts[2], turn], axis=0)
                products.append((
                    dot_nt(main[row], jnp.concatenate([whole, whole], axis=1)),
                    dot_nt(main[row, 0:16, :], jnp.concatenate([wrap, wrap], axis=1))))
            for col in range(width + 4):
                x = col - 2
                begin = shifts[1 if x < 0 else 2 if x >= width else 0, 0, pair] + x
                turn = lax.rem(256 - begin, 128)
                here = (lane + begin >= 0) & (lane + begin < 128)
                pieces = []
                for whole, ends in products:
                    rows = slice(col * 8, (col + 1) * 8)
                    a = whole[rows, 0:128]
                    b = ends[rows] if x < 0 else whole[rows, 128:256]
                    pieces.append(jnp.where(here, pltpu.roll(a, turn, 1), pltpu.roll(b, turn, 1)))
                hi, lo = split2(jnp.concatenate(pieces, axis=0))
                rows = slice(col * group + side * 16, col * group + side * 16 + 16)
                volume_hi[rows, pair * 128:(pair + 1) * 128] = hi
                volume_lo[rows, pair * 128:(pair + 1) * 128] = lo

    def convolved(conv, hi_ref, lo_ref, start, cols):
        rows = slice(start * group, (start + cols + 2) * group)
        hi, lo = hi_ref[rows, :], lo_ref[rows, :]
        if cols == COLS:
            wh, wl = w_hi[conv], w_lo[conv]
        else:
            picked = [
                jnp.concatenate([w[conv, tap * span:tap * span + cols * group, 0:(cols + 2) * group]
                                 for tap in range(3)], axis=0)
                for w in (w_hi, w_lo)
            ]
            wh, wl = picked
        both = dot(wh, hi) + dot(wl, hi) + dot(wh, lo)
        size = cols * group
        level = lax.broadcasted_iota(jnp.int32, (size, 128), 1)
        result = []
        for pair in range(pairs):
            lanes = slice(pair * 128, (pair + 1) * 128)
            before = jnp.where(level >= 1, pltpu.roll(both[0:size, lanes], 1, 1), 0.0)
            after = jnp.where(level < DISP - 1, pltpu.roll(both[2 * size:, lanes], 127, 1), 0.0)
            result.append(jnp.maximum(both[size:2 * size, lanes] + before + after, 0.0))
        return result

    for start in range(0, width + 2, COLS):
        cols = min(COLS, width + 2 - start)
        results = convolved(0, volume_hi, volume_lo, start, cols)
        at = lax.broadcasted_iota(jnp.int32, (cols * group, 128), 0)
        for pair in range(pairs):
            value = results[pair]
            if start == 0:
                value = jnp.where((at < group) & (tile == 0), 0.0, value)
            if start + cols == width + 2:
                value = jnp.where((at >= (cols - 1) * group) & (tile == count - 1), 0.0, value)
            hi, lo = split2(value)
            rows = slice(start * group, (start + cols) * group)
            first_hi[rows, pair * 128:(pair + 1) * 128] = hi
            first_lo[rows, pair * 128:(pair + 1) * 128] = lo
    for start in range(0, width, COLS):
        cols = min(COLS, width - start)
        total = reduce(jnp.add, convolved(1, first_hi, first_lo, start, cols))
        score = jnp.sum(total.reshape(cols * ROWS, GROUPS, 128), axis=1)
        sums[start * ROWS:(start + cols) * ROWS, :] = score
    score = sums[...]
    weight = jnp.exp(score - jnp.max(score, axis=1, keepdims=True))
    level = lax.broadcasted_iota(jnp.int32, score.shape, 1).astype(F32)
    mean = jnp.sum(weight * level, axis=1, keepdims=True) / (jnp.sum(weight, axis=1, keepdims=True) * DISP)
    pixel = lax.broadcasted_iota(jnp.int32, score.shape, 0)
    placed = jnp.where(pixel // ROWS == lax.broadcasted_iota(jnp.int32, score.shape, 1), mean, 0.0)
    pick = jnp.where(
        lax.broadcasted_iota(jnp.int32, (16, width * ROWS), 1) % ROWS
        == lax.broadcasted_iota(jnp.int32, (16, width * ROWS), 0), 1.0, 0.0).astype(BF16)
    final = reduce(jnp.add, [dot(pick, part) for part in split3(placed)])
    out[...] = final[:ROWS, :width]
    for step, copies in ((1, upward), (-1, downward)):
        @pl.when(present(step))
        def _(copies=copies):
            for copy in copies:
                copy.wait_send()

    for step, copy in (*sends, *rims):
        @pl.when(present(-step))
        def _(copy=copy):
            copy.wait_send()

    for going, forward in forwards:
        @pl.when(going)
        def _(forward=forward):
            forward.wait_send()


def on_device(reference_feat, secondary_feat, pair_offsets, w_query_key, w_value, conv_first, conv_second):
    pairs = secondary_feat.shape[0]
    images = pairs + 1
    width, features = reference_feat.shape[1:]
    wide = width + 2 * HALO
    group = ROWS * GROUPS
    lanes = pairs * DISP
    held = (ROWS + 2) * wide + 256 - 3 * wide
    copies = 9 + 3 * pairs
    banded = pltpu.VMEM((2, 3 * COLS * group, (COLS + 2) * group), BF16)
    first, second = (jnp.transpose(conv, (2, 3, 4, 0, 1)) for conv in (conv_first, conv_second))
    return pl.pallas_call(
        functools.partial(stereo_kernel, images, width, lax.axis_size("tile")),
        out_shape=jax.ShapeDtypeStruct((ROWS, width), F32),
        in_specs=[pl.BlockSpec(memory_space=pltpu.HBM)] * 7,
        out_specs=pl.BlockSpec(memory_space=pltpu.VMEM),
        scratch_shapes=[
            pltpu.VMEM((images, ROWS, HALO, features), F32),
            pltpu.VMEM((images, ROWS, HALO, features), F32),
            pltpu.VMEM((images, ROWS, width, features), F32),
            pltpu.VMEM((2 * CH, features), F32),
            pltpu.VMEM((2, 3, 3, 3, GROUPS, GROUPS), F32),
            pltpu.VMEM((6 * ROWS, GROUPS, 128), F32),
            pltpu.VMEM((images, ROWS, wide, 2 * CH), F32),
            pltpu.VMEM((ROWS, wide, 256), F32),
            pltpu.VMEM((images, ROWS, wide, 256), BF16),
            pltpu.VMEM((images, held, 128), BF16),
            pltpu.VMEM((images, held, 128), BF16),
            pltpu.VMEM((ROWS, 2, wide, 128), F32),
            pltpu.VMEM((ROWS, (width + 4) * GROUPS, 256), BF16),
            banded, banded,
            pltpu.VMEM((4, pairs, width - 2 * HALO, LANES), F32),
            pltpu.VMEM((4, pairs, 2 * HALO, LANES), F32),
            pltpu.VMEM((pairs, HALO, LANES), F32),
            pltpu.VMEM((1, pairs), jnp.int32),
            pltpu.VMEM((1, pairs), jnp.int32),
            pltpu.SMEM((3, 1, pairs), jnp.int32),
            pltpu.VMEM(((width + 4) * group, lanes), BF16),
            pltpu.VMEM(((width + 4) * group, lanes), BF16),
            pltpu.VMEM(((width + 2) * group, lanes), BF16),
            pltpu.VMEM(((width + 2) * group, lanes), BF16),
            pltpu.VMEM((width * ROWS, 128), F32),
            pltpu.SemaphoreType.DMA((9,)),
            pltpu.SemaphoreType.DMA((copies,)),
            pltpu.SemaphoreType.DMA((copies,)),
        ],
        compiler_params=pltpu.CompilerParams(
            vmem_limit_bytes=60 << 20, collective_id=0, has_side_effects=True),
    )(pair_offsets.T, reference_feat, secondary_feat, w_query_key.T, w_value.T, first, second)


def solution(mesh):
    return jax.shard_map(
        on_device,
        mesh=mesh,
        in_specs=(
            P("groups", "tile", None),
            P("groups", None, "tile", None),
            P("groups", "tile"),
            P(),
            P(),
            P(),
            P(),
        ),
        out_specs=P("groups", "tile"),
        check_vma=False,
    )
```

```python
import functools
from functools import reduce

import jax
import jax.numpy as jnp
from jax import lax
from jax.experimental import pallas as pl
from jax.experimental.pallas import tpu as pltpu
from jax.sharding import PartitionSpec as P

GROUPS = 8
DISP = 128
RAD = 3
ROWS = 4
CH = 64
LANES = ROWS * CH
HALO = 8
F32 = jnp.float32
BF16 = jnp.bfloat16


def dot(a, b):
    return jnp.dot(a, b, preferred_element_type=F32)


def split2(x):
    hi = x.astype(BF16)
    return hi, (x - hi.astype(F32)).astype(BF16)


def split3(x):
    hi = x.astype(BF16)
    rest = x - hi.astype(F32)
    mid = rest.astype(BF16)
    return hi, mid, (rest - mid.astype(F32)).astype(BF16)


def dot_nt(a, b):
    return lax.dot_general(a, b, (((1,), (1,)), ((), ())), preferred_element_type=F32)


def rounded(value):
    hi = value.astype(BF16).astype(F32)
    return hi, value - hi


def lower_half(value):
    return lax.broadcasted_iota(jnp.int32, value.shape, 1) < CH


def band_weights(taps, spread, w_hi, w_lo):
    group = ROWS * GROUPS
    empty = jnp.zeros((GROUPS, GROUPS), F32)
    for conv in range(2):
        for col in range(3):
            for phase in range(2):
                for row in range(ROWS):
                    pieces = []
                    for level in range(4):
                        for source in range(ROWS):
                            step, depth = source - row + 1, level - phase
                            used = 0 <= step < 3 and 0 <= depth < 3
                            pieces.append(taps[conv, step, col, depth] if used else empty)
                    spread[(conv * 3 + col) * 2 + phase, row * GROUPS:(row + 1) * GROUPS, :] = (
                        jnp.concatenate(pieces, axis=1))
    blank = jnp.zeros((2 * group, 128), BF16)
    layout = (((2, None), (1, 2)), ((0, 1), (None, 0)))
    for conv in range(2):
        for part in range(2):
            for col in range(2):
                rows = slice((2 * part + col) * 2 * group, (2 * part + col + 1) * 2 * group)
                for place in range(2):
                    tap = layout[part][col][place]
                    lanes = slice(place * 128, (place + 1) * 128)
                    hi, lo = blank, blank
                    if tap is not None:
                        hi, lo = split2(jnp.concatenate(
                            [spread[(conv * 3 + tap) * 2 + phase] for phase in range(2)], axis=0))
                    w_hi[conv, rows, lanes] = hi
                    w_lo[conv, rows, lanes] = lo


def stereo_kernel(images, width, count, offsets, ref, sec, wq, wv, first, second, out,
                  left, right, own, weights, taps, spread, projected, bias, queries, keys, values, edge, main,
                  w_hi, w_lo, middle, rim, behind, window, wrap, before, after, shifts,
                  volume_hi, volume_lo, first_hi, first_lo, sums, local, send, recv):
    pairs = images - 1
    wide = width + 2 * HALO
    reach = 256
    group = ROWS * GROUPS
    half = width // 2
    column_rows = 4 * group
    tile = lax.axis_index("tile")
    lane = lax.broadcasted_iota(jnp.int32, (8, 128), 1)

    def present(step):
        return (tile + step >= 0) & (tile + step < count)

    def remote(source, target, place, step):
        return pltpu.make_async_remote_copy(
            src_ref=source, dst_ref=target, send_sem=send.at[place], recv_sem=recv.at[place],
            device_id={"tile": tile + step}, device_id_type=pl.DeviceIdType.MESH)

    barrier = pltpu.get_barrier_semaphore()
    partners = 0
    for step in (1, -1, 2, -2, 3, -3):
        @pl.when(present(step))
        def _(step=step):
            pl.semaphore_signal(barrier, inc=1, device_id={"tile": tile + step}, device_id_type=pl.DeviceIdType.MESH)

        partners = partners + jnp.where(present(step), 1, 0)
    loads = [
        pltpu.make_async_copy(source, target, local.at[place])
        for place, (source, target) in enumerate((
            (wq, weights.at[pl.ds(0, CH)]),
            (wv, weights.at[pl.ds(CH, CH)]),
            (sec, own.at[pl.ds(1, pairs)]),
            (ref, own.at[0]),
            (first, taps.at[0]),
            (second, taps.at[1]),
            (offsets, shifts.at[0]),
        ))
    ]
    for load in loads:
        load.start()
    pl.semaphore_wait(barrier, partners)

    tail = pl.ds(width - HALO, HALO)
    head = pl.ds(0, HALO)
    upward = [
        remote(sec.at[:, :, tail, :], left.at[pl.ds(1, pairs)], 0, 1),
        remote(ref.at[:, tail, :], left.at[0], 1, 1),
        remote(offsets, before, 2, 1),
    ]
    downward = [
        remote(sec.at[:, :, head, :], right.at[pl.ds(1, pairs)], 3, -1),
        remote(ref.at[:, head, :], right.at[0], 4, -1),
        remote(offsets, after, 5, -1),
    ]
    for step, copies in ((1, upward), (-1, downward)):
        @pl.when(present(step))
        def _(copies=copies):
            for copy in copies:
                copy.start()
    for step, halo, entry in ((-1, left, before), (1, right, after)):
        @pl.when(jnp.logical_not(present(step)))
        def _(halo=halo, entry=entry):
            halo[...] = jnp.zeros_like(halo)
            entry[...] = jnp.zeros_like(entry)
    for step in (1, 2, 3):
        @pl.when(jnp.logical_not(present(step)))
        def _(step=step):
            middle[step] = jnp.zeros(middle.shape[1:], F32)
            rim[step] = jnp.zeros(rim.shape[1:], F32)

    spot = lax.broadcasted_iota(jnp.int32, (wide, reach), 1)
    query = lax.broadcasted_iota(jnp.int32, (wide, reach), 0)
    key = spot - jnp.where(spot >= 2 * wide, 2 * wide, jnp.where(spot >= wide, wide, 0))
    column = key + (tile * width - HALO)
    near = (key - query <= RAD) & (query - key <= RAD) & (column >= 0) & (column < count * width) & (spot < 3 * wide)
    for row in range(ROWS):
        allowed = near
        if row == 0:
            allowed = allowed & (spot >= wide)
        if row == ROWS - 1:
            allowed = allowed & (spot < 2 * wide)
        bias[row] = jnp.where(allowed, 0.0, -1e30)
    for image in range(images):
        for at, size in ((0, wide), ((ROWS + 1) * wide, reach - 2 * wide)):
            keys[image, at:at + size, :] = jnp.zeros((size, 128), BF16)
            values[image, at:at + size, :] = jnp.zeros((size, 128), BF16)
        for row in range(ROWS):
            for at in (0, HALO + width):
                projected[image, row, at:at + HALO, :] = jnp.zeros((HALO, 128), F32)
    loads[0].wait()
    loads[1].wait()
    packed = jnp.concatenate(split2(weights[...]), axis=0)

    def project(value):
        hi, lo = split2(value)
        both = dot_nt(hi, packed) + dot_nt(lo, packed)
        return both[:, :128] + both[:, 128:]

    def project_own(image):
        both = project(own[image].reshape(ROWS * width, own.shape[3]))
        for row in range(ROWS):
            projected[image, row, HALO:HALO + width, :] = both[row * width:(row + 1) * width]

    ones = jnp.ones((reach, 128), BF16)

    def prepare(parts):
        for image in range(images):
            for row in range(ROWS):
                for at, size in parts:
                    value = projected[image, row, at:at + size, :]
                    low = lower_half(value)
                    hi, rest = rounded(value)
                    turned_hi, turned_rest = pltpu.roll(hi, CH, 1), pltpu.roll(rest, CH, 1)
                    queries[image, row, at:at + size, :] = jnp.concatenate(
                        [jnp.where(low, hi, turned_hi) * (1.0 / CH), jnp.where(low, rest, turned_rest) * (1.0 / CH)],
                        axis=1).astype(BF16)
                    rows = slice((row + 1) * wide + at, (row + 1) * wide + at + size)
                    keys[image, rows, :] = jnp.where(low, hi, turned_rest).astype(BF16)
                    values[image, rows, :] = jnp.where(low, turned_hi, rest).astype(BF16)

    def attention(parts):
        def taken(array):
            pieces = [array[at:at + size] for at, size in parts]
            return pieces[0] if len(pieces) == 1 else jnp.concatenate(pieces, axis=0)

        places = [(image, row) for image in (*range(1, images), 0) for row in range(ROWS)]
        scores = []
        for image, row in places:
            seen = keys[image, row * wide:row * wide + reach, :]
            scores.append(
                dot_nt(taken(queries.at[image, row]), jnp.concatenate([seen, seen], axis=1)) + taken(bias.at[row]))
        raised = [split2(jnp.exp(score - jnp.max(score, axis=1, keepdims=True))) for score in scores]
        result = [[None] * ROWS for _ in range(images)]
        for (image, row), (hi, lo) in zip(places, raised):
            mixed = jnp.concatenate([values[image, row * wide:row * wide + reach, :], ones], axis=1)
            total = dot(hi, mixed) + dot(lo, mixed)
            shared = total[:, :128] + pltpu.roll(total[:, :128], CH, 1)
            value = taken(projected.at[image, row])
            value = jnp.where(lower_half(value), pltpu.roll(value, CH, 1), value)
            result[image][row] = value + shared / total[:, 128:]
        return result

    def paired(parts, place):
        return jnp.where(lower_half(parts[0]), parts[2 * place], parts[2 * place + 1])

    def keep_reference(parts, start):
        size = parts[0].shape[0]
        column = lax.broadcasted_iota(jnp.int32, (size, 128), 0) + (tile * width - HALO + start)
        inside = (column >= 0) & (column < count * width)
        for row in range(ROWS):
            scaled = jnp.where(inside, parts[row], 0.0) * (1.0 / (CH // GROUPS))
            for place, part in enumerate(rounded(scaled)):
                edge[row, place, start:start + size, :] = part

    inner = ((2 * HALO, width - 2 * HALO),)
    outer = ((0, 2 * HALO), (width, 2 * HALO))
    loads[2].wait()
    loads[3].wait()
    sends = []
    for image in range(images):
        project_own(image)
    prepare(((0, wide),))
    features = attention(inner)
    for pair in range(pairs):
        for place in range(2):
            middle[0, pair, place] = paired(features[pair + 1], place)
        for step in (1, 3):
            copy = remote(middle.at[0, pair], middle.at[step, pair], 6 + 3 * pair + step - 1, -step)
            sends.append((step, copy))

            @pl.when(present(-step))
            def _(copy=copy):
                copy.start()

    keep_reference(features[0], 2 * HALO)
    loads[4].wait()
    loads[5].wait()
    loads[6].wait()
    band_weights(taps, spread, w_hi, w_lo)
    for step, copies in ((1, upward), (-1, downward)):
        @pl.when(present(-step))
        def _(copies=copies):
            for copy in copies:
                copy.wait_recv()

    entries = [
        pltpu.make_async_copy(source, shifts.at[place], local.at[6 + place])
        for place, source in ((1, before), (2, after))
    ]
    for entry in entries:
        entry.start()
    size = images * ROWS * HALO
    both = project(jnp.concatenate(
        [left[...].reshape(size, own.shape[3]), right[...].reshape(size, own.shape[3])], axis=0))
    for image in range(images):
        for row in range(ROWS):
            base = (image * ROWS + row) * HALO
            projected[image, row, 0:HALO, :] = both[base:base + HALO]
            projected[image, row, HALO + width:wide, :] = both[size + base:size + base + HALO]
    prepare(outer)
    features = attention(outer)
    for pair in range(pairs):
        for place in range(2):
            feature = paired(features[pair + 1], place)
            behind[pair, place] = feature[:HALO]
            rim[0, pair, place] = feature[HALO:3 * HALO]
    rims = []
    for step in (1, 2, 3):
        copy = remote(rim.at[0], rim.at[step], 6 + 3 * pairs + step - 1, -step)
        rims.append((step, copy))

        @pl.when(present(-step))
        def _(copy=copy):
            copy.start()

    odd = tile % 2 == 1
    forwards = []
    for step, copy in sends:
        @pl.when(present(step))
        def _(copy=copy):
            copy.wait_recv()

        pair = len(forwards) // 2
        offset, chosen = (-1, odd) if step == 1 else (1, jnp.logical_not(odd))
        forward = remote(middle.at[step, pair], middle.at[2, pair], 7 + 3 * pair, offset)
        going = chosen & present(step)
        forwards.append((going, forward))

        @pl.when(going)
        def _(forward=forward):
            forward.start()

    keep_reference([part[:2 * HALO] for part in features[0]], 0)
    keep_reference([part[2 * HALO:] for part in features[0]], width)
    own_group = (lane % CH) // (CH // GROUPS) == lax.broadcasted_iota(jnp.int32, (8, 128), 0)
    pad = HALO - 2
    for row in range(ROWS):
        for place in range(2):
            for col in range(0, width + 4, 2):
                pair_rows = [
                    jnp.where(own_group, jnp.broadcast_to(edge[row, place, pad + at:pad + at + 1, :], (8, 128)), 0.0)
                    for at in (col, col + 1)
                ]
                main[row, col * 8:col * 8 + 16, place * 128:(place + 1) * 128] = (
                    jnp.concatenate(pair_rows, axis=0).astype(BF16))
    for entry in entries:
        entry.wait()

    def joined(hi, lo, row):
        low = lower_half(hi)
        if row % 2 == 0:
            return jnp.where(low, hi, pltpu.roll(lo, CH, 1))
        return jnp.where(low, pltpu.roll(hi, CH, 1), lo)

    for step, copy in rims:
        @pl.when(present(step))
        def _(copy=copy):
            copy.wait_recv()

    for pair in range(pairs):
        @pl.when(present(2))
        def _(forward=forwards[2 * pair][1]):
            forward.wait_recv()

    for pair in range(pairs):
        for side in range(2):
            for step in range(4):
                start = step * width
                window[pair, side, start:start + HALO, :] = rim[step, pair, side, :HALO, :]
                window[pair, side, start + HALO:start + width - HALO, :] = middle[step, pair, side]
                window[pair, side, start + width - HALO:start + width, :] = rim[step, pair, side, HALO:, :]
            wrap[pair, side, :width - HALO, :] = jnp.zeros((width - HALO, 128), F32)
            wrap[pair, side, width - HALO:, :] = behind[pair, side]
    odds = [lax.rem(shifts[0, 0, pair], 2) for pair in range(pairs)]
    floors = [lax.div(shifts[0, 0, pair] - odds[pair], 2) for pair in range(pairs)]
    ceilings = [floors[pair] + odds[pair] for pair in range(pairs)]
    first_half = lower_half(lane)

    def turned(value, begin, pair):
        return pltpu.roll(value, (256 + CH * pair - begin) & 127, 1)

    def halves(value, flag):
        return jnp.where(flag, value[1], value[0]), jnp.where(flag, value[0], value[1])

    def levels(even, odd):
        size = even.shape[0]
        at = lax.broadcasted_iota(jnp.int32, (size, 128), 1) % CH
        return (
            jnp.where(at >= 1, pltpu.roll(odd, 1, 1), 0.0), even, odd,
            jnp.where(at < CH - 1, pltpu.roll(even, 127, 1), 0.0))

    for side in range(2):
        products = []
        for row in (2 * side, 2 * side + 1):
            for pair in range(pairs):
                flag = odds[pair] == 1
                strided = [window[pair, side, pl.ds(at, 2 * width, stride=2), :] for at in range(2)]
                strided_wrap = [
                    jnp.concatenate([strided[at][:3 * half], wrap[pair, side, pl.ds(at, half, stride=2), :]], axis=0)
                    for at in range(2)
                ]
                whole, ends = [
                    jnp.concatenate([joined(*rounded(part), row) for part in halves(value, flag)], axis=0).astype(BF16)
                    for value in (strided, strided_wrap)
                ]
                products.append((
                    dot_nt(main[row], jnp.concatenate([whole, whole], axis=1)),
                    dot_nt(main[row, 0:16, :], jnp.concatenate([ends, ends], axis=1))))
        for col in range(width + 4):
            x = col - 2
            evens, odds_of = [], []
            for place in range(2):
                made = []
                for pair in range(pairs):
                    whole, ends = products[place * pairs + pair]
                    source = (ends if x < 0 else whole)[col * 8:(col + 1) * 8]
                    same, other = source[:, :128], source[:, 128:]
                    if 0 <= x < width:
                        low, high = floors[pair] + (x + x % 2) // 2, ceilings[pair] + x // 2
                        if x % 2:
                            made.append((turned(other, high, pair), turned(same, low, pair)))
                        else:
                            made.append((turned(same, low, pair), turned(other, high, pair)))
                    else:
                        q = odds[pair]
                        begin = shifts[1 if x < 0 else 2, 0, pair] + x + 256
                        match = lax.rem(begin, 2) == q
                        made.append((
                            turned(jnp.where(match, same, other),
                                   lax.div(jnp.where(match, begin - q, begin - 1 + q), 2) - 128, pair),
                            turned(jnp.where(match, other, same),
                                   lax.div(jnp.where(match, begin + q, begin + 1 - q), 2) - 128, pair)))
                evens.append(jnp.where(first_half, made[0][0], made[1][0]))
                odds_of.append(jnp.where(first_half, made[0][1], made[1][1]))
            for at, value in enumerate(levels(jnp.concatenate(evens, axis=0), jnp.concatenate(odds_of, axis=0))):
                hi, lo = split2(value)
                for part, base in ((0, -2), (1, half - 2)):
                    if 0 <= x - base < half + 4:
                        start = (x - base) * column_rows + at * group + side * 16
                        volume_hi[start:start + 16, part * 128:(part + 1) * 128] = hi
                        volume_lo[start:start + 16, part * 128:(part + 1) * 128] = lo

    def convolved(conv, hi_ref, lo_ref, tiles, finish):
        carry = None
        out_rows = column_rows
        for at in range(tiles):
            rows = slice(at * 2 * column_rows, (at + 1) * 2 * column_rows)
            hi, lo = hi_ref[rows, :], lo_ref[rows, :]
            used = slice(out_rows if at == 0 else 0, out_rows if at == tiles - 1 else 2 * out_rows)
            wh, wl = w_hi[conv, used, :], w_lo[conv, used, :]
            both = dot(wh, hi) + dot(wl, hi) + dot(wh, lo)
            if at:
                finish(at - 1, jnp.maximum(carry + both[:out_rows], 0.0))
            carry = both if at == 0 else both[out_rows:]

    def finish_first(at, value):
        for part in range(2):
            lanes = slice(part * 128, (part + 1) * 128)
            for col in range(2):
                rows = value[col * 2 * group:(col + 1) * 2 * group, lanes]
                if part == 0 and at == 0 and col == 0:
                    rows = jnp.where(tile == 0, 0.0, rows)
                if part == 1 and at == half // 2 and col == 1:
                    rows = jnp.where(tile == count - 1, 0.0, rows)
                start = (2 * at + col) * column_rows
                for place, piece in enumerate(levels(rows[:group], rows[group:])):
                    hi, lo = split2(piece)
                    first_hi[start + place * group:start + (place + 1) * group, lanes] = hi
                    first_lo[start + place * group:start + (place + 1) * group, lanes] = lo

    def finish_second(at, value):
        for part in range(2):
            pieces = []
            for col in range(2):
                rows = value[col * 2 * group:(col + 1) * 2 * group, part * 128:(part + 1) * 128]
                total = rows + pltpu.roll(rows, CH, 1)
                pieces.append(jnp.where(lower_half(total[:group]), total[:group], total[group:]))
            score = jnp.sum(jnp.concatenate(pieces, axis=0).reshape(2 * ROWS, GROUPS, 128), axis=1)
            start = (part * half + 2 * at) * ROWS
            sums[start:start + 2 * ROWS, :] = score

    convolved(0, volume_hi, volume_lo, half // 2 + 2, finish_first)
    convolved(1, first_hi, first_lo, half // 2 + 1, finish_second)
    score = sums[...]
    weight = jnp.exp(score - jnp.max(score, axis=1, keepdims=True))
    spot = lax.broadcasted_iota(jnp.int32, score.shape, 1)
    level = jnp.where(spot < CH, 2 * spot, 2 * spot - (2 * CH - 1)).astype(F32)
    mean = jnp.sum(weight * level, axis=1, keepdims=True) / (jnp.sum(weight, axis=1, keepdims=True) * DISP)
    pixel = lax.broadcasted_iota(jnp.int32, score.shape, 0)
    placed = jnp.where(pixel // ROWS == spot, mean, 0.0)
    pick = jnp.where(
        lax.broadcasted_iota(jnp.int32, (16, width * ROWS), 1) % ROWS
        == lax.broadcasted_iota(jnp.int32, (16, width * ROWS), 0), 1.0, 0.0).astype(BF16)
    final = reduce(jnp.add, [dot(pick, part) for part in split3(placed)])
    out[...] = final[:ROWS, :width]
    for step, copies in ((1, upward), (-1, downward)):
        @pl.when(present(step))
        def _(copies=copies):
            for copy in copies:
                copy.wait_send()

    for step, copy in (*sends, *rims):
        @pl.when(present(-step))
        def _(copy=copy):
            copy.wait_send()

    for going, forward in forwards:
        @pl.when(going)
        def _(forward=forward):
            forward.wait_send()


def on_device(reference_feat, secondary_feat, pair_offsets, w_query_key, w_value, conv_first, conv_second):
    pairs = secondary_feat.shape[0]
    images = pairs + 1
    width, features = reference_feat.shape[1:]
    wide = width + 2 * HALO
    group = ROWS * GROUPS
    held = (ROWS + 2) * wide + 256 - 3 * wide
    copies = 9 + 3 * pairs
    banded = pltpu.VMEM((2, 8 * group, 8 * group), BF16)
    costs = pltpu.VMEM(((width // 2 + 4) * 4 * group, 256), BF16)
    firsts = pltpu.VMEM(((width // 2 + 2) * 4 * group, 256), BF16)
    first, second = (jnp.transpose(conv, (2, 3, 4, 0, 1)) for conv in (conv_first, conv_second))
    return pl.pallas_call(
        functools.partial(stereo_kernel, images, width, lax.axis_size("tile")),
        out_shape=jax.ShapeDtypeStruct((ROWS, width), F32),
        in_specs=[pl.BlockSpec(memory_space=pltpu.HBM)] * 7,
        out_specs=pl.BlockSpec(memory_space=pltpu.VMEM),
        scratch_shapes=[
            pltpu.VMEM((images, ROWS, HALO, features), F32),
            pltpu.VMEM((images, ROWS, HALO, features), F32),
            pltpu.VMEM((images, ROWS, width, features), F32),
            pltpu.VMEM((2 * CH, features), F32),
            pltpu.VMEM((2, 3, 3, 3, GROUPS, GROUPS), F32),
            pltpu.VMEM((12, group, 128), F32),
            pltpu.VMEM((images, ROWS, wide, 2 * CH), F32),
            pltpu.VMEM((ROWS, wide, 256), F32),
            pltpu.VMEM((images, ROWS, wide, 256), BF16),
            pltpu.VMEM((images, held, 128), BF16),
            pltpu.VMEM((images, held, 128), BF16),
            pltpu.VMEM((ROWS, 2, wide, 128), F32),
            pltpu.VMEM((ROWS, (width + 4) * GROUPS, 256), BF16),
            banded, banded,
            pltpu.VMEM((4, pairs, 2, width - 2 * HALO, 128), F32),
            pltpu.VMEM((4, pairs, 2, 2 * HALO, 128), F32),
            pltpu.VMEM((pairs, 2, HALO, 128), F32),
            pltpu.VMEM((pairs, 2, 4 * width, 128), F32),
            pltpu.VMEM((pairs, 2, width, 128), F32),
            pltpu.VMEM((1, pairs), jnp.int32),
            pltpu.VMEM((1, pairs), jnp.int32),
            pltpu.SMEM((3, 1, pairs), jnp.int32),
            costs, costs, firsts, firsts,
            pltpu.VMEM((width * ROWS, 128), F32),
            pltpu.SemaphoreType.DMA((9,)),
            pltpu.SemaphoreType.DMA((copies,)),
            pltpu.SemaphoreType.DMA((copies,)),
        ],
        compiler_params=pltpu.CompilerParams(
            vmem_limit_bytes=60 << 20, collective_id=0, has_side_effects=True),
    )(pair_offsets.T, reference_feat, secondary_feat, w_query_key.T, w_value.T, first, second)


def solution(mesh):
    return jax.shard_map(
        on_device,
        mesh=mesh,
        in_specs=(
            P("groups", "tile", None),
            P("groups", None, "tile", None),
            P("groups", "tile"),
            P(),
            P(),
            P(),
            P(),
        ),
        out_specs=P("groups", "tile"),
        check_vma=False,
    )
```

```python
import functools
from functools import reduce

import jax
import jax.numpy as jnp
from jax import lax
from jax.experimental import pallas as pl
from jax.experimental.pallas import tpu as pltpu
from jax.sharding import PartitionSpec as P

GROUPS = 8
DISP = 128
RAD = 3
ROWS = 4
CH = 64
LANES = ROWS * CH
HALO = 8
F32 = jnp.float32
BF16 = jnp.bfloat16


def dot(a, b):
    return jnp.dot(a, b, preferred_element_type=F32)


def split2(x):
    hi = x.astype(BF16)
    return hi, (x - hi.astype(F32)).astype(BF16)


def split3(x):
    hi = x.astype(BF16)
    rest = x - hi.astype(F32)
    mid = rest.astype(BF16)
    return hi, mid, (rest - mid.astype(F32)).astype(BF16)


def dot_nt(a, b):
    return lax.dot_general(a, b, (((1,), (1,)), ((), ())), preferred_element_type=F32)


def rounded(value):
    hi = value.astype(BF16).astype(F32)
    return hi, value - hi


def lower_half(value):
    return lax.broadcasted_iota(jnp.int32, value.shape, 1) < CH


def band_weights(taps, spread, w_hi, w_lo):
    group = ROWS * GROUPS
    empty = jnp.zeros((GROUPS, GROUPS), F32)
    for conv in range(2):
        for col in range(3):
            for phase in range(2):
                for row in range(ROWS):
                    pieces = []
                    for level in range(4):
                        for source in range(ROWS):
                            step, depth = source - row + 1, level - phase
                            used = 0 <= step < 3 and 0 <= depth < 3
                            pieces.append(taps[conv, step, col, depth] if used else empty)
                    spread[(conv * 3 + col) * 2 + phase, row * GROUPS:(row + 1) * GROUPS, :] = (
                        jnp.concatenate(pieces, axis=1))
    blank = jnp.zeros((2 * group, 128), BF16)
    layout = (((2, None), (1, 2)), ((0, 1), (None, 0)))
    for conv in range(2):
        for part in range(2):
            for col in range(2):
                rows = slice((2 * part + col) * 2 * group, (2 * part + col + 1) * 2 * group)
                for place in range(2):
                    tap = layout[part][col][place]
                    lanes = slice(place * 128, (place + 1) * 128)
                    hi, lo = blank, blank
                    if tap is not None:
                        hi, lo = split2(jnp.concatenate(
                            [spread[(conv * 3 + tap) * 2 + phase] for phase in range(2)], axis=0))
                    w_hi[conv, rows, lanes] = hi
                    w_lo[conv, rows, lanes] = lo


def stereo_kernel(images, width, count, offsets, ref, sec, wq, wv, first, second, out,
                  left, right, own, weights, taps, spread, projected, bias, queries, keys, values, edge, main,
                  w_hi, w_lo, middle, rim, behind, window, wrap, before, after, shifts,
                  volume_hi, volume_lo, first_hi, first_lo, sums, local, send, recv):
    pairs = images - 1
    wide = width + 2 * HALO
    reach = 256
    group = ROWS * GROUPS
    half = width // 2
    column_rows = 4 * group
    tile = lax.axis_index("tile")
    lane = lax.broadcasted_iota(jnp.int32, (8, 128), 1)

    def present(step):
        return (tile + step >= 0) & (tile + step < count)

    def remote(source, target, place, step):
        return pltpu.make_async_remote_copy(
            src_ref=source, dst_ref=target, send_sem=send.at[place], recv_sem=recv.at[place],
            device_id={"tile": tile + step}, device_id_type=pl.DeviceIdType.MESH)

    barrier = pltpu.get_barrier_semaphore()
    partners = 0
    for step in (1, -1, 2, -2, 3, -3):
        @pl.when(present(step))
        def _(step=step):
            pl.semaphore_signal(barrier, inc=1, device_id={"tile": tile + step}, device_id_type=pl.DeviceIdType.MESH)

        partners = partners + jnp.where(present(step), 1, 0)
    loads = [
        pltpu.make_async_copy(source, target, local.at[place])
        for place, (source, target) in enumerate((
            (wq, weights.at[pl.ds(0, CH)]),
            (wv, weights.at[pl.ds(CH, CH)]),
            (sec, own.at[pl.ds(1, pairs)]),
            (ref, own.at[0]),
            (first, taps.at[0]),
            (second, taps.at[1]),
            (offsets, shifts.at[0]),
        ))
    ]
    for load in loads:
        load.start()
    pl.semaphore_wait(barrier, partners)

    tail = pl.ds(width - HALO, HALO)
    head = pl.ds(0, HALO)
    upward = [
        remote(sec.at[:, :, tail, :], left.at[pl.ds(1, pairs)], 0, 1),
        remote(ref.at[:, tail, :], left.at[0], 1, 1),
        remote(offsets, before, 2, 1),
    ]
    downward = [
        remote(sec.at[:, :, head, :], right.at[pl.ds(1, pairs)], 3, -1),
        remote(ref.at[:, head, :], right.at[0], 4, -1),
        remote(offsets, after, 5, -1),
    ]
    for step, copies in ((1, upward), (-1, downward)):
        @pl.when(present(step))
        def _(copies=copies):
            for copy in copies:
                copy.start()
    for step, halo, entry in ((-1, left, before), (1, right, after)):
        @pl.when(jnp.logical_not(present(step)))
        def _(halo=halo, entry=entry):
            halo[...] = jnp.zeros_like(halo)
            entry[...] = jnp.zeros_like(entry)
    for step in (1, 2, 3):
        @pl.when(jnp.logical_not(present(step)))
        def _(step=step):
            middle[step] = jnp.zeros(middle.shape[1:], F32)
            rim[step] = jnp.zeros(rim.shape[1:], F32)

    spot = lax.broadcasted_iota(jnp.int32, (wide, reach), 1)
    query = lax.broadcasted_iota(jnp.int32, (wide, reach), 0)
    key = spot - jnp.where(spot >= 2 * wide, 2 * wide, jnp.where(spot >= wide, wide, 0))
    column = key + (tile * width - HALO)
    near = (key - query <= RAD) & (query - key <= RAD) & (column >= 0) & (column < count * width) & (spot < 3 * wide)
    for row in range(ROWS):
        allowed = near
        if row == 0:
            allowed = allowed & (spot >= wide)
        if row == ROWS - 1:
            allowed = allowed & (spot < 2 * wide)
        bias[row] = jnp.where(allowed, 0.0, -1e30)
    for image in range(images):
        for at, size in ((0, wide), ((ROWS + 1) * wide, reach - 2 * wide)):
            keys[image, at:at + size, :] = jnp.zeros((size, 128), BF16)
            values[image, at:at + size, :] = jnp.zeros((size, 128), BF16)
        for row in range(ROWS):
            for at in (0, HALO + width):
                projected[image, row, at:at + HALO, :] = jnp.zeros((HALO, 128), F32)
    loads[0].wait()
    loads[1].wait()
    packed = jnp.concatenate(split2(weights[...]), axis=0)

    def project(value):
        hi, lo = split2(value)
        both = dot_nt(hi, packed) + dot_nt(lo, packed)
        return both[:, :128] + both[:, 128:]

    def project_own(image):
        both = project(own[image].reshape(ROWS * width, own.shape[3]))
        for row in range(ROWS):
            projected[image, row, HALO:HALO + width, :] = both[row * width:(row + 1) * width]

    ones = jnp.ones((reach, 128), BF16)

    def prepare(which, parts):
        for image in which:
            for row in range(ROWS):
                for at, size in parts:
                    value = projected[image, row, at:at + size, :]
                    low = lower_half(value)
                    hi, rest = rounded(value)
                    turned_hi, turned_rest = pltpu.roll(hi, CH, 1), pltpu.roll(rest, CH, 1)
                    queries[image, row, at:at + size, :] = jnp.concatenate(
                        [jnp.where(low, hi, turned_hi) * (1.0 / CH), jnp.where(low, rest, turned_rest) * (1.0 / CH)],
                        axis=1).astype(BF16)
                    rows = slice((row + 1) * wide + at, (row + 1) * wide + at + size)
                    keys[image, rows, :] = jnp.where(low, hi, turned_rest).astype(BF16)
                    values[image, rows, :] = jnp.where(low, turned_hi, rest).astype(BF16)

    def attention(which, parts):
        def taken(array):
            pieces = [array[at:at + size] for at, size in parts]
            return pieces[0] if len(pieces) == 1 else jnp.concatenate(pieces, axis=0)

        places = [(image, row) for image in which for row in range(ROWS)]
        scores = []
        for image, row in places:
            seen = keys[image, row * wide:row * wide + reach, :]
            scores.append(
                dot_nt(taken(queries.at[image, row]), jnp.concatenate([seen, seen], axis=1)) + taken(bias.at[row]))
        raised = [split2(jnp.exp(score - jnp.max(score, axis=1, keepdims=True))) for score in scores]
        result = [[None] * ROWS for _ in range(images)]
        for (image, row), (hi, lo) in zip(places, raised):
            mixed = jnp.concatenate([values[image, row * wide:row * wide + reach, :], ones], axis=1)
            total = dot(hi, mixed) + dot(lo, mixed)
            shared = total[:, :128] + pltpu.roll(total[:, :128], CH, 1)
            value = taken(projected.at[image, row])
            value = jnp.where(lower_half(value), pltpu.roll(value, CH, 1), value)
            result[image][row] = value + shared / total[:, 128:]
        return result

    def paired(parts, place):
        return jnp.where(lower_half(parts[0]), parts[2 * place], parts[2 * place + 1])

    def keep_reference(parts, start):
        size = parts[0].shape[0]
        column = lax.broadcasted_iota(jnp.int32, (size, 128), 0) + (tile * width - HALO + start)
        inside = (column >= 0) & (column < count * width)
        for row in range(ROWS):
            scaled = jnp.where(inside, parts[row], 0.0) * (1.0 / (CH // GROUPS))
            for place, part in enumerate(rounded(scaled)):
                edge[row, place, start:start + size, :] = part

    inner = ((0, wide),)
    others = tuple(range(1, images))
    rest = HALO // 2
    outer = ((0, 2 * HALO), (width, 2 * HALO))
    loads[2].wait()
    loads[3].wait()
    sends = []
    for image in range(images):
        project_own(image)
    prepare((*others, 0), inner)
    features = attention((*others, 0), inner)
    for pair in range(pairs):
        for place in range(2):
            middle[0, pair, place] = paired(features[pair + 1], place)[HALO + rest:HALO + width - rest]
        for step in (1, 3):
            copy = remote(middle.at[0, pair], middle.at[step, pair], 6 + 3 * pair + step - 1, -step)
            sends.append((step, copy))

            @pl.when(present(-step))
            def _(copy=copy):
                copy.start()

    keep_reference(features[0], 0)
    loads[4].wait()
    loads[5].wait()
    loads[6].wait()
    band_weights(taps, spread, w_hi, w_lo)
    def arrived(chosen):
        for step, copies in ((1, upward), (-1, downward)):
            @pl.when(present(-step))
            def _(copies=copies):
                for copy in copies[chosen]:
                    copy.wait_recv()

    def project_halo(start, stop):
        size = (stop - start) * ROWS * HALO
        both = project(jnp.concatenate(
            [side[start:stop].reshape(size, own.shape[3]) for side in (left, right)], axis=0))
        for image in range(start, stop):
            for row in range(ROWS):
                base = ((image - start) * ROWS + row) * HALO
                projected[image, row, 0:HALO, :] = both[base:base + HALO]
                projected[image, row, HALO + width:wide, :] = both[size + base:size + base + HALO]

    arrived(slice(0, 1))
    project_halo(1, images)
    prepare(others, outer)
    features = attention(others, outer)
    for pair in range(pairs):
        for place in range(2):
            feature = paired(features[pair + 1], place)
            behind[pair, place] = feature[:HALO]
            rim[0, pair, place] = jnp.concatenate(
                [feature[HALO:HALO + rest], feature[2 * HALO + rest:3 * HALO]], axis=0)
    rims = []
    for step in (1, 2, 3):
        copy = remote(rim.at[0], rim.at[step], 6 + 3 * pairs + step - 1, -step)
        rims.append((step, copy))

        @pl.when(present(-step))
        def _(copy=copy):
            copy.start()

    arrived(slice(1, 3))
    entries = [
        pltpu.make_async_copy(source, shifts.at[place], local.at[6 + place])
        for place, source in ((1, before), (2, after))
    ]
    for entry in entries:
        entry.start()
    project_halo(0, 1)
    prepare((0,), outer)
    features = attention((0,), outer)
    odd = tile % 2 == 1
    forwards = []
    for step, copy in sends:
        @pl.when(present(step))
        def _(copy=copy):
            copy.wait_recv()

        pair = len(forwards) // 2
        offset, chosen = (-1, odd) if step == 1 else (1, jnp.logical_not(odd))
        forward = remote(middle.at[step, pair], middle.at[2, pair], 7 + 3 * pair, offset)
        going = chosen & present(step)
        forwards.append((going, forward))

        @pl.when(going)
        def _(forward=forward):
            forward.start()

    keep_reference([part[:2 * HALO] for part in features[0]], 0)
    keep_reference([part[2 * HALO:] for part in features[0]], width)
    own_group = (lane % CH) // (CH // GROUPS) == lax.broadcasted_iota(jnp.int32, (8, 128), 0)
    pad = HALO - 2
    for row in range(ROWS):
        for place in range(2):
            for col in range(0, width + 4, 2):
                pair_rows = [
                    jnp.where(own_group, jnp.broadcast_to(edge[row, place, pad + at:pad + at + 1, :], (8, 128)), 0.0)
                    for at in (col, col + 1)
                ]
                main[row, col * 8:col * 8 + 16, place * 128:(place + 1) * 128] = (
                    jnp.concatenate(pair_rows, axis=0).astype(BF16))
    for entry in entries:
        entry.wait()

    def joined(hi, lo, row):
        low = lower_half(hi)
        if row % 2 == 0:
            return jnp.where(low, hi, pltpu.roll(lo, CH, 1))
        return jnp.where(low, pltpu.roll(hi, CH, 1), lo)

    for step, copy in rims:
        @pl.when(present(step))
        def _(copy=copy):
            copy.wait_recv()

    for pair in range(pairs):
        @pl.when(present(2))
        def _(forward=forwards[2 * pair][1]):
            forward.wait_recv()

    for pair in range(pairs):
        for side in range(2):
            for step in range(4):
                start = step * width
                window[pair, side, start:start + rest, :] = rim[step, pair, side, :rest, :]
                window[pair, side, start + rest:start + width - rest, :] = middle[step, pair, side]
                window[pair, side, start + width - rest:start + width, :] = rim[step, pair, side, rest:, :]
            wrap[pair, side, :width - HALO, :] = jnp.zeros((width - HALO, 128), F32)
            wrap[pair, side, width - HALO:, :] = behind[pair, side]
    odds = [lax.rem(shifts[0, 0, pair], 2) for pair in range(pairs)]
    floors = [lax.div(shifts[0, 0, pair] - odds[pair], 2) for pair in range(pairs)]
    ceilings = [floors[pair] + odds[pair] for pair in range(pairs)]
    first_half = lower_half(lane)

    def turned(value, begin, pair):
        return pltpu.roll(value, (256 + CH * pair - begin) & 127, 1)

    def halves(value, flag):
        return jnp.where(flag, value[1], value[0]), jnp.where(flag, value[0], value[1])

    def levels(even, odd):
        size = even.shape[0]
        at = lax.broadcasted_iota(jnp.int32, (size, 128), 1) % CH
        return (
            jnp.where(at >= 1, pltpu.roll(odd, 1, 1), 0.0), even, odd,
            jnp.where(at < CH - 1, pltpu.roll(even, 127, 1), 0.0))

    for side in range(2):
        products = []
        for row in (2 * side, 2 * side + 1):
            for pair in range(pairs):
                flag = odds[pair] == 1
                strided = [window[pair, side, pl.ds(at, 2 * width, stride=2), :] for at in range(2)]
                strided_wrap = [
                    jnp.concatenate([strided[at][:3 * half], wrap[pair, side, pl.ds(at, half, stride=2), :]], axis=0)
                    for at in range(2)
                ]
                whole, ends = [
                    jnp.concatenate([joined(*rounded(part), row) for part in halves(value, flag)], axis=0).astype(BF16)
                    for value in (strided, strided_wrap)
                ]
                products.append((
                    dot_nt(main[row], jnp.concatenate([whole, whole], axis=1)),
                    dot_nt(main[row, 0:16, :], jnp.concatenate([ends, ends], axis=1))))
        for col in range(width + 4):
            x = col - 2
            evens, odds_of = [], []
            for place in range(2):
                made = []
                for pair in range(pairs):
                    whole, ends = products[place * pairs + pair]
                    source = (ends if x < 0 else whole)[col * 8:(col + 1) * 8]
                    same, other = source[:, :128], source[:, 128:]
                    if 0 <= x < width:
                        low, high = floors[pair] + (x + x % 2) // 2, ceilings[pair] + x // 2
                        if x % 2:
                            made.append((turned(other, high, pair), turned(same, low, pair)))
                        else:
                            made.append((turned(same, low, pair), turned(other, high, pair)))
                    else:
                        q = odds[pair]
                        begin = shifts[1 if x < 0 else 2, 0, pair] + x + 256
                        match = lax.rem(begin, 2) == q
                        made.append((
                            turned(jnp.where(match, same, other),
                                   lax.div(jnp.where(match, begin - q, begin - 1 + q), 2) - 128, pair),
                            turned(jnp.where(match, other, same),
                                   lax.div(jnp.where(match, begin + q, begin + 1 - q), 2) - 128, pair)))
                evens.append(jnp.where(first_half, made[0][0], made[1][0]))
                odds_of.append(jnp.where(first_half, made[0][1], made[1][1]))
            for at, value in enumerate(levels(jnp.concatenate(evens, axis=0), jnp.concatenate(odds_of, axis=0))):
                hi, lo = split2(value)
                for part, base in ((0, -2), (1, half - 2)):
                    if 0 <= x - base < half + 4:
                        start = (x - base) * column_rows + at * group + side * 16
                        volume_hi[start:start + 16, part * 128:(part + 1) * 128] = hi
                        volume_lo[start:start + 16, part * 128:(part + 1) * 128] = lo

    def convolved(conv, hi_ref, lo_ref, tiles, finish):
        carry = None
        out_rows = column_rows
        for at in range(tiles):
            rows = slice(at * 2 * column_rows, (at + 1) * 2 * column_rows)
            hi, lo = hi_ref[rows, :], lo_ref[rows, :]
            used = slice(out_rows if at == 0 else 0, out_rows if at == tiles - 1 else 2 * out_rows)
            wh, wl = w_hi[conv, used, :], w_lo[conv, used, :]
            both = dot(wh, hi) + dot(wl, hi) + dot(wh, lo)
            if at:
                finish(at - 1, jnp.maximum(carry + both[:out_rows], 0.0))
            carry = both if at == 0 else both[out_rows:]

    def finish_first(at, value):
        for part in range(2):
            lanes = slice(part * 128, (part + 1) * 128)
            for col in range(2):
                rows = value[col * 2 * group:(col + 1) * 2 * group, lanes]
                if part == 0 and at == 0 and col == 0:
                    rows = jnp.where(tile == 0, 0.0, rows)
                if part == 1 and at == half // 2 and col == 1:
                    rows = jnp.where(tile == count - 1, 0.0, rows)
                start = (2 * at + col) * column_rows
                for place, piece in enumerate(levels(rows[:group], rows[group:])):
                    hi, lo = split2(piece)
                    first_hi[start + place * group:start + (place + 1) * group, lanes] = hi
                    first_lo[start + place * group:start + (place + 1) * group, lanes] = lo

    def finish_second(at, value):
        for part in range(2):
            pieces = []
            for col in range(2):
                rows = value[col * 2 * group:(col + 1) * 2 * group, part * 128:(part + 1) * 128]
                total = rows + pltpu.roll(rows, CH, 1)
                pieces.append(jnp.where(lower_half(total[:group]), total[:group], total[group:]))
            score = jnp.sum(jnp.concatenate(pieces, axis=0).reshape(2 * ROWS, GROUPS, 128), axis=1)
            start = (part * half + 2 * at) * ROWS
            sums[start:start + 2 * ROWS, :] = score

    convolved(0, volume_hi, volume_lo, half // 2 + 2, finish_first)
    convolved(1, first_hi, first_lo, half // 2 + 1, finish_second)
    score = sums[...]
    weight = jnp.exp(score - jnp.max(score, axis=1, keepdims=True))
    spot = lax.broadcasted_iota(jnp.int32, score.shape, 1)
    level = jnp.where(spot < CH, 2 * spot, 2 * spot - (2 * CH - 1)).astype(F32)
    mean = jnp.sum(weight * level, axis=1, keepdims=True) / (jnp.sum(weight, axis=1, keepdims=True) * DISP)
    pixel = lax.broadcasted_iota(jnp.int32, score.shape, 0)
    placed = jnp.where(pixel // ROWS == spot, mean, 0.0)
    pick = jnp.where(
        lax.broadcasted_iota(jnp.int32, (16, width * ROWS), 1) % ROWS
        == lax.broadcasted_iota(jnp.int32, (16, width * ROWS), 0), 1.0, 0.0).astype(BF16)
    final = reduce(jnp.add, [dot(pick, part) for part in split3(placed)])
    out[...] = final[:ROWS, :width]
    for step, copies in ((1, upward), (-1, downward)):
        @pl.when(present(step))
        def _(copies=copies):
            for copy in copies:
                copy.wait_send()

    for step, copy in (*sends, *rims):
        @pl.when(present(-step))
        def _(copy=copy):
            copy.wait_send()

    for going, forward in forwards:
        @pl.when(going)
        def _(forward=forward):
            forward.wait_send()


def on_device(reference_feat, secondary_feat, pair_offsets, w_query_key, w_value, conv_first, conv_second):
    pairs = secondary_feat.shape[0]
    images = pairs + 1
    width, features = reference_feat.shape[1:]
    wide = width + 2 * HALO
    group = ROWS * GROUPS
    held = (ROWS + 2) * wide + 256 - 3 * wide
    copies = 9 + 3 * pairs
    banded = pltpu.VMEM((2, 8 * group, 8 * group), BF16)
    costs = pltpu.VMEM(((width // 2 + 4) * 4 * group, 256), BF16)
    firsts = pltpu.VMEM(((width // 2 + 2) * 4 * group, 256), BF16)
    first, second = (jnp.transpose(conv, (2, 3, 4, 0, 1)) for conv in (conv_first, conv_second))
    return pl.pallas_call(
        functools.partial(stereo_kernel, images, width, lax.axis_size("tile")),
        out_shape=jax.ShapeDtypeStruct((ROWS, width), F32),
        in_specs=[pl.BlockSpec(memory_space=pltpu.HBM)] * 7,
        out_specs=pl.BlockSpec(memory_space=pltpu.VMEM),
        scratch_shapes=[
            pltpu.VMEM((images, ROWS, HALO, features), F32),
            pltpu.VMEM((images, ROWS, HALO, features), F32),
            pltpu.VMEM((images, ROWS, width, features), F32),
            pltpu.VMEM((2 * CH, features), F32),
            pltpu.VMEM((2, 3, 3, 3, GROUPS, GROUPS), F32),
            pltpu.VMEM((12, group, 128), F32),
            pltpu.VMEM((images, ROWS, wide, 2 * CH), F32),
            pltpu.VMEM((ROWS, wide, 256), F32),
            pltpu.VMEM((images, ROWS, wide, 256), BF16),
            pltpu.VMEM((images, held, 128), BF16),
            pltpu.VMEM((images, held, 128), BF16),
            pltpu.VMEM((ROWS, 2, wide, 128), F32),
            pltpu.VMEM((ROWS, (width + 4) * GROUPS, 256), BF16),
            banded, banded,
            pltpu.VMEM((4, pairs, 2, width - HALO, 128), F32),
            pltpu.VMEM((4, pairs, 2, HALO, 128), F32),
            pltpu.VMEM((pairs, 2, HALO, 128), F32),
            pltpu.VMEM((pairs, 2, 4 * width, 128), F32),
            pltpu.VMEM((pairs, 2, width, 128), F32),
            pltpu.VMEM((1, pairs), jnp.int32),
            pltpu.VMEM((1, pairs), jnp.int32),
            pltpu.SMEM((3, 1, pairs), jnp.int32),
            costs, costs, firsts, firsts,
            pltpu.VMEM((width * ROWS, 128), F32),
            pltpu.SemaphoreType.DMA((9,)),
            pltpu.SemaphoreType.DMA((copies,)),
            pltpu.SemaphoreType.DMA((copies,)),
        ],
        compiler_params=pltpu.CompilerParams(
            vmem_limit_bytes=55168 << 10, collective_id=0, has_side_effects=True),
    )(pair_offsets.T, reference_feat, secondary_feat, w_query_key.T, w_value.T, first, second)


def solution(mesh):
    return jax.shard_map(
        on_device,
        mesh=mesh,
        in_specs=(
            P("groups", "tile", None),
            P("groups", None, "tile", None),
            P("groups", "tile"),
            P(),
            P(),
            P(),
            P(),
        ),
        out_specs=P("groups", "tile"),
        check_vma=False,
    )
```

```python
import functools
from functools import reduce

import jax
import jax.numpy as jnp
from jax import lax
from jax.experimental import pallas as pl
from jax.experimental.pallas import tpu as pltpu
from jax.sharding import PartitionSpec as P

GROUPS = 8
DISP = 128
RAD = 3
ROWS = 4
CH = 64
LANES = ROWS * CH
HALO = 8
F32 = jnp.float32
BF16 = jnp.bfloat16


def dot(a, b):
    return jnp.dot(a, b, preferred_element_type=F32)


def split2(x):
    hi = x.astype(BF16)
    return hi, (x - hi.astype(F32)).astype(BF16)


def split3(x):
    hi = x.astype(BF16)
    rest = x - hi.astype(F32)
    mid = rest.astype(BF16)
    return hi, mid, (rest - mid.astype(F32)).astype(BF16)


def dot_nt(a, b):
    return lax.dot_general(a, b, (((1,), (1,)), ((), ())), preferred_element_type=F32)


def rounded(value):
    hi = value.astype(BF16).astype(F32)
    return hi, value - hi


def lower_half(value):
    return lax.broadcasted_iota(jnp.int32, value.shape, 1) < CH


def band_weights(taps, spread, turned, w_hi, w_lo):
    group = ROWS * GROUPS
    empty = jnp.zeros((GROUPS, GROUPS), F32)
    for conv in range(2):
        for col in range(3):
            for phase in range(2):
                for row in range(ROWS):
                    pieces = []
                    for level in range(4):
                        for source in range(ROWS):
                            step, depth = source - row + 1, level - phase
                            used = 0 <= step < 3 and 0 <= depth < 3
                            pieces.append(taps[conv, step, col, depth] if used else empty)
                    spread[(conv * 3 + col) * 2 + phase, row * GROUPS:(row + 1) * GROUPS, :] = (
                        jnp.concatenate(pieces, axis=1))
    size = 4 * group
    layout = (((2, None), (1, 2)), ((0, 1), (None, 0)))
    for conv in range(2):
        for part in range(2):
            for place in range(2):
                lanes = slice(place * 128, (place + 1) * 128)
                pieces = []
                for col in range(2):
                    tap = layout[part][col][place]
                    if tap is None:
                        pieces.append(jnp.zeros((2 * group, 128), F32))
                    else:
                        pieces.extend(spread[(conv * 3 + tap) * 2 + phase] for phase in range(2))
                whole = jnp.concatenate(pieces, axis=0)
                if conv == 0:
                    hi, lo = split2(whole)
                    w_hi[0, part * size:(part + 1) * size, lanes] = hi
                    w_lo[0, part * size:(part + 1) * size, lanes] = lo
                    continue
                turned[part, place] = whole
                for channel in range(GROUPS):
                    hi, lo = split2(turned[part, place, pl.ds(channel, 2 * GROUPS, stride=GROUPS), :])
                    rows = slice(part * size + channel * 2 * GROUPS, part * size + (channel + 1) * 2 * GROUPS)
                    w_hi[1, rows, lanes] = hi
                    w_lo[1, rows, lanes] = lo


def stereo_kernel(images, width, count, offsets, ref, sec, wq, wv, first, second, out,
                  left, right, own, weights, taps, spread, ordered, projected, bias, queries, keys, values, edge, main,
                  w_hi, w_lo, middle, rim, behind, window, wrap, before, after, shifts,
                  volume_hi, volume_lo, first_hi, first_lo, sums, local, send, recv):
    pairs = images - 1
    wide = width + 2 * HALO
    reach = 256
    group = ROWS * GROUPS
    half = width // 2
    column_rows = 4 * group
    tile = lax.axis_index("tile")
    lane = lax.broadcasted_iota(jnp.int32, (8, 128), 1)

    def present(step):
        return (tile + step >= 0) & (tile + step < count)

    def remote(source, target, place, step):
        return pltpu.make_async_remote_copy(
            src_ref=source, dst_ref=target, send_sem=send.at[place], recv_sem=recv.at[place],
            device_id={"tile": tile + step}, device_id_type=pl.DeviceIdType.MESH)

    barrier = pltpu.get_barrier_semaphore()
    partners = 0
    for step in (1, -1, 2, -2, 3, -3):
        @pl.when(present(step))
        def _(step=step):
            pl.semaphore_signal(barrier, inc=1, device_id={"tile": tile + step}, device_id_type=pl.DeviceIdType.MESH)

        partners = partners + jnp.where(present(step), 1, 0)
    loads = [
        pltpu.make_async_copy(source, target, local.at[place])
        for place, (source, target) in enumerate((
            (wq, weights.at[pl.ds(0, CH)]),
            (wv, weights.at[pl.ds(CH, CH)]),
            (sec, own.at[pl.ds(1, pairs)]),
            (ref, own.at[0]),
            (first, taps.at[0]),
            (second, taps.at[1]),
            (offsets, shifts.at[0]),
        ))
    ]
    for load in loads:
        load.start()
    pl.semaphore_wait(barrier, partners)

    tail = pl.ds(width - HALO, HALO)
    head = pl.ds(0, HALO)
    upward = [
        remote(sec.at[:, :, tail, :], left.at[pl.ds(1, pairs)], 0, 1),
        remote(ref.at[:, tail, :], left.at[0], 1, 1),
        remote(offsets, before, 2, 1),
    ]
    downward = [
        remote(sec.at[:, :, head, :], right.at[pl.ds(1, pairs)], 3, -1),
        remote(ref.at[:, head, :], right.at[0], 4, -1),
        remote(offsets, after, 5, -1),
    ]
    for step, copies in ((1, upward), (-1, downward)):
        @pl.when(present(step))
        def _(copies=copies):
            for copy in copies:
                copy.start()
    for step, halo, entry in ((-1, left, before), (1, right, after)):
        @pl.when(jnp.logical_not(present(step)))
        def _(halo=halo, entry=entry):
            halo[...] = jnp.zeros_like(halo)
            entry[...] = jnp.zeros_like(entry)
    for step in (1, 2, 3):
        @pl.when(jnp.logical_not(present(step)))
        def _(step=step):
            middle[step] = jnp.zeros(middle.shape[1:], F32)
            rim[step] = jnp.zeros(rim.shape[1:], F32)

    spot = lax.broadcasted_iota(jnp.int32, (wide, reach), 1)
    query = lax.broadcasted_iota(jnp.int32, (wide, reach), 0)
    key = spot - jnp.where(spot >= 2 * wide, 2 * wide, jnp.where(spot >= wide, wide, 0))
    column = key + (tile * width - HALO)
    near = (key - query <= RAD) & (query - key <= RAD) & (column >= 0) & (column < count * width) & (spot < 3 * wide)
    for row in range(ROWS):
        allowed = near
        if row == 0:
            allowed = allowed & (spot >= wide)
        if row == ROWS - 1:
            allowed = allowed & (spot < 2 * wide)
        bias[row] = jnp.where(allowed, 0.0, -1e30)
    for image in range(images):
        for at, size in ((0, wide), ((ROWS + 1) * wide, reach - 2 * wide)):
            keys[image, at:at + size, :] = jnp.zeros((size, 128), BF16)
            values[image, at:at + size, :] = jnp.zeros((size, 128), BF16)
        for row in range(ROWS):
            for at in (0, HALO + width):
                projected[image, row, at:at + HALO, :] = jnp.zeros((HALO, 128), F32)
    loads[0].wait()
    loads[1].wait()
    packed = jnp.concatenate(split2(weights[...]), axis=0)

    def project(value):
        hi, lo = split2(value)
        both = dot_nt(hi, packed) + dot_nt(lo, packed)
        return both[:, :128] + both[:, 128:]

    def project_own(image):
        both = project(own[image].reshape(ROWS * width, own.shape[3]))
        for row in range(ROWS):
            projected[image, row, HALO:HALO + width, :] = both[row * width:(row + 1) * width]

    ones = jnp.ones((reach, 128), BF16)

    def prepare(which, parts):
        for image in which:
            for row in range(ROWS):
                for at, size in parts:
                    value = projected[image, row, at:at + size, :]
                    low = lower_half(value)
                    hi, rest = rounded(value)
                    turned_hi, turned_rest = pltpu.roll(hi, CH, 1), pltpu.roll(rest, CH, 1)
                    queries[image, row, at:at + size, :] = jnp.concatenate(
                        [jnp.where(low, hi, turned_hi) * (1.0 / CH), jnp.where(low, rest, turned_rest) * (1.0 / CH)],
                        axis=1).astype(BF16)
                    rows = slice((row + 1) * wide + at, (row + 1) * wide + at + size)
                    keys[image, rows, :] = jnp.where(low, hi, turned_rest).astype(BF16)
                    values[image, rows, :] = jnp.where(low, turned_hi, rest).astype(BF16)

    def attention(which, parts):
        def taken(array):
            pieces = [array[at:at + size] for at, size in parts]
            return pieces[0] if len(pieces) == 1 else jnp.concatenate(pieces, axis=0)

        places = [(image, row) for image in which for row in range(ROWS)]
        scores = []
        for image, row in places:
            seen = keys[image, row * wide:row * wide + reach, :]
            scores.append(
                dot_nt(taken(queries.at[image, row]), jnp.concatenate([seen, seen], axis=1)) + taken(bias.at[row]))
        raised = [split2(jnp.exp(score - jnp.max(score, axis=1, keepdims=True))) for score in scores]
        result = [[None] * ROWS for _ in range(images)]
        for (image, row), (hi, lo) in zip(places, raised):
            mixed = jnp.concatenate([values[image, row * wide:row * wide + reach, :], ones], axis=1)
            total = dot(hi, mixed) + dot(lo, mixed)
            shared = total[:, :128] + pltpu.roll(total[:, :128], CH, 1)
            value = taken(projected.at[image, row])
            value = jnp.where(lower_half(value), pltpu.roll(value, CH, 1), value)
            result[image][row] = value + shared / total[:, 128:]
        return result

    def paired(parts, place):
        return jnp.where(lower_half(parts[0]), parts[2 * place], parts[2 * place + 1])

    def keep_reference(parts, start):
        size = parts[0].shape[0]
        column = lax.broadcasted_iota(jnp.int32, (size, 128), 0) + (tile * width - HALO + start)
        inside = (column >= 0) & (column < count * width)
        for row in range(ROWS):
            scaled = jnp.where(inside, parts[row], 0.0) * (1.0 / (CH // GROUPS))
            for place, part in enumerate(rounded(scaled)):
                edge[row, place, start:start + size, :] = part

    inner = ((0, wide),)
    others = tuple(range(1, images))
    rest = HALO // 2
    outer = ((0, 2 * HALO), (width, 2 * HALO))
    loads[2].wait()
    sends = []
    for image in others:
        project_own(image)
    prepare(others, inner)
    features = attention(others, inner)
    for pair in range(pairs):
        for place in range(2):
            middle[0, pair, place] = paired(features[pair + 1], place)[HALO + rest:HALO + width - rest]
        for step in (1, 3):
            copy = remote(middle.at[0, pair], middle.at[step, pair], 6 + 3 * pair + step - 1, -step)
            sends.append((step, copy))

            @pl.when(present(-step))
            def _(copy=copy):
                copy.start()

    loads[3].wait()
    project_own(0)
    prepare((0,), inner)
    keep_reference(attention((0,), inner)[0], 0)
    loads[4].wait()
    loads[5].wait()
    loads[6].wait()
    band_weights(taps, spread, ordered, w_hi, w_lo)
    def arrived(chosen):
        for step, copies in ((1, upward), (-1, downward)):
            @pl.when(present(-step))
            def _(copies=copies):
                for copy in copies[chosen]:
                    copy.wait_recv()

    def project_halo(start, stop):
        size = (stop - start) * ROWS * HALO
        both = project(jnp.concatenate(
            [side[start:stop].reshape(size, own.shape[3]) for side in (left, right)], axis=0))
        for image in range(start, stop):
            for row in range(ROWS):
                base = ((image - start) * ROWS + row) * HALO
                projected[image, row, 0:HALO, :] = both[base:base + HALO]
                projected[image, row, HALO + width:wide, :] = both[size + base:size + base + HALO]

    arrived(slice(0, 1))
    project_halo(1, images)
    prepare(others, outer)
    features = attention(others, outer)
    for pair in range(pairs):
        for place in range(2):
            feature = paired(features[pair + 1], place)
            behind[pair, place] = feature[:HALO]
            rim[0, pair, place] = jnp.concatenate(
                [feature[HALO:HALO + rest], feature[2 * HALO + rest:3 * HALO]], axis=0)
    rims = []
    for step in (1, 2, 3):
        copy = remote(rim.at[0], rim.at[step], 6 + 3 * pairs + step - 1, -step)
        rims.append((step, copy))

        @pl.when(present(-step))
        def _(copy=copy):
            copy.start()

    arrived(slice(1, 3))
    entries = [
        pltpu.make_async_copy(source, shifts.at[place], local.at[6 + place])
        for place, source in ((1, before), (2, after))
    ]
    for entry in entries:
        entry.start()
    project_halo(0, 1)
    prepare((0,), outer)
    features = attention((0,), outer)
    odd = tile % 2 == 1
    forwards = []
    for step, copy in sends:
        @pl.when(present(step))
        def _(copy=copy):
            copy.wait_recv()

        pair = len(forwards) // 2
        offset, chosen = (-1, odd) if step == 1 else (1, jnp.logical_not(odd))
        forward = remote(middle.at[step, pair], middle.at[2, pair], 7 + 3 * pair, offset)
        going = chosen & present(step)
        forwards.append((going, forward))

        @pl.when(going)
        def _(forward=forward):
            forward.start()

    keep_reference([part[:2 * HALO] for part in features[0]], 0)
    keep_reference([part[2 * HALO:] for part in features[0]], width)
    own_group = (lane % CH) // (CH // GROUPS) == lax.broadcasted_iota(jnp.int32, (8, 128), 0)
    pad = HALO - 2
    for row in range(ROWS):
        for place in range(2):
            for col in range(0, width + 4, 2):
                pair_rows = [
                    jnp.where(own_group, jnp.broadcast_to(edge[row, place, pad + at:pad + at + 1, :], (8, 128)), 0.0)
                    for at in (col, col + 1)
                ]
                main[row, col * 8:col * 8 + 16, place * 128:(place + 1) * 128] = (
                    jnp.concatenate(pair_rows, axis=0).astype(BF16))
    for entry in entries:
        entry.wait()

    def joined(hi, lo, row):
        low = lower_half(hi)
        if row % 2 == 0:
            return jnp.where(low, hi, pltpu.roll(lo, CH, 1))
        return jnp.where(low, pltpu.roll(hi, CH, 1), lo)

    for step, copy in rims:
        @pl.when(present(step))
        def _(copy=copy):
            copy.wait_recv()

    for pair in range(pairs):
        @pl.when(present(2))
        def _(forward=forwards[2 * pair][1]):
            forward.wait_recv()

    for pair in range(pairs):
        for side in range(2):
            for step in range(4):
                start = step * width
                window[pair, side, start:start + rest, :] = rim[step, pair, side, :rest, :]
                window[pair, side, start + rest:start + width - rest, :] = middle[step, pair, side]
                window[pair, side, start + width - rest:start + width, :] = rim[step, pair, side, rest:, :]
            wrap[pair, side, :width - HALO, :] = jnp.zeros((width - HALO, 128), F32)
            wrap[pair, side, width - HALO:, :] = behind[pair, side]
    odds = [lax.rem(shifts[0, 0, pair], 2) for pair in range(pairs)]
    floors = [lax.div(shifts[0, 0, pair] - odds[pair], 2) for pair in range(pairs)]
    ceilings = [floors[pair] + odds[pair] for pair in range(pairs)]
    first_half = lower_half(lane)

    def turned(value, begin, pair):
        return pltpu.roll(value, (256 + CH * pair - begin) & 127, 1)

    def halves(value, flag):
        return jnp.where(flag, value[1], value[0]), jnp.where(flag, value[0], value[1])

    def levels(even, odd):
        size = even.shape[0]
        at = lax.broadcasted_iota(jnp.int32, (size, 128), 1) % CH
        return (
            jnp.where(at >= 1, pltpu.roll(odd, 1, 1), 0.0), even, odd,
            jnp.where(at < CH - 1, pltpu.roll(even, 127, 1), 0.0))

    for side in range(2):
        products = []
        for row in (2 * side, 2 * side + 1):
            for pair in range(pairs):
                flag = odds[pair] == 1
                strided = [window[pair, side, pl.ds(at, 2 * width, stride=2), :] for at in range(2)]
                strided_wrap = [
                    jnp.concatenate([strided[at][:3 * half], wrap[pair, side, pl.ds(at, half, stride=2), :]], axis=0)
                    for at in range(2)
                ]
                whole, ends = [
                    jnp.concatenate([joined(*rounded(part), row) for part in halves(value, flag)], axis=0).astype(BF16)
                    for value in (strided, strided_wrap)
                ]
                products.append((
                    dot_nt(main[row], jnp.concatenate([whole, whole], axis=1)),
                    dot_nt(main[row, 0:16, :], jnp.concatenate([ends, ends], axis=1))))
        for col in range(width + 4):
            x = col - 2
            evens, odds_of = [], []
            for place in range(2):
                made = []
                for pair in range(pairs):
                    whole, ends = products[place * pairs + pair]
                    source = (ends if x < 0 else whole)[col * 8:(col + 1) * 8]
                    same, other = source[:, :128], source[:, 128:]
                    if 0 <= x < width:
                        low, high = floors[pair] + (x + x % 2) // 2, ceilings[pair] + x // 2
                        if x % 2:
                            made.append((turned(other, high, pair), turned(same, low, pair)))
                        else:
                            made.append((turned(same, low, pair), turned(other, high, pair)))
                    else:
                        q = odds[pair]
                        begin = shifts[1 if x < 0 else 2, 0, pair] + x + 256
                        match = lax.rem(begin, 2) == q
                        made.append((
                            turned(jnp.where(match, same, other),
                                   lax.div(jnp.where(match, begin - q, begin - 1 + q), 2) - 128, pair),
                            turned(jnp.where(match, other, same),
                                   lax.div(jnp.where(match, begin + q, begin + 1 - q), 2) - 128, pair)))
                evens.append(jnp.where(first_half, made[0][0], made[1][0]))
                odds_of.append(jnp.where(first_half, made[0][1], made[1][1]))
            for at, value in enumerate(levels(jnp.concatenate(evens, axis=0), jnp.concatenate(odds_of, axis=0))):
                hi, lo = split2(value)
                for part, base in ((0, -2), (1, half - 2)):
                    if 0 <= x - base < half + 4:
                        start = (x - base) * column_rows + at * group + side * 16
                        volume_hi[start:start + 16, part * 128:(part + 1) * 128] = hi
                        volume_lo[start:start + 16, part * 128:(part + 1) * 128] = lo

    def convolved(conv, hi_ref, lo_ref, tiles, finish):
        carry = None
        out_rows = column_rows
        for at in range(tiles):
            rows = slice(at * 2 * column_rows, (at + 1) * 2 * column_rows)
            hi, lo = hi_ref[rows, :], lo_ref[rows, :]
            used = slice(out_rows if at == 0 else 0, out_rows if at == tiles - 1 else 2 * out_rows)
            wh, wl = w_hi[conv, used, :], w_lo[conv, used, :]
            both = dot(wh, hi) + dot(wl, hi) + dot(wh, lo)
            if at:
                finish(at - 1, jnp.maximum(carry + both[:out_rows], 0.0))
            carry = both if at == 0 else both[out_rows:]

    def finish_first(at, value):
        for part in range(2):
            lanes = slice(part * 128, (part + 1) * 128)
            for col in range(2):
                rows = value[col * 2 * group:(col + 1) * 2 * group, lanes]
                if part == 0 and at == 0 and col == 0:
                    rows = jnp.where(tile == 0, 0.0, rows)
                if part == 1 and at == half // 2 and col == 1:
                    rows = jnp.where(tile == count - 1, 0.0, rows)
                start = (2 * at + col) * column_rows
                for place, piece in enumerate(levels(rows[:group], rows[group:])):
                    hi, lo = split2(piece)
                    first_hi[start + place * group:start + (place + 1) * group, lanes] = hi
                    first_lo[start + place * group:start + (place + 1) * group, lanes] = lo

    def finish_second(at, value):
        top = lax.broadcasted_iota(jnp.int32, (8, 128), 0) < ROWS
        for part in range(2):
            totals = []
            for col in range(2):
                total = reduce(jnp.add, [
                    value[channel * 16 + col * 8:channel * 16 + col * 8 + 8, part * 128:(part + 1) * 128]
                    for channel in range(GROUPS)
                ])
                total = total + pltpu.roll(total, CH, 1)
                totals.append((total, pltpu.roll(total, ROWS, 0)))
            upper = jnp.where(first_half, totals[0][0], totals[0][1])
            lower = jnp.where(first_half, totals[1][1], totals[1][0])
            start = (part * half + 2 * at) * ROWS
            sums[start:start + 2 * ROWS, :] = jnp.where(top, upper, lower)

    convolved(0, volume_hi, volume_lo, half // 2 + 2, finish_first)
    convolved(1, first_hi, first_lo, half // 2 + 1, finish_second)
    score = sums[...]
    weight = jnp.exp(score - jnp.max(score, axis=1, keepdims=True))
    spot = lax.broadcasted_iota(jnp.int32, score.shape, 1)
    level = jnp.where(spot < CH, 2 * spot, 2 * spot - (2 * CH - 1)).astype(F32)
    mean = jnp.sum(weight * level, axis=1, keepdims=True) / (jnp.sum(weight, axis=1, keepdims=True) * DISP)
    pixel = lax.broadcasted_iota(jnp.int32, score.shape, 0)
    placed = jnp.where(pixel // ROWS == spot, mean, 0.0)
    pick = jnp.where(
        lax.broadcasted_iota(jnp.int32, (16, width * ROWS), 1) % ROWS
        == lax.broadcasted_iota(jnp.int32, (16, width * ROWS), 0), 1.0, 0.0).astype(BF16)
    final = reduce(jnp.add, [dot(pick, part) for part in split3(placed)])
    out[...] = final[:ROWS, :width]
    for step, copies in ((1, upward), (-1, downward)):
        @pl.when(present(step))
        def _(copies=copies):
            for copy in copies:
                copy.wait_send()

    for step, copy in (*sends, *rims):
        @pl.when(present(-step))
        def _(copy=copy):
            copy.wait_send()

    for going, forward in forwards:
        @pl.when(going)
        def _(forward=forward):
            forward.wait_send()


def on_device(reference_feat, secondary_feat, pair_offsets, w_query_key, w_value, conv_first, conv_second):
    pairs = secondary_feat.shape[0]
    images = pairs + 1
    width, features = reference_feat.shape[1:]
    wide = width + 2 * HALO
    group = ROWS * GROUPS
    held = (ROWS + 2) * wide + 256 - 3 * wide
    copies = 9 + 3 * pairs
    banded = pltpu.VMEM((2, 8 * group, 8 * group), BF16)
    costs = pltpu.VMEM(((width // 2 + 4) * 4 * group, 256), BF16)
    firsts = pltpu.VMEM(((width // 2 + 2) * 4 * group, 256), BF16)
    first, second = (jnp.transpose(conv, (2, 3, 4, 0, 1)) for conv in (conv_first, conv_second))
    return pl.pallas_call(
        functools.partial(stereo_kernel, images, width, lax.axis_size("tile")),
        out_shape=jax.ShapeDtypeStruct((ROWS, width), F32),
        in_specs=[pl.BlockSpec(memory_space=pltpu.HBM)] * 7,
        out_specs=pl.BlockSpec(memory_space=pltpu.VMEM),
        scratch_shapes=[
            pltpu.VMEM((images, ROWS, HALO, features), F32),
            pltpu.VMEM((images, ROWS, HALO, features), F32),
            pltpu.VMEM((images, ROWS, width, features), F32),
            pltpu.VMEM((2 * CH, features), F32),
            pltpu.VMEM((2, 3, 3, 3, GROUPS, GROUPS), F32),
            pltpu.VMEM((12, group, 128), F32),
            pltpu.VMEM((2, 2, 4 * group, 128), F32),
            pltpu.VMEM((images, ROWS, wide, 2 * CH), F32),
            pltpu.VMEM((ROWS, wide, 256), F32),
            pltpu.VMEM((images, ROWS, wide, 256), BF16),
            pltpu.VMEM((images, held, 128), BF16),
            pltpu.VMEM((images, held, 128), BF16),
            pltpu.VMEM((ROWS, 2, wide, 128), F32),
            pltpu.VMEM((ROWS, (width + 4) * GROUPS, 256), BF16),
            banded, banded,
            pltpu.VMEM((4, pairs, 2, width - HALO, 128), F32),
            pltpu.VMEM((4, pairs, 2, HALO, 128), F32),
            pltpu.VMEM((pairs, 2, HALO, 128), F32),
            pltpu.VMEM((pairs, 2, 4 * width, 128), F32),
            pltpu.VMEM((pairs, 2, width, 128), F32),
            pltpu.VMEM((1, pairs), jnp.int32),
            pltpu.VMEM((1, pairs), jnp.int32),
            pltpu.SMEM((3, 1, pairs), jnp.int32),
            costs, costs, firsts, firsts,
            pltpu.VMEM((width * ROWS, 128), F32),
            pltpu.SemaphoreType.DMA((9,)),
            pltpu.SemaphoreType.DMA((copies,)),
            pltpu.SemaphoreType.DMA((copies,)),
        ],
        compiler_params=pltpu.CompilerParams(
            vmem_limit_bytes=55168 << 10, collective_id=0, has_side_effects=True),
    )(pair_offsets.T, reference_feat, secondary_feat, w_query_key.T, w_value.T, first, second)


def solution(mesh):
    return jax.shard_map(
        on_device,
        mesh=mesh,
        in_specs=(
            P("groups", "tile", None),
            P("groups", None, "tile", None),
            P("groups", "tile"),
            P(),
            P(),
            P(),
            P(),
        ),
        out_specs=P("groups", "tile"),
        check_vma=False,
    )
```

```python
import functools
from functools import reduce

import jax
import jax.numpy as jnp
from jax import lax
from jax.experimental import pallas as pl
from jax.experimental.pallas import tpu as pltpu
from jax.sharding import PartitionSpec as P

GROUPS = 8
DISP = 128
RAD = 3
ROWS = 4
CH = 64
LANES = ROWS * CH
HALO = 8
F32 = jnp.float32
BF16 = jnp.bfloat16


def dot(a, b):
    return jnp.dot(a, b, preferred_element_type=F32)


def split2(x):
    hi = x.astype(BF16)
    return hi, (x - hi.astype(F32)).astype(BF16)


def split3(x):
    hi = x.astype(BF16)
    rest = x - hi.astype(F32)
    mid = rest.astype(BF16)
    return hi, mid, (rest - mid.astype(F32)).astype(BF16)


def dot_nt(a, b):
    return lax.dot_general(a, b, (((1,), (1,)), ((), ())), preferred_element_type=F32)


def rounded(value):
    hi = value.astype(BF16).astype(F32)
    return hi, value - hi


def lower_half(value):
    return lax.broadcasted_iota(jnp.int32, value.shape, 1) < CH


def band_weights(taps, spread, turned, w_hi, w_lo):
    group = ROWS * GROUPS
    empty = jnp.zeros((GROUPS, GROUPS), F32)
    for conv in range(2):
        for col in range(3):
            for phase in range(2):
                for row in range(ROWS):
                    pieces = []
                    for level in range(4):
                        for source in range(ROWS):
                            step, depth = source - row + 1, level - phase
                            used = 0 <= step < 3 and 0 <= depth < 3
                            pieces.append(taps[conv, step, col, depth] if used else empty)
                    spread[(conv * 3 + col) * 2 + phase, row * GROUPS:(row + 1) * GROUPS, :] = (
                        jnp.concatenate(pieces, axis=1))
    size = 4 * group
    layout = (((2, None), (1, 2)), ((0, 1), (None, 0)))
    for conv in range(2):
        for part in range(2):
            for place in range(2):
                lanes = slice(place * 128, (place + 1) * 128)
                pieces = []
                for col in range(2):
                    tap = layout[part][col][place]
                    if tap is None:
                        pieces.append(jnp.zeros((2 * group, 128), F32))
                    else:
                        pieces.extend(spread[(conv * 3 + tap) * 2 + phase] for phase in range(2))
                whole = jnp.concatenate(pieces, axis=0)
                if conv == 0:
                    hi, lo = split2(whole)
                    w_hi[0, part * size:(part + 1) * size, lanes] = hi
                    w_lo[0, part * size:(part + 1) * size, lanes] = lo
                    continue
                turned[part, place] = whole
                for channel in range(GROUPS):
                    hi, lo = split2(turned[part, place, pl.ds(channel, 2 * GROUPS, stride=GROUPS), :])
                    rows = slice(part * size + channel * 2 * GROUPS, part * size + (channel + 1) * 2 * GROUPS)
                    w_hi[1, rows, lanes] = hi
                    w_lo[1, rows, lanes] = lo


def stereo_kernel(images, width, count, offsets, ref, sec, wq, wv, first, second, out,
                  left, right, own, weights, taps, spread, ordered, projected, bias, queries, keys, values, edge, main,
                  w_hi, w_lo, middle, rim, behind, window, wrap, before, after, shifts,
                  volume_hi, volume_lo, first_hi, first_lo, sums, local, send, recv):
    pairs = images - 1
    wide = width + 2 * HALO
    reach = 256
    group = ROWS * GROUPS
    half = width // 2
    column_rows = 4 * group
    tile = lax.axis_index("tile")
    lane = lax.broadcasted_iota(jnp.int32, (8, 128), 1)

    def present(step):
        return (tile + step >= 0) & (tile + step < count)

    def remote(source, target, place, step):
        return pltpu.make_async_remote_copy(
            src_ref=source, dst_ref=target, send_sem=send.at[place], recv_sem=recv.at[place],
            device_id={"tile": tile + step}, device_id_type=pl.DeviceIdType.MESH)

    barrier = pltpu.get_barrier_semaphore()
    partners = 0
    for step in (1, -1, 2, -2, 3, -3):
        @pl.when(present(step))
        def _(step=step):
            pl.semaphore_signal(barrier, inc=1, device_id={"tile": tile + step}, device_id_type=pl.DeviceIdType.MESH)

        partners = partners + jnp.where(present(step), 1, 0)
    loads = [
        pltpu.make_async_copy(source, target, local.at[place])
        for place, (source, target) in enumerate((
            (wq, weights.at[pl.ds(0, CH)]),
            (wv, weights.at[pl.ds(CH, CH)]),
            (sec, own.at[pl.ds(1, pairs)]),
            (ref, own.at[0]),
            (first, taps.at[0]),
            (second, taps.at[1]),
            (offsets, shifts.at[0]),
        ))
    ]
    for load in loads:
        load.start()
    pl.semaphore_wait(barrier, partners)

    tail = pl.ds(width - HALO, HALO)
    head = pl.ds(0, HALO)
    upward = [
        remote(sec.at[:, :, tail, :], left.at[pl.ds(1, pairs)], 0, 1),
        remote(ref.at[:, tail, :], left.at[0], 1, 1),
        remote(offsets, before, 2, 1),
    ]
    downward = [
        remote(sec.at[:, :, head, :], right.at[pl.ds(1, pairs)], 3, -1),
        remote(ref.at[:, head, :], right.at[0], 4, -1),
        remote(offsets, after, 5, -1),
    ]
    for step, copies in ((1, upward), (-1, downward)):
        @pl.when(present(step))
        def _(copies=copies):
            for copy in copies:
                copy.start()
    for step, halo, entry in ((-1, left, before), (1, right, after)):
        @pl.when(jnp.logical_not(present(step)))
        def _(halo=halo, entry=entry):
            halo[...] = jnp.zeros_like(halo)
            entry[...] = jnp.zeros_like(entry)
    for step in (1, 2, 3):
        @pl.when(jnp.logical_not(present(step)))
        def _(step=step):
            middle[step] = jnp.zeros(middle.shape[1:], F32)
            rim[step] = jnp.zeros(rim.shape[1:], F32)

    spot = lax.broadcasted_iota(jnp.int32, (wide, reach), 1)
    query = lax.broadcasted_iota(jnp.int32, (wide, reach), 0)
    key = spot - jnp.where(spot >= 2 * wide, 2 * wide, jnp.where(spot >= wide, wide, 0))
    column = key + (tile * width - HALO)
    near = (key - query <= RAD) & (query - key <= RAD) & (column >= 0) & (column < count * width) & (spot < 3 * wide)
    for row in range(ROWS):
        allowed = near
        if row == 0:
            allowed = allowed & (spot >= wide)
        if row == ROWS - 1:
            allowed = allowed & (spot < 2 * wide)
        bias[row] = jnp.where(allowed, 0.0, -1e30)
    for image in range(images):
        for at, size in ((0, wide), ((ROWS + 1) * wide, reach - 2 * wide)):
            keys[image, at:at + size, :] = jnp.zeros((size, 128), BF16)
            values[image, at:at + size, :] = jnp.zeros((size, 128), BF16)
        for row in range(ROWS):
            for at in (0, HALO + width):
                projected[image, row, at:at + HALO, :] = jnp.zeros((HALO, 128), F32)
    loads[0].wait()
    loads[1].wait()
    packed = jnp.concatenate(split2(weights[...]), axis=0)

    def project(value):
        hi, lo = split2(value)
        both = dot_nt(hi, packed) + dot_nt(lo, packed)
        return both[:, :128] + both[:, 128:]

    def project_own(image):
        both = project(own[image].reshape(ROWS * width, own.shape[3]))
        for row in range(ROWS):
            projected[image, row, HALO:HALO + width, :] = both[row * width:(row + 1) * width]

    ones = jnp.ones((reach, 128), BF16)

    def prepare(which, parts):
        for image in which:
            for row in range(ROWS):
                for at, size in parts:
                    value = projected[image, row, at:at + size, :]
                    low = lower_half(value)
                    hi, rest = rounded(value)
                    turned_hi, turned_rest = pltpu.roll(hi, CH, 1), pltpu.roll(rest, CH, 1)
                    queries[image, row, at:at + size, :] = jnp.concatenate(
                        [jnp.where(low, hi, turned_hi) * (1.0 / CH), jnp.where(low, rest, turned_rest) * (1.0 / CH)],
                        axis=1).astype(BF16)
                    rows = slice((row + 1) * wide + at, (row + 1) * wide + at + size)
                    keys[image, rows, :] = jnp.where(low, hi, turned_rest).astype(BF16)
                    values[image, rows, :] = jnp.where(low, turned_hi, rest).astype(BF16)

    def attention(which, parts):
        def taken(array):
            pieces = [array[at:at + size] for at, size in parts]
            return pieces[0] if len(pieces) == 1 else jnp.concatenate(pieces, axis=0)

        places = [(image, row) for image in which for row in range(ROWS)]
        scores = []
        for image, row in places:
            seen = keys[image, row * wide:row * wide + reach, :]
            scores.append(
                dot_nt(taken(queries.at[image, row]), jnp.concatenate([seen, seen], axis=1)) + taken(bias.at[row]))
        raised = [split2(jnp.exp(score - jnp.max(score, axis=1, keepdims=True))) for score in scores]
        result = [[None] * ROWS for _ in range(images)]
        for (image, row), (hi, lo) in zip(places, raised):
            mixed = jnp.concatenate([values[image, row * wide:row * wide + reach, :], ones], axis=1)
            total = dot(hi, mixed) + dot(lo, mixed)
            shared = total[:, :128] + pltpu.roll(total[:, :128], CH, 1)
            value = taken(projected.at[image, row])
            value = jnp.where(lower_half(value), pltpu.roll(value, CH, 1), value)
            result[image][row] = value + shared / total[:, 128:]
        return result

    def paired(parts, place):
        return jnp.where(lower_half(parts[0]), parts[2 * place], parts[2 * place + 1])

    def keep_reference(parts, start):
        size = parts[0].shape[0]
        column = lax.broadcasted_iota(jnp.int32, (size, 128), 0) + (tile * width - HALO + start)
        inside = (column >= 0) & (column < count * width)
        for row in range(ROWS):
            scaled = jnp.where(inside, parts[row], 0.0) * (1.0 / (CH // GROUPS))
            for place, part in enumerate(rounded(scaled)):
                edge[row, place, start:start + size, :] = part

    inner = ((0, wide),)
    others = tuple(range(1, images))
    rest = HALO // 2
    outer = ((0, 2 * HALO), (width, 2 * HALO))
    loads[2].wait()
    loads[3].wait()
    sends = []
    for image in range(images):
        project_own(image)
    prepare((*others, 0), inner)
    features = attention((*others, 0), inner)
    for pair in range(pairs):
        for place in range(2):
            middle[0, pair, place] = paired(features[pair + 1], place)[HALO + rest:HALO + width - rest]
        for step in (1, 3):
            copy = remote(middle.at[0, pair], middle.at[step, pair], 6 + 3 * pair + step - 1, -step)
            sends.append((step, copy))

            @pl.when(present(-step))
            def _(copy=copy):
                copy.start()

    keep_reference(features[0], 0)
    loads[4].wait()
    loads[5].wait()
    loads[6].wait()
    band_weights(taps, spread, ordered, w_hi, w_lo)
    def arrived(chosen):
        for step, copies in ((1, upward), (-1, downward)):
            @pl.when(present(-step))
            def _(copies=copies):
                for copy in copies[chosen]:
                    copy.wait_recv()

    def project_halo(start, stop):
        size = (stop - start) * ROWS * HALO
        both = project(jnp.concatenate(
            [side[start:stop].reshape(size, own.shape[3]) for side in (left, right)], axis=0))
        for image in range(start, stop):
            for row in range(ROWS):
                base = ((image - start) * ROWS + row) * HALO
                projected[image, row, 0:HALO, :] = both[base:base + HALO]
                projected[image, row, HALO + width:wide, :] = both[size + base:size + base + HALO]

    arrived(slice(0, 1))
    project_halo(1, images)
    prepare(others, outer)
    features = attention(others, outer)
    for pair in range(pairs):
        for place in range(2):
            feature = paired(features[pair + 1], place)
            behind[pair, place] = feature[:HALO]
            rim[0, pair, place] = jnp.concatenate(
                [feature[HALO:HALO + rest], feature[2 * HALO + rest:3 * HALO]], axis=0)
    rims = []
    for step in (1, 2, 3):
        copy = remote(rim.at[0], rim.at[step], 6 + 3 * pairs + step - 1, -step)
        rims.append((step, copy))

        @pl.when(present(-step))
        def _(copy=copy):
            copy.start()

    arrived(slice(1, 3))
    entries = [
        pltpu.make_async_copy(source, shifts.at[place], local.at[6 + place])
        for place, source in ((1, before), (2, after))
    ]
    for entry in entries:
        entry.start()
    project_halo(0, 1)
    prepare((0,), outer)
    features = attention((0,), outer)
    odd = tile % 2 == 1
    forwards = []
    for step, copy in sends:
        @pl.when(present(step))
        def _(copy=copy):
            copy.wait_recv()

        pair = len(forwards) // 2
        offset, chosen = (-1, odd) if step == 1 else (1, jnp.logical_not(odd))
        forward = remote(middle.at[step, pair], middle.at[2, pair], 7 + 3 * pair, offset)
        going = chosen & present(step)
        forwards.append((going, forward))

        @pl.when(going)
        def _(forward=forward):
            forward.start()

    keep_reference([part[:2 * HALO] for part in features[0]], 0)
    keep_reference([part[2 * HALO:] for part in features[0]], width)
    own_group = (lane % CH) // (CH // GROUPS) == lax.broadcasted_iota(jnp.int32, (8, 128), 0)
    pad = HALO - 2
    for row in range(ROWS):
        for place in range(2):
            for col in range(0, width + 4, 2):
                pair_rows = [
                    jnp.where(own_group, jnp.broadcast_to(edge[row, place, pad + at:pad + at + 1, :], (8, 128)), 0.0)
                    for at in (col, col + 1)
                ]
                main[row, col * 8:col * 8 + 16, place * 128:(place + 1) * 128] = (
                    jnp.concatenate(pair_rows, axis=0).astype(BF16))
    for entry in entries:
        entry.wait()

    def joined(hi, lo, row):
        low = lower_half(hi)
        if row % 2 == 0:
            return jnp.where(low, hi, pltpu.roll(lo, CH, 1))
        return jnp.where(low, pltpu.roll(hi, CH, 1), lo)

    for step, copy in rims:
        @pl.when(present(step))
        def _(copy=copy):
            copy.wait_recv()

    for pair in range(pairs):
        @pl.when(present(2))
        def _(forward=forwards[2 * pair][1]):
            forward.wait_recv()

    for pair in range(pairs):
        for side in range(2):
            for step in range(4):
                start = step * width
                window[pair, side, start:start + rest, :] = rim[step, pair, side, :rest, :]
                window[pair, side, start + rest:start + width - rest, :] = middle[step, pair, side]
                window[pair, side, start + width - rest:start + width, :] = rim[step, pair, side, rest:, :]
            wrap[pair, side, :width - HALO, :] = jnp.zeros((width - HALO, 128), F32)
            wrap[pair, side, width - HALO:, :] = behind[pair, side]
    odds = [lax.rem(shifts[0, 0, pair], 2) for pair in range(pairs)]
    floors = [lax.div(shifts[0, 0, pair] - odds[pair], 2) for pair in range(pairs)]
    ceilings = [floors[pair] + odds[pair] for pair in range(pairs)]
    first_half = lower_half(lane)

    def turned(value, begin, pair):
        return pltpu.roll(value, (256 + CH * pair - begin) & 127, 1)

    def halves(value, flag):
        return jnp.where(flag, value[1], value[0]), jnp.where(flag, value[0], value[1])

    def levels(even, odd):
        size = even.shape[0]
        at = lax.broadcasted_iota(jnp.int32, (size, 128), 1) % CH
        return (
            jnp.where(at >= 1, pltpu.roll(odd, 1, 1), 0.0), even, odd,
            jnp.where(at < CH - 1, pltpu.roll(even, 127, 1), 0.0))

    for side in range(2):
        products = []
        for row in (2 * side, 2 * side + 1):
            for pair in range(pairs):
                flag = odds[pair] == 1
                strided = [window[pair, side, pl.ds(at, 2 * width, stride=2), :] for at in range(2)]
                strided_wrap = [
                    jnp.concatenate([strided[at][:3 * half], wrap[pair, side, pl.ds(at, half, stride=2), :]], axis=0)
                    for at in range(2)
                ]
                whole, ends = [
                    jnp.concatenate([joined(*rounded(part), row) for part in halves(value, flag)], axis=0).astype(BF16)
                    for value in (strided, strided_wrap)
                ]
                products.append((
                    dot_nt(main[row], jnp.concatenate([whole, whole], axis=1)),
                    dot_nt(main[row, 0:16, :], jnp.concatenate([ends, ends], axis=1))))
        for col in range(width + 4):
            x = col - 2
            evens, odds_of = [], []
            for place in range(2):
                made = []
                for pair in range(pairs):
                    whole, ends = products[place * pairs + pair]
                    source = (ends if x < 0 else whole)[col * 8:(col + 1) * 8]
                    same, other = source[:, :128], source[:, 128:]
                    if 0 <= x < width:
                        low, high = floors[pair] + (x + x % 2) // 2, ceilings[pair] + x // 2
                        if x % 2:
                            made.append((turned(other, high, pair), turned(same, low, pair)))
                        else:
                            made.append((turned(same, low, pair), turned(other, high, pair)))
                    else:
                        q = odds[pair]
                        begin = shifts[1 if x < 0 else 2, 0, pair] + x + 256
                        match = lax.rem(begin, 2) == q
                        made.append((
                            turned(jnp.where(match, same, other),
                                   lax.div(jnp.where(match, begin - q, begin - 1 + q), 2) - 128, pair),
                            turned(jnp.where(match, other, same),
                                   lax.div(jnp.where(match, begin + q, begin + 1 - q), 2) - 128, pair)))
                evens.append(jnp.where(first_half, made[0][0], made[1][0]))
                odds_of.append(jnp.where(first_half, made[0][1], made[1][1]))
            for at, value in enumerate(levels(jnp.concatenate(evens, axis=0), jnp.concatenate(odds_of, axis=0))):
                hi, lo = split2(value)
                for part, base in ((0, -2), (1, half - 2)):
                    if 0 <= x - base < half + 4:
                        start = (x - base) * column_rows + at * group + side * 16
                        volume_hi[start:start + 16, part * 128:(part + 1) * 128] = hi
                        volume_lo[start:start + 16, part * 128:(part + 1) * 128] = lo

    def convolved(conv, hi_ref, lo_ref, tiles, finish):
        carry = None
        out_rows = column_rows
        for at in range(tiles):
            rows = slice(at * 2 * column_rows, (at + 1) * 2 * column_rows)
            hi, lo = hi_ref[rows, :], lo_ref[rows, :]
            used = slice(out_rows if at == 0 else 0, out_rows if at == tiles - 1 else 2 * out_rows)
            wh, wl = w_hi[conv, used, :], w_lo[conv, used, :]
            both = dot(wh, hi) + dot(wl, hi) + dot(wh, lo)
            if at:
                finish(at - 1, jnp.maximum(carry + both[:out_rows], 0.0))
            carry = both if at == 0 else both[out_rows:]

    def finish_first(at, value):
        for part in range(2):
            lanes = slice(part * 128, (part + 1) * 128)
            for col in range(2):
                rows = value[col * 2 * group:(col + 1) * 2 * group, lanes]
                if part == 0 and at == 0 and col == 0:
                    rows = jnp.where(tile == 0, 0.0, rows)
                if part == 1 and at == half // 2 and col == 1:
                    rows = jnp.where(tile == count - 1, 0.0, rows)
                start = (2 * at + col) * column_rows
                for place, piece in enumerate(levels(rows[:group], rows[group:])):
                    hi, lo = split2(piece)
                    first_hi[start + place * group:start + (place + 1) * group, lanes] = hi
                    first_lo[start + place * group:start + (place + 1) * group, lanes] = lo

    def finish_second(at, value):
        top = lax.broadcasted_iota(jnp.int32, (8, 128), 0) < ROWS
        for part in range(2):
            totals = []
            for col in range(2):
                total = reduce(jnp.add, [
                    value[channel * 16 + col * 8:channel * 16 + col * 8 + 8, part * 128:(part + 1) * 128]
                    for channel in range(GROUPS)
                ])
                total = total + pltpu.roll(total, CH, 1)
                totals.append((total, pltpu.roll(total, ROWS, 0)))
            upper = jnp.where(first_half, totals[0][0], totals[0][1])
            lower = jnp.where(first_half, totals[1][1], totals[1][0])
            start = (part * half + 2 * at) * ROWS
            sums[start:start + 2 * ROWS, :] = jnp.where(top, upper, lower)

    convolved(0, volume_hi, volume_lo, half // 2 + 2, finish_first)
    convolved(1, first_hi, first_lo, half // 2 + 1, finish_second)
    score = sums[...]
    weight = jnp.exp(score - jnp.max(score, axis=1, keepdims=True))
    spot = lax.broadcasted_iota(jnp.int32, score.shape, 1)
    level = jnp.where(spot < CH, 2 * spot, 2 * spot - (2 * CH - 1)).astype(F32)
    mean = jnp.sum(weight * level, axis=1, keepdims=True) / (jnp.sum(weight, axis=1, keepdims=True) * DISP)
    pixel = lax.broadcasted_iota(jnp.int32, score.shape, 0)
    placed = jnp.where(pixel // ROWS == spot, mean, 0.0)
    pick = jnp.where(
        lax.broadcasted_iota(jnp.int32, (16, width * ROWS), 1) % ROWS
        == lax.broadcasted_iota(jnp.int32, (16, width * ROWS), 0), 1.0, 0.0).astype(BF16)
    final = reduce(jnp.add, [dot(pick, part) for part in split3(placed)])
    out[...] = final[:ROWS, :width]
    for step, copies in ((1, upward), (-1, downward)):
        @pl.when(present(step))
        def _(copies=copies):
            for copy in copies:
                copy.wait_send()

    for step, copy in (*sends, *rims):
        @pl.when(present(-step))
        def _(copy=copy):
            copy.wait_send()

    for going, forward in forwards:
        @pl.when(going)
        def _(forward=forward):
            forward.wait_send()


def on_device(reference_feat, secondary_feat, pair_offsets, w_query_key, w_value, conv_first, conv_second):
    pairs = secondary_feat.shape[0]
    images = pairs + 1
    width, features = reference_feat.shape[1:]
    wide = width + 2 * HALO
    group = ROWS * GROUPS
    held = (ROWS + 2) * wide + 256 - 3 * wide
    copies = 9 + 3 * pairs
    banded = pltpu.VMEM((2, 8 * group, 8 * group), BF16)
    costs = pltpu.VMEM(((width // 2 + 4) * 4 * group, 256), BF16)
    firsts = pltpu.VMEM(((width // 2 + 2) * 4 * group, 256), BF16)
    first, second = (jnp.transpose(conv, (2, 3, 4, 0, 1)) for conv in (conv_first, conv_second))
    return pl.pallas_call(
        functools.partial(stereo_kernel, images, width, lax.axis_size("tile")),
        out_shape=jax.ShapeDtypeStruct((ROWS, width), F32),
        in_specs=[pl.BlockSpec(memory_space=pltpu.HBM)] * 7,
        out_specs=pl.BlockSpec(memory_space=pltpu.VMEM),
        scratch_shapes=[
            pltpu.VMEM((images, ROWS, HALO, features), F32),
            pltpu.VMEM((images, ROWS, HALO, features), F32),
            pltpu.VMEM((images, ROWS, width, features), F32),
            pltpu.VMEM((2 * CH, features), F32),
            pltpu.VMEM((2, 3, 3, 3, GROUPS, GROUPS), F32),
            pltpu.VMEM((12, group, 128), F32),
            pltpu.VMEM((2, 2, 4 * group, 128), F32),
            pltpu.VMEM((images, ROWS, wide, 2 * CH), F32),
            pltpu.VMEM((ROWS, wide, 256), F32),
            pltpu.VMEM((images, ROWS, wide, 256), BF16),
            pltpu.VMEM((images, held, 128), BF16),
            pltpu.VMEM((images, held, 128), BF16),
            pltpu.VMEM((ROWS, 2, wide, 128), F32),
            pltpu.VMEM((ROWS, (width + 4) * GROUPS, 256), BF16),
            banded, banded,
            pltpu.VMEM((4, pairs, 2, width - HALO, 128), F32),
            pltpu.VMEM((4, pairs, 2, HALO, 128), F32),
            pltpu.VMEM((pairs, 2, HALO, 128), F32),
            pltpu.VMEM((pairs, 2, 4 * width, 128), F32),
            pltpu.VMEM((pairs, 2, width, 128), F32),
            pltpu.VMEM((1, pairs), jnp.int32),
            pltpu.VMEM((1, pairs), jnp.int32),
            pltpu.SMEM((3, 1, pairs), jnp.int32),
            costs, costs, firsts, firsts,
            pltpu.VMEM((width * ROWS, 128), F32),
            pltpu.SemaphoreType.DMA((9,)),
            pltpu.SemaphoreType.DMA((copies,)),
            pltpu.SemaphoreType.DMA((copies,)),
        ],
        compiler_params=pltpu.CompilerParams(
            vmem_limit_bytes=55168 << 10, collective_id=0, has_side_effects=True),
    )(pair_offsets.T, reference_feat, secondary_feat, w_query_key.T, w_value.T, first, second)


def solution(mesh):
    return jax.shard_map(
        on_device,
        mesh=mesh,
        in_specs=(
            P("groups", "tile", None),
            P("groups", None, "tile", None),
            P("groups", "tile"),
            P(),
            P(),
            P(),
            P(),
        ),
        out_specs=P("groups", "tile"),
        check_vma=False,
    )
```

```python
import functools
from functools import reduce

import jax
import jax.numpy as jnp
from jax import lax
from jax.experimental import pallas as pl
from jax.experimental.pallas import tpu as pltpu
from jax.sharding import PartitionSpec as P

GROUPS = 8
DISP = 128
RAD = 3
ROWS = 4
CH = 64
LANES = ROWS * CH
HALO = 8
F32 = jnp.float32
BF16 = jnp.bfloat16


def dot(a, b):
    return jnp.dot(a, b, preferred_element_type=F32)


def split2(x):
    hi = x.astype(BF16)
    return hi, (x - hi.astype(F32)).astype(BF16)


def split3(x):
    hi = x.astype(BF16)
    rest = x - hi.astype(F32)
    mid = rest.astype(BF16)
    return hi, mid, (rest - mid.astype(F32)).astype(BF16)


def dot_nt(a, b):
    return lax.dot_general(a, b, (((1,), (1,)), ((), ())), preferred_element_type=F32)


def rounded(value):
    hi = value.astype(BF16).astype(F32)
    return hi, value - hi


def lower_half(value):
    return lax.broadcasted_iota(jnp.int32, value.shape, 1) < CH


def band_weights(taps, spread, turned, w_hi, w_lo):
    group = ROWS * GROUPS
    empty = jnp.zeros((GROUPS, GROUPS), F32)
    for conv in range(2):
        for col in range(3):
            for phase in range(2):
                for row in range(ROWS):
                    pieces = []
                    for level in range(4):
                        for source in range(ROWS):
                            step, depth = source - row + 1, level - phase
                            used = 0 <= step < 3 and 0 <= depth < 3
                            pieces.append(taps[conv, step, col, depth] if used else empty)
                    spread[(conv * 3 + col) * 2 + phase, row * GROUPS:(row + 1) * GROUPS, :] = (
                        jnp.concatenate(pieces, axis=1))
    size = 4 * group
    layout = (((2, None), (1, 2)), ((0, 1), (None, 0)))
    for conv in range(2):
        for part in range(2):
            for place in range(2):
                lanes = slice(place * 128, (place + 1) * 128)
                pieces = []
                for col in range(2):
                    tap = layout[part][col][place]
                    if tap is None:
                        pieces.append(jnp.zeros((2 * group, 128), F32))
                    else:
                        pieces.extend(spread[(conv * 3 + tap) * 2 + phase] for phase in range(2))
                whole = jnp.concatenate(pieces, axis=0)
                if conv == 0:
                    hi, lo = split2(whole)
                    w_hi[0, part * size:(part + 1) * size, lanes] = hi
                    w_lo[0, part * size:(part + 1) * size, lanes] = lo
                    continue
                turned[part, place] = whole
                for channel in range(GROUPS):
                    hi, lo = split2(turned[part, place, pl.ds(channel, 2 * GROUPS, stride=GROUPS), :])
                    rows = slice(part * size + channel * 2 * GROUPS, part * size + (channel + 1) * 2 * GROUPS)
                    w_hi[1, rows, lanes] = hi
                    w_lo[1, rows, lanes] = lo


def stereo_kernel(images, width, count, offsets, ref, sec, wq, wv, first, second, out,
                  left, right, own, weights, taps, spread, ordered, projected, bias, queries, keys, values, edge, main,
                  w_hi, w_lo, middle, rim, behind, window, wrap, before, after, shifts,
                  volume_hi, volume_lo, first_hi, first_lo, sums, local, send, recv):
    pairs = images - 1
    wide = width + 2 * HALO
    reach = 256
    group = ROWS * GROUPS
    half = width // 2
    column_rows = 4 * group
    tile = lax.axis_index("tile")
    lane = lax.broadcasted_iota(jnp.int32, (8, 128), 1)

    def present(step):
        return (tile + step >= 0) & (tile + step < count)

    def remote(source, target, place, step):
        return pltpu.make_async_remote_copy(
            src_ref=source, dst_ref=target, send_sem=send.at[place], recv_sem=recv.at[place],
            device_id={"tile": tile + step}, device_id_type=pl.DeviceIdType.MESH)

    barrier = pltpu.get_barrier_semaphore()
    partners = 0
    for step in (1, -1, 2, -2, 3, -3):
        @pl.when(present(step))
        def _(step=step):
            pl.semaphore_signal(barrier, inc=1, device_id={"tile": tile + step}, device_id_type=pl.DeviceIdType.MESH)

        partners = partners + jnp.where(present(step), 1, 0)
    loads = [
        pltpu.make_async_copy(source, target, local.at[place])
        for place, (source, target) in enumerate((
            (wq, weights.at[pl.ds(0, CH)]),
            (wv, weights.at[pl.ds(CH, CH)]),
            (sec, own.at[pl.ds(1, pairs)]),
            (ref, own.at[0]),
            (first, taps.at[0]),
            (second, taps.at[1]),
            (offsets, shifts.at[0]),
        ))
    ]
    for load in loads:
        load.start()
    pl.semaphore_wait(barrier, partners)

    tail = pl.ds(width - HALO, HALO)
    head = pl.ds(0, HALO)
    upward = [
        remote(sec.at[:, :, tail, :], left.at[pl.ds(1, pairs)], 0, 1),
        remote(ref.at[:, tail, :], left.at[0], 1, 1),
        remote(offsets, before, 2, 1),
    ]
    downward = [
        remote(sec.at[:, :, head, :], right.at[pl.ds(1, pairs)], 3, -1),
        remote(ref.at[:, head, :], right.at[0], 4, -1),
        remote(offsets, after, 5, -1),
    ]
    for step, copies in ((1, upward), (-1, downward)):
        @pl.when(present(step))
        def _(copies=copies):
            for copy in copies:
                copy.start()
    for step, halo, entry in ((-1, left, before), (1, right, after)):
        @pl.when(jnp.logical_not(present(step)))
        def _(halo=halo, entry=entry):
            halo[...] = jnp.zeros_like(halo)
            entry[...] = jnp.zeros_like(entry)
    for step in (1, 2, 3):
        @pl.when(jnp.logical_not(present(step)))
        def _(step=step):
            middle[step] = jnp.zeros(middle.shape[1:], F32)
            rim[step] = jnp.zeros(rim.shape[1:], F32)

    spot = lax.broadcasted_iota(jnp.int32, (wide, reach), 1)
    query = lax.broadcasted_iota(jnp.int32, (wide, reach), 0)
    key = spot - jnp.where(spot >= 2 * wide, 2 * wide, jnp.where(spot >= wide, wide, 0))
    column = key + (tile * width - HALO)
    near = (key - query <= RAD) & (query - key <= RAD) & (column >= 0) & (column < count * width) & (spot < 3 * wide)
    for row in range(ROWS):
        allowed = near
        if row == 0:
            allowed = allowed & (spot >= wide)
        if row == ROWS - 1:
            allowed = allowed & (spot < 2 * wide)
        bias[row] = jnp.where(allowed, 0.0, -1e30)
    for image in range(images):
        for at, size in ((0, wide), ((ROWS + 1) * wide, reach - 2 * wide)):
            keys[image, at:at + size, :] = jnp.zeros((size, 128), BF16)
            values[image, at:at + size, :] = jnp.zeros((size, 128), BF16)
        for row in range(ROWS):
            for at in (0, HALO + width):
                projected[image, row, at:at + HALO, :] = jnp.zeros((HALO, 128), F32)
    loads[0].wait()
    loads[1].wait()
    packed = jnp.concatenate(split2(weights[...]), axis=0)

    def project(value):
        hi, lo = split2(value)
        both = dot_nt(hi, packed) + dot_nt(lo, packed)
        return both[:, :128] + both[:, 128:]

    def project_own(image):
        both = project(own[image].reshape(ROWS * width, own.shape[3]))
        for row in range(ROWS):
            projected[image, row, HALO:HALO + width, :] = both[row * width:(row + 1) * width]

    ones = jnp.ones((reach, 128), BF16)

    def prepare(which, parts):
        for image in which:
            for row in range(ROWS):
                for at, size in parts:
                    value = projected[image, row, at:at + size, :]
                    low = lower_half(value)
                    hi, rest = rounded(value)
                    turned_hi, turned_rest = pltpu.roll(hi, CH, 1), pltpu.roll(rest, CH, 1)
                    queries[image, row, at:at + size, :] = jnp.concatenate(
                        [jnp.where(low, hi, turned_hi) * (1.0 / CH), jnp.where(low, rest, turned_rest) * (1.0 / CH)],
                        axis=1).astype(BF16)
                    rows = slice((row + 1) * wide + at, (row + 1) * wide + at + size)
                    keys[image, rows, :] = jnp.where(low, hi, turned_rest).astype(BF16)
                    values[image, rows, :] = jnp.where(low, turned_hi, rest).astype(BF16)

    def attention(which, parts):
        def taken(array):
            pieces = [array[at:at + size] for at, size in parts]
            return pieces[0] if len(pieces) == 1 else jnp.concatenate(pieces, axis=0)

        places = [(image, row) for image in which for row in range(ROWS)]
        scores = []
        for image, row in places:
            seen = keys[image, row * wide:row * wide + reach, :]
            scores.append(
                dot_nt(taken(queries.at[image, row]), jnp.concatenate([seen, seen], axis=1)) + taken(bias.at[row]))
        raised = [split2(jnp.exp(score - jnp.max(score, axis=1, keepdims=True))) for score in scores]
        result = [[None] * ROWS for _ in range(images)]
        for (image, row), (hi, lo) in zip(places, raised):
            mixed = jnp.concatenate([values[image, row * wide:row * wide + reach, :], ones], axis=1)
            total = dot(hi, mixed) + dot(lo, mixed)
            shared = total[:, :128] + pltpu.roll(total[:, :128], CH, 1)
            value = taken(projected.at[image, row])
            value = jnp.where(lower_half(value), pltpu.roll(value, CH, 1), value)
            result[image][row] = value + shared / total[:, 128:]
        return result

    def paired(parts, place):
        return jnp.where(lower_half(parts[0]), parts[2 * place], parts[2 * place + 1])

    def keep_reference(parts, start):
        size = parts[0].shape[0]
        column = lax.broadcasted_iota(jnp.int32, (size, 128), 0) + (tile * width - HALO + start)
        inside = (column >= 0) & (column < count * width)
        for row in range(ROWS):
            scaled = jnp.where(inside, parts[row], 0.0) * (1.0 / (CH // GROUPS))
            for place, part in enumerate(rounded(scaled)):
                edge[row, place, start:start + size, :] = part

    inner = ((0, wide),)
    others = tuple(range(1, images))
    rest = HALO // 2
    outer = ((0, 2 * HALO), (width, 2 * HALO))
    loads[2].wait()
    loads[3].wait()
    sends = []
    for image in range(images):
        project_own(image)
    prepare((*others, 0), inner)
    features = attention((*others, 0), inner)
    for pair in range(pairs):
        for place in range(2):
            middle[0, pair, place] = paired(features[pair + 1], place)[HALO + rest:HALO + width - rest]
    for step in (1, 3):
        copy = remote(middle.at[0], middle.at[step], 5 + step, -step)
        sends.append((step, copy))

        @pl.when(present(-step))
        def _(copy=copy):
            copy.start()

    keep_reference(features[0], 0)
    loads[4].wait()
    loads[5].wait()
    loads[6].wait()
    band_weights(taps, spread, ordered, w_hi, w_lo)
    def arrived(chosen):
        for step, copies in ((1, upward), (-1, downward)):
            @pl.when(present(-step))
            def _(copies=copies):
                for copy in copies[chosen]:
                    copy.wait_recv()

    def project_halo(start, stop):
        size = (stop - start) * ROWS * HALO
        both = project(jnp.concatenate(
            [side[start:stop].reshape(size, own.shape[3]) for side in (left, right)], axis=0))
        for image in range(start, stop):
            for row in range(ROWS):
                base = ((image - start) * ROWS + row) * HALO
                projected[image, row, 0:HALO, :] = both[base:base + HALO]
                projected[image, row, HALO + width:wide, :] = both[size + base:size + base + HALO]

    arrived(slice(0, 1))
    project_halo(1, images)
    prepare(others, outer)
    features = attention(others, outer)
    for pair in range(pairs):
        for place in range(2):
            feature = paired(features[pair + 1], place)
            behind[pair, place] = feature[:HALO]
            rim[0, pair, place] = jnp.concatenate(
                [feature[HALO:HALO + rest], feature[2 * HALO + rest:3 * HALO]], axis=0)
    rims = []
    for step in (1, 2, 3):
        copy = remote(rim.at[0], rim.at[step], 8 + step, -step)
        rims.append((step, copy))

        @pl.when(present(-step))
        def _(copy=copy):
            copy.start()

    arrived(slice(1, 3))
    entries = [
        pltpu.make_async_copy(source, shifts.at[place], local.at[6 + place])
        for place, source in ((1, before), (2, after))
    ]
    for entry in entries:
        entry.start()
    project_halo(0, 1)
    prepare((0,), outer)
    features = attention((0,), outer)
    odd = tile % 2 == 1
    forwards = []
    for step, copy in sends:
        @pl.when(present(step))
        def _(copy=copy):
            copy.wait_recv()

        offset, chosen = (-1, odd) if step == 1 else (1, jnp.logical_not(odd))
        forward = remote(middle.at[step], middle.at[2], 7, offset)
        going = chosen & present(step)
        forwards.append((going, forward))

        @pl.when(going)
        def _(forward=forward):
            forward.start()

    keep_reference([part[:2 * HALO] for part in features[0]], 0)
    keep_reference([part[2 * HALO:] for part in features[0]], width)
    own_group = (lane % CH) // (CH // GROUPS) == lax.broadcasted_iota(jnp.int32, (8, 128), 0)
    pad = HALO - 2
    for row in range(ROWS):
        for place in range(2):
            for col in range(0, width + 4, 2):
                pair_rows = [
                    jnp.where(own_group, jnp.broadcast_to(edge[row, place, pad + at:pad + at + 1, :], (8, 128)), 0.0)
                    for at in (col, col + 1)
                ]
                main[row, col * 8:col * 8 + 16, place * 128:(place + 1) * 128] = (
                    jnp.concatenate(pair_rows, axis=0).astype(BF16))
    for entry in entries:
        entry.wait()

    def joined(hi, lo, row):
        low = lower_half(hi)
        if row % 2 == 0:
            return jnp.where(low, hi, pltpu.roll(lo, CH, 1))
        return jnp.where(low, pltpu.roll(hi, CH, 1), lo)

    for step, copy in rims:
        @pl.when(present(step))
        def _(copy=copy):
            copy.wait_recv()

    @pl.when(present(2))
    def _(forward=forwards[0][1]):
        forward.wait_recv()

    for pair in range(pairs):
        for side in range(2):
            for step in range(4):
                start = step * width
                window[pair, side, start:start + rest, :] = rim[step, pair, side, :rest, :]
                window[pair, side, start + rest:start + width - rest, :] = middle[step, pair, side]
                window[pair, side, start + width - rest:start + width, :] = rim[step, pair, side, rest:, :]
            wrap[pair, side, :width - HALO, :] = jnp.zeros((width - HALO, 128), F32)
            wrap[pair, side, width - HALO:, :] = behind[pair, side]
    odds = [lax.rem(shifts[0, 0, pair], 2) for pair in range(pairs)]
    floors = [lax.div(shifts[0, 0, pair] - odds[pair], 2) for pair in range(pairs)]
    ceilings = [floors[pair] + odds[pair] for pair in range(pairs)]
    first_half = lower_half(lane)

    def turned(value, begin, pair):
        return pltpu.roll(value, (256 + CH * pair - begin) & 127, 1)

    def halves(value, flag):
        return jnp.where(flag, value[1], value[0]), jnp.where(flag, value[0], value[1])

    def levels(even, odd):
        size = even.shape[0]
        at = lax.broadcasted_iota(jnp.int32, (size, 128), 1) % CH
        return (
            jnp.where(at >= 1, pltpu.roll(odd, 1, 1), 0.0), even, odd,
            jnp.where(at < CH - 1, pltpu.roll(even, 127, 1), 0.0))

    for side in range(2):
        products = []
        for row in (2 * side, 2 * side + 1):
            for pair in range(pairs):
                flag = odds[pair] == 1
                strided = [window[pair, side, pl.ds(at, 2 * width, stride=2), :] for at in range(2)]
                strided_wrap = [
                    jnp.concatenate([strided[at][:3 * half], wrap[pair, side, pl.ds(at, half, stride=2), :]], axis=0)
                    for at in range(2)
                ]
                whole, ends = [
                    jnp.concatenate([joined(*rounded(part), row) for part in halves(value, flag)], axis=0).astype(BF16)
                    for value in (strided, strided_wrap)
                ]
                products.append((
                    dot_nt(main[row], jnp.concatenate([whole, whole], axis=1)),
                    dot_nt(main[row, 0:16, :], jnp.concatenate([ends, ends], axis=1))))
        for col in range(width + 4):
            x = col - 2
            evens, odds_of = [], []
            for place in range(2):
                made = []
                for pair in range(pairs):
                    whole, ends = products[place * pairs + pair]
                    source = (ends if x < 0 else whole)[col * 8:(col + 1) * 8]
                    same, other = source[:, :128], source[:, 128:]
                    if 0 <= x < width:
                        low, high = floors[pair] + (x + x % 2) // 2, ceilings[pair] + x // 2
                        if x % 2:
                            made.append((turned(other, high, pair), turned(same, low, pair)))
                        else:
                            made.append((turned(same, low, pair), turned(other, high, pair)))
                    else:
                        q = odds[pair]
                        begin = shifts[1 if x < 0 else 2, 0, pair] + x + 256
                        match = lax.rem(begin, 2) == q
                        made.append((
                            turned(jnp.where(match, same, other),
                                   lax.div(jnp.where(match, begin - q, begin - 1 + q), 2) - 128, pair),
                            turned(jnp.where(match, other, same),
                                   lax.div(jnp.where(match, begin + q, begin + 1 - q), 2) - 128, pair)))
                evens.append(jnp.where(first_half, made[0][0], made[1][0]))
                odds_of.append(jnp.where(first_half, made[0][1], made[1][1]))
            for at, value in enumerate(levels(jnp.concatenate(evens, axis=0), jnp.concatenate(odds_of, axis=0))):
                hi, lo = split2(value)
                for part, base in ((0, -2), (1, half - 2)):
                    if 0 <= x - base < half + 4:
                        start = (x - base) * column_rows + at * group + side * 16
                        volume_hi[start:start + 16, part * 128:(part + 1) * 128] = hi
                        volume_lo[start:start + 16, part * 128:(part + 1) * 128] = lo

    def convolved(conv, hi_ref, lo_ref, tiles, finish):
        carry = None
        out_rows = column_rows
        for at in range(tiles):
            rows = slice(at * 2 * column_rows, (at + 1) * 2 * column_rows)
            hi, lo = hi_ref[rows, :], lo_ref[rows, :]
            used = slice(out_rows if at == 0 else 0, out_rows if at == tiles - 1 else 2 * out_rows)
            wh, wl = w_hi[conv, used, :], w_lo[conv, used, :]
            both = dot(wh, hi) + dot(wl, hi) + dot(wh, lo)
            if at:
                finish(at - 1, jnp.maximum(carry + both[:out_rows], 0.0))
            carry = both if at == 0 else both[out_rows:]

    def finish_first(at, value):
        for part in range(2):
            lanes = slice(part * 128, (part + 1) * 128)
            for col in range(2):
                rows = value[col * 2 * group:(col + 1) * 2 * group, lanes]
                if part == 0 and at == 0 and col == 0:
                    rows = jnp.where(tile == 0, 0.0, rows)
                if part == 1 and at == half // 2 and col == 1:
                    rows = jnp.where(tile == count - 1, 0.0, rows)
                start = (2 * at + col) * column_rows
                for place, piece in enumerate(levels(rows[:group], rows[group:])):
                    hi, lo = split2(piece)
                    first_hi[start + place * group:start + (place + 1) * group, lanes] = hi
                    first_lo[start + place * group:start + (place + 1) * group, lanes] = lo

    def finish_second(at, value):
        top = lax.broadcasted_iota(jnp.int32, (8, 128), 0) < ROWS
        for part in range(2):
            totals = []
            for col in range(2):
                total = reduce(jnp.add, [
                    value[channel * 16 + col * 8:channel * 16 + col * 8 + 8, part * 128:(part + 1) * 128]
                    for channel in range(GROUPS)
                ])
                total = total + pltpu.roll(total, CH, 1)
                totals.append((total, pltpu.roll(total, ROWS, 0)))
            upper = jnp.where(first_half, totals[0][0], totals[0][1])
            lower = jnp.where(first_half, totals[1][1], totals[1][0])
            start = (part * half + 2 * at) * ROWS
            sums[start:start + 2 * ROWS, :] = jnp.where(top, upper, lower)

    convolved(0, volume_hi, volume_lo, half // 2 + 2, finish_first)
    convolved(1, first_hi, first_lo, half // 2 + 1, finish_second)
    score = sums[...]
    weight = jnp.exp(score - jnp.max(score, axis=1, keepdims=True))
    spot = lax.broadcasted_iota(jnp.int32, score.shape, 1)
    level = jnp.where(spot < CH, 2 * spot, 2 * spot - (2 * CH - 1)).astype(F32)
    mean = jnp.sum(weight * level, axis=1, keepdims=True) / (jnp.sum(weight, axis=1, keepdims=True) * DISP)
    pixel = lax.broadcasted_iota(jnp.int32, score.shape, 0)
    placed = jnp.where(pixel // ROWS == spot, mean, 0.0)
    pick = jnp.where(
        lax.broadcasted_iota(jnp.int32, (16, width * ROWS), 1) % ROWS
        == lax.broadcasted_iota(jnp.int32, (16, width * ROWS), 0), 1.0, 0.0).astype(BF16)
    final = reduce(jnp.add, [dot(pick, part) for part in split3(placed)])
    out[...] = final[:ROWS, :width]
    for step, copies in ((1, upward), (-1, downward)):
        @pl.when(present(step))
        def _(copies=copies):
            for copy in copies:
                copy.wait_send()

    for step, copy in (*sends, *rims):
        @pl.when(present(-step))
        def _(copy=copy):
            copy.wait_send()

    for going, forward in forwards:
        @pl.when(going)
        def _(forward=forward):
            forward.wait_send()


def on_device(reference_feat, secondary_feat, pair_offsets, w_query_key, w_value, conv_first, conv_second):
    pairs = secondary_feat.shape[0]
    images = pairs + 1
    width, features = reference_feat.shape[1:]
    wide = width + 2 * HALO
    group = ROWS * GROUPS
    held = (ROWS + 2) * wide + 256 - 3 * wide
    copies = 12
    banded = pltpu.VMEM((2, 8 * group, 8 * group), BF16)
    costs = pltpu.VMEM(((width // 2 + 4) * 4 * group, 256), BF16)
    firsts = pltpu.VMEM(((width // 2 + 2) * 4 * group, 256), BF16)
    first, second = (jnp.transpose(conv, (2, 3, 4, 0, 1)) for conv in (conv_first, conv_second))
    return pl.pallas_call(
        functools.partial(stereo_kernel, images, width, lax.axis_size("tile")),
        out_shape=jax.ShapeDtypeStruct((ROWS, width), F32),
        in_specs=[pl.BlockSpec(memory_space=pltpu.HBM)] * 7,
        out_specs=pl.BlockSpec(memory_space=pltpu.VMEM),
        scratch_shapes=[
            pltpu.VMEM((images, ROWS, HALO, features), F32),
            pltpu.VMEM((images, ROWS, HALO, features), F32),
            pltpu.VMEM((images, ROWS, width, features), F32),
            pltpu.VMEM((2 * CH, features), F32),
            pltpu.VMEM((2, 3, 3, 3, GROUPS, GROUPS), F32),
            pltpu.VMEM((12, group, 128), F32),
            pltpu.VMEM((2, 2, 4 * group, 128), F32),
            pltpu.VMEM((images, ROWS, wide, 2 * CH), F32),
            pltpu.VMEM((ROWS, wide, 256), F32),
            pltpu.VMEM((images, ROWS, wide, 256), BF16),
            pltpu.VMEM((images, held, 128), BF16),
            pltpu.VMEM((images, held, 128), BF16),
            pltpu.VMEM((ROWS, 2, wide, 128), F32),
            pltpu.VMEM((ROWS, (width + 4) * GROUPS, 256), BF16),
            banded, banded,
            pltpu.VMEM((4, pairs, 2, width - HALO, 128), F32),
            pltpu.VMEM((4, pairs, 2, HALO, 128), F32),
            pltpu.VMEM((pairs, 2, HALO, 128), F32),
            pltpu.VMEM((pairs, 2, 4 * width, 128), F32),
            pltpu.VMEM((pairs, 2, width, 128), F32),
            pltpu.VMEM((1, pairs), jnp.int32),
            pltpu.VMEM((1, pairs), jnp.int32),
            pltpu.SMEM((3, 1, pairs), jnp.int32),
            costs, costs, firsts, firsts,
            pltpu.VMEM((width * ROWS, 128), F32),
            pltpu.SemaphoreType.DMA((9,)),
            pltpu.SemaphoreType.DMA((copies,)),
            pltpu.SemaphoreType.DMA((copies,)),
        ],
        compiler_params=pltpu.CompilerParams(
            vmem_limit_bytes=55168 << 10, collective_id=0, has_side_effects=True),
    )(pair_offsets.T, reference_feat, secondary_feat, w_query_key.T, w_value.T, first, second)


def solution(mesh):
    return jax.shard_map(
        on_device,
        mesh=mesh,
        in_specs=(
            P("groups", "tile", None),
            P("groups", None, "tile", None),
            P("groups", "tile"),
            P(),
            P(),
            P(),
            P(),
        ),
        out_specs=P("groups", "tile"),
        check_vma=False,
    )
```

```python
import functools
from functools import reduce

import jax
import jax.numpy as jnp
from jax import lax
from jax.experimental import pallas as pl
from jax.experimental.pallas import tpu as pltpu
from jax.sharding import PartitionSpec as P

GROUPS = 8
DISP = 128
RAD = 3
ROWS = 4
CH = 64
LANES = ROWS * CH
HALO = 8
F32 = jnp.float32
BF16 = jnp.bfloat16


def dot(a, b):
    return jnp.dot(a, b, preferred_element_type=F32)


def split2(x):
    hi = x.astype(BF16)
    return hi, (x - hi.astype(F32)).astype(BF16)


def split3(x):
    hi = x.astype(BF16)
    rest = x - hi.astype(F32)
    mid = rest.astype(BF16)
    return hi, mid, (rest - mid.astype(F32)).astype(BF16)


def dot_nt(a, b):
    return lax.dot_general(a, b, (((1,), (1,)), ((), ())), preferred_element_type=F32)


def rounded(value):
    hi = value.astype(BF16).astype(F32)
    return hi, value - hi


def lower_half(value):
    return lax.broadcasted_iota(jnp.int32, value.shape, 1) < CH


def band_weights(taps, spread, turned, w_hi, w_lo):
    group = ROWS * GROUPS
    empty = jnp.zeros((GROUPS, GROUPS), F32)
    for conv in range(2):
        for col in range(3):
            for phase in range(2):
                for row in range(ROWS):
                    pieces = []
                    for level in range(4):
                        for source in range(ROWS):
                            step, depth = source - row + 1, level - phase
                            used = 0 <= step < 3 and 0 <= depth < 3
                            pieces.append(taps[conv, step, col, depth] if used else empty)
                    spread[(conv * 3 + col) * 2 + phase, row * GROUPS:(row + 1) * GROUPS, :] = (
                        jnp.concatenate(pieces, axis=1))
    size = 4 * group
    layout = (((2, None), (1, 2)), ((0, 1), (None, 0)))
    for conv in range(2):
        for part in range(2):
            for place in range(2):
                lanes = slice(place * 128, (place + 1) * 128)
                pieces = []
                for col in range(2):
                    tap = layout[part][col][place]
                    if tap is None:
                        pieces.append(jnp.zeros((2 * group, 128), F32))
                    else:
                        pieces.extend(spread[(conv * 3 + tap) * 2 + phase] for phase in range(2))
                whole = jnp.concatenate(pieces, axis=0)
                if conv == 0:
                    hi, lo = split2(whole)
                    w_hi[0, part * size:(part + 1) * size, lanes] = hi
                    w_lo[0, part * size:(part + 1) * size, lanes] = lo
                    continue
                turned[part, place] = whole
                for channel in range(GROUPS):
                    hi, lo = split2(turned[part, place, pl.ds(channel, 2 * GROUPS, stride=GROUPS), :])
                    rows = slice(part * size + channel * 2 * GROUPS, part * size + (channel + 1) * 2 * GROUPS)
                    w_hi[1, rows, lanes] = hi
                    w_lo[1, rows, lanes] = lo


def stereo_kernel(images, width, count, offsets, ref, sec, wq, wv, first, second, out,
                  left, right, own, weights, taps, spread, ordered, projected, bias, queries, keys, values, edge, main,
                  w_hi, w_lo, middle, rim, behind, window, wrap, before, after, shifts,
                  volume_hi, volume_lo, first_hi, first_lo, sums, local, send, recv):
    pairs = images - 1
    wide = width + 2 * HALO
    reach = 256
    group = ROWS * GROUPS
    half = width // 2
    column_rows = 4 * group
    tile = lax.axis_index("tile")
    lane = lax.broadcasted_iota(jnp.int32, (8, 128), 1)

    def present(step):
        return (tile + step >= 0) & (tile + step < count)

    def remote(source, target, place, step):
        return pltpu.make_async_remote_copy(
            src_ref=source, dst_ref=target, send_sem=send.at[place], recv_sem=recv.at[place],
            device_id={"tile": tile + step}, device_id_type=pl.DeviceIdType.MESH)

    barrier = pltpu.get_barrier_semaphore()
    partners = 0
    for step in (1, -1, 2, -2, 3, -3):
        @pl.when(present(step))
        def _(step=step):
            pl.semaphore_signal(barrier, inc=1, device_id={"tile": tile + step}, device_id_type=pl.DeviceIdType.MESH)

        partners = partners + jnp.where(present(step), 1, 0)
    loads = [
        pltpu.make_async_copy(source, target, local.at[place])
        for place, (source, target) in enumerate((
            (wq, weights.at[pl.ds(0, CH)]),
            (wv, weights.at[pl.ds(CH, CH)]),
            (sec, own.at[pl.ds(1, pairs)]),
            (ref, own.at[0]),
            (first, taps.at[0]),
            (second, taps.at[1]),
            (offsets, shifts.at[0]),
        ))
    ]
    for load in loads:
        load.start()
    pl.semaphore_wait(barrier, partners)

    tail = pl.ds(width - HALO, HALO)
    head = pl.ds(0, HALO)
    upward = [
        remote(sec.at[:, :, tail, :], left.at[pl.ds(1, pairs)], 0, 1),
        remote(ref.at[:, tail, :], left.at[0], 1, 1),
        remote(offsets, before, 2, 1),
    ]
    downward = [
        remote(sec.at[:, :, head, :], right.at[pl.ds(1, pairs)], 3, -1),
        remote(ref.at[:, head, :], right.at[0], 4, -1),
        remote(offsets, after, 5, -1),
    ]
    for step, copies in ((1, upward), (-1, downward)):
        @pl.when(present(step))
        def _(copies=copies):
            for copy in copies:
                copy.start()
    for step, halo, entry in ((-1, left, before), (1, right, after)):
        @pl.when(jnp.logical_not(present(step)))
        def _(halo=halo, entry=entry):
            halo[...] = jnp.zeros_like(halo)
            entry[...] = jnp.zeros_like(entry)
    for step in (1, 2, 3):
        @pl.when(jnp.logical_not(present(step)))
        def _(step=step):
            middle[step] = jnp.zeros(middle.shape[1:], F32)
            rim[step] = jnp.zeros(rim.shape[1:], F32)

    spot = lax.broadcasted_iota(jnp.int32, (wide, reach), 1)
    query = lax.broadcasted_iota(jnp.int32, (wide, reach), 0)
    key = spot - jnp.where(spot >= 2 * wide, 2 * wide, jnp.where(spot >= wide, wide, 0))
    column = key + (tile * width - HALO)
    near = (key - query <= RAD) & (query - key <= RAD) & (column >= 0) & (column < count * width) & (spot < 3 * wide)
    for row in range(ROWS):
        allowed = near
        if row == 0:
            allowed = allowed & (spot >= wide)
        if row == ROWS - 1:
            allowed = allowed & (spot < 2 * wide)
        bias[row] = jnp.where(allowed, 0.0, -1e30)
    for image in range(images):
        for at, size in ((0, wide), ((ROWS + 1) * wide, reach - 2 * wide)):
            keys[image, at:at + size, :] = jnp.zeros((size, 128), BF16)
            values[image, at:at + size, :] = jnp.zeros((size, 128), BF16)
        for row in range(ROWS):
            for at in (0, HALO + width):
                projected[image, row, at:at + HALO, :] = jnp.zeros((HALO, 128), F32)
    loads[0].wait()
    loads[1].wait()
    packed = jnp.concatenate(split2(weights[...]), axis=0)

    def project(value):
        hi, lo = split2(value)
        both = dot_nt(hi, packed) + dot_nt(lo, packed)
        return both[:, :128] + both[:, 128:]

    def project_own(image):
        both = project(own[image].reshape(ROWS * width, own.shape[3]))
        for row in range(ROWS):
            projected[image, row, HALO:HALO + width, :] = both[row * width:(row + 1) * width]

    ones = jnp.ones((reach, 128), BF16)

    def prepare(which, parts):
        for image in which:
            for row in range(ROWS):
                for at, size in parts:
                    value = projected[image, row, at:at + size, :]
                    low = lower_half(value)
                    hi, rest = rounded(value)
                    turned_hi, turned_rest = pltpu.roll(hi, CH, 1), pltpu.roll(rest, CH, 1)
                    queries[image, row, at:at + size, :] = jnp.concatenate(
                        [jnp.where(low, hi, turned_hi) * (1.0 / CH), jnp.where(low, rest, turned_rest) * (1.0 / CH)],
                        axis=1).astype(BF16)
                    rows = slice((row + 1) * wide + at, (row + 1) * wide + at + size)
                    keys[image, rows, :] = jnp.where(low, hi, turned_rest).astype(BF16)
                    values[image, rows, :] = jnp.where(low, turned_hi, rest).astype(BF16)

    def attention(which, parts):
        def taken(array):
            pieces = [array[at:at + size] for at, size in parts]
            return pieces[0] if len(pieces) == 1 else jnp.concatenate(pieces, axis=0)

        places = [(image, row) for image in which for row in range(ROWS)]
        scores = []
        for image, row in places:
            seen = keys[image, row * wide:row * wide + reach, :]
            scores.append(
                dot_nt(taken(queries.at[image, row]), jnp.concatenate([seen, seen], axis=1)) + taken(bias.at[row]))
        raised = [split2(jnp.exp(score - jnp.max(score, axis=1, keepdims=True))) for score in scores]
        result = [[None] * ROWS for _ in range(images)]
        for (image, row), (hi, lo) in zip(places, raised):
            mixed = jnp.concatenate([values[image, row * wide:row * wide + reach, :], ones], axis=1)
            total = dot(hi, mixed) + dot(lo, mixed)
            shared = total[:, :128] + pltpu.roll(total[:, :128], CH, 1)
            value = taken(projected.at[image, row])
            value = jnp.where(lower_half(value), pltpu.roll(value, CH, 1), value)
            result[image][row] = value + shared / total[:, 128:]
        return result

    def paired(parts, place):
        return jnp.where(lower_half(parts[0]), parts[2 * place], parts[2 * place + 1])

    def keep_reference(parts, start):
        size = parts[0].shape[0]
        column = lax.broadcasted_iota(jnp.int32, (size, 128), 0) + (tile * width - HALO + start)
        inside = (column >= 0) & (column < count * width)
        for row in range(ROWS):
            scaled = jnp.where(inside, parts[row], 0.0) * (1.0 / (CH // GROUPS))
            for place, part in enumerate(rounded(scaled)):
                edge[row, place, start:start + size, :] = part

    inner = ((0, wide),)
    others = tuple(range(1, images))
    rest = HALO // 2
    outer = ((0, 2 * HALO), (width, 2 * HALO))
    loads[2].wait()
    loads[3].wait()
    sends = []
    for image in range(images):
        project_own(image)
    prepare(others, inner)
    features = attention(others, inner)
    for pair in range(pairs):
        for place in range(2):
            middle[0, pair, place] = paired(features[pair + 1], place)[HALO + rest:HALO + width - rest]
    for step in (1, 3):
        copy = remote(middle.at[0], middle.at[step], 5 + step, -step)
        sends.append((step, copy))

        @pl.when(present(-step))
        def _(copy=copy):
            copy.start()

    loads[4].wait()
    loads[5].wait()
    loads[6].wait()
    band_weights(taps, spread, ordered, w_hi, w_lo)
    def arrived(chosen):
        for step, copies in ((1, upward), (-1, downward)):
            @pl.when(present(-step))
            def _(copies=copies):
                for copy in copies[chosen]:
                    copy.wait_recv()

    def project_halo(start, stop):
        size = (stop - start) * ROWS * HALO
        both = project(jnp.concatenate(
            [side[start:stop].reshape(size, own.shape[3]) for side in (left, right)], axis=0))
        for image in range(start, stop):
            for row in range(ROWS):
                base = ((image - start) * ROWS + row) * HALO
                projected[image, row, 0:HALO, :] = both[base:base + HALO]
                projected[image, row, HALO + width:wide, :] = both[size + base:size + base + HALO]

    arrived(slice(0, 1))
    project_halo(1, images)
    prepare(others, outer)
    features = attention(others, outer)
    for pair in range(pairs):
        for place in range(2):
            feature = paired(features[pair + 1], place)
            behind[pair, place] = feature[:HALO]
            rim[0, pair, place] = jnp.concatenate(
                [feature[HALO:HALO + rest], feature[2 * HALO + rest:3 * HALO]], axis=0)
    rims = []
    for step in (1, 2, 3):
        copy = remote(rim.at[0], rim.at[step], 8 + step, -step)
        rims.append((step, copy))

        @pl.when(present(-step))
        def _(copy=copy):
            copy.start()

    arrived(slice(1, 3))
    entries = [
        pltpu.make_async_copy(source, shifts.at[place], local.at[6 + place])
        for place, source in ((1, before), (2, after))
    ]
    for entry in entries:
        entry.start()
    project_halo(0, 1)
    prepare((0,), inner)
    features = attention((0,), inner)
    odd = tile % 2 == 1
    forwards = []
    for step, copy in sends:
        @pl.when(present(step))
        def _(copy=copy):
            copy.wait_recv()

        offset, chosen = (-1, odd) if step == 1 else (1, jnp.logical_not(odd))
        forward = remote(middle.at[step], middle.at[2], 7, offset)
        going = chosen & present(step)
        forwards.append((going, forward))

        @pl.when(going)
        def _(forward=forward):
            forward.start()

    keep_reference(features[0], 0)
    own_group = (lane % CH) // (CH // GROUPS) == lax.broadcasted_iota(jnp.int32, (8, 128), 0)
    pad = HALO - 2
    for row in range(ROWS):
        for place in range(2):
            for col in range(0, width + 4, 2):
                pair_rows = [
                    jnp.where(own_group, jnp.broadcast_to(edge[row, place, pad + at:pad + at + 1, :], (8, 128)), 0.0)
                    for at in (col, col + 1)
                ]
                main[row, col * 8:col * 8 + 16, place * 128:(place + 1) * 128] = (
                    jnp.concatenate(pair_rows, axis=0).astype(BF16))
    for entry in entries:
        entry.wait()

    def joined(hi, lo, row):
        low = lower_half(hi)
        if row % 2 == 0:
            return jnp.where(low, hi, pltpu.roll(lo, CH, 1))
        return jnp.where(low, pltpu.roll(hi, CH, 1), lo)

    for step, copy in rims:
        @pl.when(present(step))
        def _(copy=copy):
            copy.wait_recv()

    @pl.when(present(2))
    def _(forward=forwards[0][1]):
        forward.wait_recv()

    for pair in range(pairs):
        for side in range(2):
            for step in range(4):
                start = step * width
                window[pair, side, start:start + rest, :] = rim[step, pair, side, :rest, :]
                window[pair, side, start + rest:start + width - rest, :] = middle[step, pair, side]
                window[pair, side, start + width - rest:start + width, :] = rim[step, pair, side, rest:, :]
            wrap[pair, side, :width - HALO, :] = jnp.zeros((width - HALO, 128), F32)
            wrap[pair, side, width - HALO:, :] = behind[pair, side]
    odds = [lax.rem(shifts[0, 0, pair], 2) for pair in range(pairs)]
    floors = [lax.div(shifts[0, 0, pair] - odds[pair], 2) for pair in range(pairs)]
    ceilings = [floors[pair] + odds[pair] for pair in range(pairs)]
    first_half = lower_half(lane)

    def turned(value, begin, pair):
        return pltpu.roll(value, (256 + CH * pair - begin) & 127, 1)

    def halves(value, flag):
        return jnp.where(flag, value[1], value[0]), jnp.where(flag, value[0], value[1])

    def levels(even, odd):
        size = even.shape[0]
        at = lax.broadcasted_iota(jnp.int32, (size, 128), 1) % CH
        return (
            jnp.where(at >= 1, pltpu.roll(odd, 1, 1), 0.0), even, odd,
            jnp.where(at < CH - 1, pltpu.roll(even, 127, 1), 0.0))

    for side in range(2):
        products = []
        for row in (2 * side, 2 * side + 1):
            for pair in range(pairs):
                flag = odds[pair] == 1
                strided = [window[pair, side, pl.ds(at, 2 * width, stride=2), :] for at in range(2)]
                strided_wrap = [
                    jnp.concatenate([strided[at][:3 * half], wrap[pair, side, pl.ds(at, half, stride=2), :]], axis=0)
                    for at in range(2)
                ]
                whole, ends = [
                    jnp.concatenate([joined(*rounded(part), row) for part in halves(value, flag)], axis=0).astype(BF16)
                    for value in (strided, strided_wrap)
                ]
                products.append((
                    dot_nt(main[row], jnp.concatenate([whole, whole], axis=1)),
                    dot_nt(main[row, 0:16, :], jnp.concatenate([ends, ends], axis=1))))
        for col in range(width + 4):
            x = col - 2
            evens, odds_of = [], []
            for place in range(2):
                made = []
                for pair in range(pairs):
                    whole, ends = products[place * pairs + pair]
                    source = (ends if x < 0 else whole)[col * 8:(col + 1) * 8]
                    same, other = source[:, :128], source[:, 128:]
                    if 0 <= x < width:
                        low, high = floors[pair] + (x + x % 2) // 2, ceilings[pair] + x // 2
                        if x % 2:
                            made.append((turned(other, high, pair), turned(same, low, pair)))
                        else:
                            made.append((turned(same, low, pair), turned(other, high, pair)))
                    else:
                        q = odds[pair]
                        begin = shifts[1 if x < 0 else 2, 0, pair] + x + 256
                        match = lax.rem(begin, 2) == q
                        made.append((
                            turned(jnp.where(match, same, other),
                                   lax.div(jnp.where(match, begin - q, begin - 1 + q), 2) - 128, pair),
                            turned(jnp.where(match, other, same),
                                   lax.div(jnp.where(match, begin + q, begin + 1 - q), 2) - 128, pair)))
                evens.append(jnp.where(first_half, made[0][0], made[1][0]))
                odds_of.append(jnp.where(first_half, made[0][1], made[1][1]))
            for at, value in enumerate(levels(jnp.concatenate(evens, axis=0), jnp.concatenate(odds_of, axis=0))):
                hi, lo = split2(value)
                for part, base in ((0, -2), (1, half - 2)):
                    if 0 <= x - base < half + 4:
                        start = (x - base) * column_rows + at * group + side * 16
                        volume_hi[start:start + 16, part * 128:(part + 1) * 128] = hi
                        volume_lo[start:start + 16, part * 128:(part + 1) * 128] = lo

    def convolved(conv, hi_ref, lo_ref, tiles, finish):
        carry = None
        out_rows = column_rows
        for at in range(tiles):
            rows = slice(at * 2 * column_rows, (at + 1) * 2 * column_rows)
            hi, lo = hi_ref[rows, :], lo_ref[rows, :]
            used = slice(out_rows if at == 0 else 0, out_rows if at == tiles - 1 else 2 * out_rows)
            wh, wl = w_hi[conv, used, :], w_lo[conv, used, :]
            both = dot(wh, hi) + dot(wl, hi) + dot(wh, lo)
            if at:
                finish(at - 1, jnp.maximum(carry + both[:out_rows], 0.0))
            carry = both if at == 0 else both[out_rows:]

    def finish_first(at, value):
        for part in range(2):
            lanes = slice(part * 128, (part + 1) * 128)
            for col in range(2):
                rows = value[col * 2 * group:(col + 1) * 2 * group, lanes]
                if part == 0 and at == 0 and col == 0:
                    rows = jnp.where(tile == 0, 0.0, rows)
                if part == 1 and at == half // 2 and col == 1:
                    rows = jnp.where(tile == count - 1, 0.0, rows)
                start = (2 * at + col) * column_rows
                for place, piece in enumerate(levels(rows[:group], rows[group:])):
                    hi, lo = split2(piece)
                    first_hi[start + place * group:start + (place + 1) * group, lanes] = hi
                    first_lo[start + place * group:start + (place + 1) * group, lanes] = lo

    def finish_second(at, value):
        top = lax.broadcasted_iota(jnp.int32, (8, 128), 0) < ROWS
        for part in range(2):
            totals = []
            for col in range(2):
                total = reduce(jnp.add, [
                    value[channel * 16 + col * 8:channel * 16 + col * 8 + 8, part * 128:(part + 1) * 128]
                    for channel in range(GROUPS)
                ])
                total = total + pltpu.roll(total, CH, 1)
                totals.append((total, pltpu.roll(total, ROWS, 0)))
            upper = jnp.where(first_half, totals[0][0], totals[0][1])
            lower = jnp.where(first_half, totals[1][1], totals[1][0])
            start = (part * half + 2 * at) * ROWS
            sums[start:start + 2 * ROWS, :] = jnp.where(top, upper, lower)

    convolved(0, volume_hi, volume_lo, half // 2 + 2, finish_first)
    convolved(1, first_hi, first_lo, half // 2 + 1, finish_second)
    score = sums[...]
    weight = jnp.exp(score - jnp.max(score, axis=1, keepdims=True))
    spot = lax.broadcasted_iota(jnp.int32, score.shape, 1)
    level = jnp.where(spot < CH, 2 * spot, 2 * spot - (2 * CH - 1)).astype(F32)
    mean = jnp.sum(weight * level, axis=1, keepdims=True) / (jnp.sum(weight, axis=1, keepdims=True) * DISP)
    pixel = lax.broadcasted_iota(jnp.int32, score.shape, 0)
    placed = jnp.where(pixel // ROWS == spot, mean, 0.0)
    pick = jnp.where(
        lax.broadcasted_iota(jnp.int32, (16, width * ROWS), 1) % ROWS
        == lax.broadcasted_iota(jnp.int32, (16, width * ROWS), 0), 1.0, 0.0).astype(BF16)
    final = reduce(jnp.add, [dot(pick, part) for part in split3(placed)])
    out[...] = final[:ROWS, :width]
    for step, copies in ((1, upward), (-1, downward)):
        @pl.when(present(step))
        def _(copies=copies):
            for copy in copies:
                copy.wait_send()

    for step, copy in (*sends, *rims):
        @pl.when(present(-step))
        def _(copy=copy):
            copy.wait_send()

    for going, forward in forwards:
        @pl.when(going)
        def _(forward=forward):
            forward.wait_send()


def on_device(reference_feat, secondary_feat, pair_offsets, w_query_key, w_value, conv_first, conv_second):
    pairs = secondary_feat.shape[0]
    images = pairs + 1
    width, features = reference_feat.shape[1:]
    wide = width + 2 * HALO
    group = ROWS * GROUPS
    held = (ROWS + 2) * wide + 256 - 3 * wide
    copies = 12
    banded = pltpu.VMEM((2, 8 * group, 8 * group), BF16)
    costs = pltpu.VMEM(((width // 2 + 4) * 4 * group, 256), BF16)
    firsts = pltpu.VMEM(((width // 2 + 2) * 4 * group, 256), BF16)
    first, second = (jnp.transpose(conv, (2, 3, 4, 0, 1)) for conv in (conv_first, conv_second))
    return pl.pallas_call(
        functools.partial(stereo_kernel, images, width, lax.axis_size("tile")),
        out_shape=jax.ShapeDtypeStruct((ROWS, width), F32),
        in_specs=[pl.BlockSpec(memory_space=pltpu.HBM)] * 7,
        out_specs=pl.BlockSpec(memory_space=pltpu.VMEM),
        scratch_shapes=[
            pltpu.VMEM((images, ROWS, HALO, features), F32),
            pltpu.VMEM((images, ROWS, HALO, features), F32),
            pltpu.VMEM((images, ROWS, width, features), F32),
            pltpu.VMEM((2 * CH, features), F32),
            pltpu.VMEM((2, 3, 3, 3, GROUPS, GROUPS), F32),
            pltpu.VMEM((12, group, 128), F32),
            pltpu.VMEM((2, 2, 4 * group, 128), F32),
            pltpu.VMEM((images, ROWS, wide, 2 * CH), F32),
            pltpu.VMEM((ROWS, wide, 256), F32),
            pltpu.VMEM((images, ROWS, wide, 256), BF16),
            pltpu.VMEM((images, held, 128), BF16),
            pltpu.VMEM((images, held, 128), BF16),
            pltpu.VMEM((ROWS, 2, wide, 128), F32),
            pltpu.VMEM((ROWS, (width + 4) * GROUPS, 256), BF16),
            banded, banded,
            pltpu.VMEM((4, pairs, 2, width - HALO, 128), F32),
            pltpu.VMEM((4, pairs, 2, HALO, 128), F32),
            pltpu.VMEM((pairs, 2, HALO, 128), F32),
            pltpu.VMEM((pairs, 2, 4 * width, 128), F32),
            pltpu.VMEM((pairs, 2, width, 128), F32),
            pltpu.VMEM((1, pairs), jnp.int32),
            pltpu.VMEM((1, pairs), jnp.int32),
            pltpu.SMEM((3, 1, pairs), jnp.int32),
            costs, costs, firsts, firsts,
            pltpu.VMEM((width * ROWS, 128), F32),
            pltpu.SemaphoreType.DMA((9,)),
            pltpu.SemaphoreType.DMA((copies,)),
            pltpu.SemaphoreType.DMA((copies,)),
        ],
        compiler_params=pltpu.CompilerParams(
            vmem_limit_bytes=55168 << 10, collective_id=0, has_side_effects=True),
    )(pair_offsets.T, reference_feat, secondary_feat, w_query_key.T, w_value.T, first, second)


def solution(mesh):
    return jax.shard_map(
        on_device,
        mesh=mesh,
        in_specs=(
            P("groups", "tile", None),
            P("groups", None, "tile", None),
            P("groups", "tile"),
            P(),
            P(),
            P(),
            P(),
        ),
        out_specs=P("groups", "tile"),
        check_vma=False,
    )
```
